32 devices in a mesh: seq: 4 (over x, core), fsdp: 8 (over z, y).
Axes of the slice: x: 2, y: 2, z: 4, core: 2. Of those that a mesh axis runs over, the one named last changes fastest.
Arguments:
- tokens: bfloat16 [8, 2048, 768], P('fsdp', 'seq'), may hold values from -6 to 6
- encoder: bfloat16 [8, 512, 768], P('fsdp', 'seq'), may hold values from -6 to 6
- cotangent: bfloat16 [8, 2048, 768], P('fsdp', 'seq'), may hold values from -6 to 6
- lengths: int32 [8], P('fsdp'), may hold values from 512 to 2048, as said below
- gains: float32 [3, 768], P(None, ('seq', 'fsdp')), may hold values from 0.5 to 1.5
- self_query: float32 [768, 768], P(('seq', 'fsdp')), may hold values from -0.0546875 to 0.0546875
- self_key: float32 [768, 768], P(('seq', 'fsdp')), may hold values from -0.21875 to 0.21875
- self_value: float32 [768, 768], P(('seq', 'fsdp')), may hold values from -0.21875 to 0.21875
- self_output: float32 [768, 768], P(('seq', 'fsdp')), may hold values from -0.875 to 0.875
- cross_query: float32 [768, 768], P(('seq', 'fsdp')), may hold values from -0.0546875 to 0.0546875
- cross_key: float32 [768, 768], P(('seq', 'fsdp')), may hold values from -0.21875 to 0.21875
- cross_value: float32 [768, 768], P(('seq', 'fsdp')), may hold values from -0.21875 to 0.21875
- cross_output: float32 [768, 768], P(('seq', 'fsdp')), may hold values from -0.875 to 0.875
- ffn_gate: float32 [768, 2048], P(('seq', 'fsdp')), may hold values from -0.21875 to 0.21875
- ffn_up: float32 [768, 2048], P(('seq', 'fsdp')), may hold values from -0.21875 to 0.21875
- ffn_down: float32 [2048, 768], P(('seq', 'fsdp')), may hold values from -0.125 to 0.125
- rel_bias: float32 [32, 12], P(None, 'seq'), may hold values from -4 to 4
Outputs:
- output: bfloat16 [8, 2048, 768], P('fsdp', 'seq')
- input_grad: float32 [8, 2048, 768], P('fsdp', 'seq')
- encoder_grad: float32 [8, 512, 768], P('fsdp', 'seq')
- gains_grad: float32 [3, 768], P(None, ('seq', 'fsdp'))
- self_query_grad: float32 [768, 768], P(('seq', 'fsdp'))
- self_key_grad: float32 [768, 768], P(('seq', 'fsdp'))
- self_value_grad: float32 [768, 768], P(('seq', 'fsdp'))
- self_output_grad: float32 [768, 768], P(('seq', 'fsdp'))
- cross_query_grad: float32 [768, 768], P(('seq', 'fsdp'))
- cross_key_grad: float32 [768, 768], P(('seq', 'fsdp'))
- cross_value_grad: float32 [768, 768], P(('seq', 'fsdp'))
- cross_output_grad: float32 [768, 768], P(('seq', 'fsdp'))
- ffn_gate_grad: float32 [768, 2048], P(('seq', 'fsdp'))
- ffn_up_grad: float32 [768, 2048], P(('seq', 'fsdp'))
- ffn_down_grad: float32 [2048, 768], P(('seq', 'fsdp'))
- rel_bias_grad: float32 [32, 12], P(None, 'seq')
The draws below stay inside these ranges and needn't reach their ends.
Inputs may be any that keep to these rules, and one draw needn't show every extreme that they name: Slot s holds one sequence in its first lengths[s] positions; the rest is padding. Some slot is full.
All inputs are finite; a program needn't handle non-finite values.
Results may differ from the reference program's by a relative error of at most 0.025.
The reference program's roundings to bfloat16 on the way count: a program that leaves them out, or rounds other values in their place, can miss the bound.
Values may be sent and summed in bfloat16 or wider, within the bound.
A program may use at most 192 MiB of HBM per device.

```python
import jax
import jax.numpy as jnp
import numpy as np
from jax import lax

D = 768
FF = 2048
HEADS = 12
HEAD = 64
BUCKETS = 32
TOK_DEV = 512
SLOTS = 8
SLOT = 2048
ENC = 512


def draw_lengths(key, part):
    first, second = jax.random.split(key)
    values = jax.random.randint(first, (SLOTS,), TOK_DEV, SLOT + 1)
    full_slot = jax.random.randint(second, (), 0, SLOTS)
    return jnp.where(jnp.arange(SLOTS) == full_slot, SLOT, values).astype(jnp.int32)


def shard_levels(key, extent, shards, smallest, top_value):
    loudness = 1.0
    for dim, shards_of in shards:
        draws = jax.random.uniform(jax.random.fold_in(jax.random.fold_in(key, 6), dim), (shards_of,), jnp.float32, smallest / len(shards), top_value / len(shards))
        loudness = loudness * jnp.repeat(jnp.exp(draws), extent[dim] // shards_of).reshape((-1,) + (1,) * (len(extent) - 1 - dim))
    return loudness


def noise(own_key, extent, scale, bound, shards=(), kind=jnp.bfloat16):
    drawn = jax.random.normal(own_key, extent, jnp.float32) * scale
    if len(shards) > 0:
        drawn = shard_levels(own_key, extent, shards, -0.22, 0.18) * drawn
    return jnp.clip(drawn, min=-bound, max=bound).astype(kind)


def setup_inputs(seed: int = 0) -> dict:
    key_list = jax.random.split(jax.random.key(seed), 18)
    tokens = noise(key_list[0], (SLOTS, SLOT, D), 1.0, 6.0, ((0, 8), (1, 4)))
    encoder = noise(key_list[1], (SLOTS, ENC, D), 1.0, 6.0, ((0, 8), (1, 4)))
    cotangent = noise(key_list[2], (SLOTS, SLOT, D), 1.0, 6.0, ((0, 8), (1, 4)))
    lengths = draw_lengths(jax.random.fold_in(key_list[17], 71), 0)
    gains = jnp.clip(1.0 + 0.1 * jax.random.normal(key_list[4], (3, D), jnp.float32), 0.5, 1.5)
    self_query = noise(key_list[5], (D, D), (16 * D) ** -0.5, 0.0546875, ((0, 32),), jnp.float32)
    self_key = noise(key_list[6], (D, D), D ** -0.5, 0.21875, ((0, 32),), jnp.float32)
    self_value = noise(key_list[7], (D, D), D ** -0.5, 0.21875, ((0, 32),), jnp.float32)
    self_output = noise(key_list[8], (D, D), (D // 16) ** -0.5, 0.875, ((0, 32),), jnp.float32)
    cross_query = noise(key_list[9], (D, D), (16 * D) ** -0.5, 0.0546875, ((0, 32),), jnp.float32)
    cross_key = noise(key_list[10], (D, D), D ** -0.5, 0.21875, ((0, 32),), jnp.float32)
    cross_value = noise(key_list[11], (D, D), D ** -0.5, 0.21875, ((0, 32),), jnp.float32)
    cross_output = noise(key_list[12], (D, D), (D // 16) ** -0.5, 0.875, ((0, 32),), jnp.float32)
    ffn_gate = noise(key_list[13], (D, FF), D ** -0.5, 0.21875, ((0, 32),), jnp.float32)
    ffn_up = noise(key_list[14], (D, FF), D ** -0.5, 0.21875, ((0, 32),), jnp.float32)
    ffn_down = noise(key_list[15], (FF, D), FF ** -0.5, 0.125, ((0, 32),), jnp.float32)
    rel_bias = noise(key_list[16], (BUCKETS, HEADS), 1.0, 4.0, ((1, 4),), jnp.float32)
    return {"tokens": tokens, "encoder": encoder, "cotangent": cotangent, "lengths": lengths, "gains": gains, "self_query": self_query, "self_key": self_key, "self_value": self_value, "self_output": self_output, "cross_query": cross_query, "cross_key": cross_key, "cross_value": cross_value, "cross_output": cross_output, "ffn_gate": ffn_gate, "ffn_up": ffn_up, "ffn_down": ffn_down, "rel_bias": rel_bias}


epsilon = 1e-06
negative = -1e+30
highest = lax.Precision.HIGHEST
bounds = np.ceil(16.0 * 8.0 ** (np.arange(1, 16) / 16.0)).astype(np.int32)

@jax.custom_vjp
def low(v):
    return lax.optimization_barrier(v.astype(jnp.bfloat16)).astype(jnp.float32)

@jax.custom_vjp
def low_back(v):
    return v

def low_keep(v):
    return (low(v), None)

def low_pass(kept, grad):
    return (grad,)

def back_keep(v):
    return (v, None)

def back_low(kept, grad):
    return (low(grad),)
low.defvjp(low_keep, low_pass)
low_back.defvjp(back_keep, back_low)

def buckets(distance):
    far = 16 + lax.optimization_barrier(jnp.sum((distance[..., None] >= jnp.asarray(bounds)).astype(jnp.int32), axis=-1))
    return jnp.where(distance < 16, distance, far).astype(jnp.int32)

def rms_norm(values, gain):
    scale = lax.rsqrt(lax.optimization_barrier(jnp.mean(values * values, axis=-1, keepdims=True)) + epsilon)
    return values * scale * gain

def project(values, matrix):
    return jnp.dot(values, matrix, precision=highest)

def attend(queries, key_rows, value_rows, bias, valid):
    rows = queries.shape[0]
    heads = queries.shape[1] // HEAD
    query_heads = queries.reshape(rows, heads, HEAD)
    key_heads = key_rows.reshape(key_rows.shape[0], heads, HEAD)
    value_heads = value_rows.reshape(value_rows.shape[0], heads, HEAD)
    scores = low_back(jnp.einsum('qhd,khd->hqk', query_heads, key_heads, precision=highest))
    if bias is not None:
        scores = jnp.where(valid[None], scores + bias, negative)
    largest = lax.optimization_barrier(jnp.max(scores, axis=-1, keepdims=True))
    expos = jnp.exp(scores - largest)
    weights = low(expos / lax.optimization_barrier(jnp.sum(expos, axis=-1, keepdims=True)))
    mixed = jnp.einsum('hqk,khd->qhd', weights, value_heads, precision=highest)
    return mixed.reshape(rows, heads * HEAD)

def slot_forward(inputs, encoded, length, rounded, table):
    gain_rows, w_query, w_key, w_value, w_output, c_query, c_key, c_value, c_output, w_gate, w_up, w_down = rounded
    rows = inputs.shape[0]
    positions = jnp.arange(rows, dtype=jnp.int32)
    distance = positions[:, None] - positions[None, :]
    valid = (distance >= 0) & (positions[None, :] < length)
    bias = jnp.take(table.T, buckets(jnp.maximum(distance, 0)), axis=1)
    normed = low(rms_norm(inputs, gain_rows[0]))
    queries = low(low_back(project(normed, w_query)))
    key_rows = low(low_back(project(normed, w_key)))
    value_rows = low(low_back(project(normed, w_value)))
    mixed = low(low_back(attend(queries, key_rows, value_rows, bias, valid)))
    attended = inputs + low_back(project(mixed, w_output))
    normed_two = low(rms_norm(attended, gain_rows[1]))
    cross_queries = low(low_back(project(normed_two, c_query)))
    cross_keys = low(low_back(project(encoded, c_key)))
    cross_values = low(low_back(project(encoded, c_value)))
    cross_mixed = low(low_back(attend(cross_queries, cross_keys, cross_values, None, None)))
    crossed = attended + low_back(project(cross_mixed, c_output))
    normed_three = low(rms_norm(crossed, gain_rows[2]))
    gate = low_back(project(normed_three, w_gate))
    upper = low_back(project(normed_three, w_up))
    hidden = low(jax.nn.gelu(gate, approximate=True) * upper)
    return crossed + low_back(project(hidden, w_down))

def reference(tokens, encoder, cotangent, lengths, gains, self_query, self_key, self_value, self_output, cross_query, cross_key, cross_value, cross_output, ffn_gate, ffn_up, ffn_down, rel_bias):
    masters = (gains, self_query, self_key, self_value, self_output, cross_query, cross_key, cross_value, cross_output, ffn_gate, ffn_up, ffn_down)

    def forward(inputs, encoded, weights, table):
        rounded = tuple((low(item) for item in weights))

        def step(carry, piece):
            return (carry, slot_forward(piece[0], piece[1], piece[2], rounded, table))
        _, result = lax.scan(jax.checkpoint(step), jnp.zeros((), jnp.float32), (inputs, encoded, lengths))
        return result
    result, pullback = jax.vjp(forward, tokens.astype(jnp.float32), encoder.astype(jnp.float32), masters, rel_bias)
    valid = (jnp.arange(SLOT, dtype=jnp.int32)[None, :] < lengths[:, None]).astype(jnp.float32)
    grad_in, grad_enc, grad_masters, grad_table = pullback(cotangent.astype(jnp.float32) * valid[..., None])
    return (result.astype(jnp.bfloat16), grad_in, grad_enc, grad_masters[0], grad_masters[1], grad_masters[2], grad_masters[3], grad_masters[4], grad_masters[5], grad_masters[6], grad_masters[7], grad_masters[8], grad_masters[9], grad_masters[10], grad_masters[11], grad_table)
```

```python
import functools
import jax
import jax.numpy as jnp
import numpy as np
from jax import lax
from jax.experimental import pallas as pl
from jax.experimental.pallas import tpu as pltpu
from jax.sharding import PartitionSpec as P

LANES = 128
BLOCK = 512
negative = -1e30
epsilon = 1e-06
highest = lax.Precision.HIGHEST
HEAD = 64


def nt(left, right):
    return lax.dot_general(left, right, (((1,), (1,)), ((), ())), preferred_element_type=jnp.float32)


def nn(left, right):
    return jnp.dot(left, right, preferred_element_type=jnp.float32)


def half_mask(head, head_size):
    lane = lax.broadcasted_iota(jnp.int32, (1, LANES), 1)
    per_tile = LANES // head_size
    return (lane // head_size) == (head % per_tile)


def attend_forward_kernel(*refs, causal, head_size):
    if causal:
        length_ref, q_ref, k_ref, v_ref, base_ref, o_ref, lse_ref, s_scr, p_scr, t_scr = refs
        length = length_ref[0]
    else:
        q_ref, k_ref, v_ref, o_ref, lse_ref, s_scr, p_scr = refs
    head = pl.program_id(0)
    first = (head % (LANES // head_size)) == 0
    mask = half_mask(head, head_size)
    rows, keys = q_ref.shape[0], k_ref.shape[0]
    block = min(BLOCK, rows)
    if causal:
        wide = jnp.broadcast_to(base_ref[0], (LANES, 3 * LANES))
        t_scr[...] = pltpu.roll(wide, 0, 1, stride=1, stride_axis=0)[:, : 2 * LANES]
    for number in range(rows // block):
        start = number * block
        queries = jnp.where(mask, q_ref[start : start + block, :], 0)
        total = start + block if causal else keys
        for low in range(0, total, BLOCK):
            high = min(low + BLOCK, total)
            s_scr[:, low:high] = nt(queries, k_ref[low:high, :])
        if causal:
            for part in range(block // LANES):
                at = slice(part * LANES, (part + 1) * LANES)
                column = start + part * LANES
                if column > 0:
                    s_scr[at, column - LANES : column + LANES] += t_scr[...]
                else:
                    s_scr[at, :LANES] += t_scr[:, LANES:]
            for low in range(0, total, BLOCK):
                high = min(low + BLOCK, total)

                @pl.when(length < high)
                def _(low=low, high=high):
                    place = low + lax.broadcasted_iota(jnp.int32, (block, high - low), 1)
                    s_scr[:, low:high] = jnp.where(place < length, s_scr[:, low:high], negative)

        sums = []
        for part in range(block // LANES):
            at = slice(part * LANES, (part + 1) * LANES)
            width = start + (part + 1) * LANES if causal else keys
            scores = s_scr[at, :width]
            largest = jnp.max(scores, axis=1, keepdims=True)
            expos = jnp.exp(scores - largest)
            totals = jnp.sum(expos, axis=1, keepdims=True)
            p_scr[at, :width] = expos.astype(jnp.bfloat16)
            if width < total:
                p_scr[at, width:total] = jnp.zeros((LANES, total - width), jnp.bfloat16)
            logsum = jnp.broadcast_to(largest + jnp.log(totals), (LANES, LANES))
            lse_ref[0, :, start + part * LANES : start + (part + 1) * LANES] = logsum.T[:8]
            sums.append(totals)
        mixed = nn(p_scr[:, :total], v_ref[:total, :])
        mixed = mixed / jnp.concatenate(sums, axis=0)
        before = jnp.where(first, jnp.zeros_like(mixed), o_ref[start : start + block, :].astype(jnp.float32))
        o_ref[start : start + block, :] = jnp.where(mask, mixed, before).astype(jnp.bfloat16)


def attend_forward(queries, keys, values, heads, head_size, padded=0, bias=None, length=None):
    causal = bias is not None
    rows, width = queries.shape
    count = keys.shape[0]
    per_tile = LANES // head_size
    block = min(BLOCK, rows)
    width = padded or width
    tile = lambda h: (0, h // per_tile)
    row_spec = pl.BlockSpec((rows, LANES), tile)
    skip = padded // LANES
    key_specs = [pl.BlockSpec((count, LANES), lambda h, n=n: (0, n * skip + h // per_tile)) for n in (1, 2)]
    in_specs = [row_spec, *key_specs]
    args = [queries, keys, values]
    scratch = [pltpu.VMEM((block, count), jnp.float32), pltpu.VMEM((block, count), jnp.bfloat16)]
    if causal:
        in_specs = [pl.BlockSpec(memory_space=pltpu.SMEM)] + in_specs + [pl.BlockSpec((1, 1, 3 * LANES), lambda h: (h, 0, 0))]
        args = [length] + args + [bias]
        scratch = scratch + [pltpu.VMEM((LANES, 2 * LANES), jnp.float32)]
    return pl.pallas_call(
        functools.partial(attend_forward_kernel, causal=causal, head_size=head_size),
        grid=(heads,),
        in_specs=in_specs,
        out_specs=[row_spec, pl.BlockSpec((1, 8, rows), lambda h: (h, 0, 0))],
        out_shape=[
            jax.ShapeDtypeStruct((rows, width), jnp.bfloat16),
            jax.ShapeDtypeStruct((heads, 8, rows), jnp.float32),
        ],
        scratch_shapes=scratch,
        compiler_params=pltpu.CompilerParams(vmem_limit_bytes=60 * 2**20),
        cost_estimate=pl.CostEstimate(
            flops=4 * heads * LANES * rows * count // (2 if causal else 1),
            bytes_accessed=4 * (rows + count) * width,
            transcendentals=heads * rows * count // (2 if causal else 1),
        ),
        name="self_forward" if causal else "cross_forward",
    )(*args)


def attend_backward_kernel(*refs, causal, head_size, heads):
    if causal:
        (length_ref, q_ref, k_ref, v_ref, do_ref, o_ref, lse_ref, base_ref, dq_ref, dk_ref, dv_ref, near_ref,
         kt_scr, dqt_scr, dk_scr, dv_scr, t_scr, row_scr) = refs
        length = length_ref[0]
    else:
        (q_ref, k_ref, v_ref, do_ref, o_ref, lse_ref, dq_ref, dk_ref, dv_ref,
         kt_scr, dqt_scr, dk_scr, dv_scr, row_scr) = refs
    head = pl.program_id(0)
    per_tile = LANES // head_size
    first = (head % per_tile) == 0
    last = ((head % per_tile) == per_tile - 1) | (head == heads - 1)
    mask = half_mask(head, head_size)
    rows, keys = q_ref.shape[0], k_ref.shape[0]
    block = min(BLOCK, rows)
    key_block = min(BLOCK, keys)

    @pl.when(first)
    def _():
        dqt_scr[...] = jnp.zeros_like(dqt_scr)
        dk_scr[...] = jnp.zeros_like(dk_scr)
        dv_scr[...] = jnp.zeros_like(dv_scr)

    if causal:
        wide = jnp.broadcast_to(base_ref[0], (LANES, 3 * LANES))
        t_scr[...] = pltpu.roll(wide, 0, 1, stride=1, stride_axis=0)[:, : 2 * LANES]
        near_ref[0] = jnp.zeros((LANES, 2 * LANES), jnp.float32)
    for low in range(0, keys, key_block):
        kt_scr[:, low : low + key_block] = jnp.where(mask, k_ref[low : low + key_block, :], 0).T
    for low in range(0, rows, block):
        at = slice(low, low + block)
        product = do_ref[at, :].astype(jnp.float32) * o_ref[at, :].astype(jnp.float32)
        delta = jnp.sum(jnp.where(mask, product, 0.0).T, axis=0, keepdims=True)
        logsum = lse_ref[0, 0:1, at]
        if causal:
            place = low + lax.broadcasted_iota(jnp.int32, (1, block), 1)
            logsum = jnp.where(place < length, logsum, -negative)
        row_scr[0:1, at] = logsum
        row_scr[1:2, at] = delta

    def piece(key_at, row_at, score_fix, near_width):
        queries = jnp.where(mask, q_ref[row_at, :], 0)
        grads = jnp.where(mask, do_ref[row_at, :], 0)
        scores = score_fix(nt(k_ref[key_at, :], queries))
        weights = jnp.exp(scores - row_scr[0:1, row_at])
        grad_weights = nt(v_ref[key_at, :], grads)
        grad_scores = weights * (grad_weights - row_scr[1:2, row_at])
        low_scores = grad_scores.astype(jnp.bfloat16)
        dv_scr[key_at, :] += nn(weights.astype(jnp.bfloat16), grads)
        dk_scr[key_at, :] += nn(low_scores, queries)
        dqt_scr[:, row_at] += nn(kt_scr[:, key_at], low_scores)
        return grad_scores

    if not causal:
        for low in range(0, keys, key_block):
            for at in range(0, rows, block):
                piece(slice(low, low + key_block), slice(at, at + block), lambda s: s, 0)
    else:
        for low in range(0, keys, block):
            for part in range(block // LANES):
                here = low + part * LANES
                width = block - part * LANES
                near = min(2 * LANES, width)

                def fix(scores, near=near):
                    head_part = scores[:, :near] + t_scr[:, :near]
                    if near == scores.shape[1]:
                        return head_part
                    return jnp.concatenate([head_part, scores[:, near:]], axis=1)

                grad = piece(slice(here, here + LANES), slice(here, low + block), fix, near)
                near_ref[0, :, :near] += grad[:, :near]
            for at in range(low + block, rows, block):
                if at == low + block:

                    def fix(scores):
                        top, bottom = scores[: block - LANES], scores[block - LANES :]
                        bottom = jnp.concatenate(
                            [bottom[:, :LANES] + t_scr[:, LANES:], bottom[:, LANES:]], axis=1
                        )
                        return jnp.concatenate([top, bottom], axis=0)
                else:
                    fix = lambda s: s
                grad = piece(slice(low, low + block), slice(at, at + block), fix, 0)
                if at == low + block:
                    near_ref[0, :, LANES:] += grad[block - LANES :, :LANES]

    @pl.when(last)
    def _():
        for low in range(0, rows, block):
            dq_ref[low : low + block, :] = dqt_scr[:, low : low + block].T.astype(jnp.bfloat16)
        dk_ref[...] = dk_scr[...].astype(jnp.bfloat16)
        dv_ref[...] = dv_scr[...].astype(jnp.bfloat16)


def attend_backward(queries, keys, values, grad_mixed, mixed, logsum, heads, head_size, padded=0, bias=None, length=None):
    causal = bias is not None
    rows, width = queries.shape
    count = keys.shape[0]
    per_tile = LANES // head_size
    width = padded or width
    tile = lambda h: (0, h // per_tile)
    row_spec = pl.BlockSpec((rows, LANES), tile)
    key_spec = pl.BlockSpec((count, LANES), tile)
    skip = padded // LANES
    key_specs = [pl.BlockSpec((count, LANES), lambda h, n=n: (0, n * skip + h // per_tile)) for n in (1, 2)]
    in_specs = [row_spec, *key_specs, row_spec, row_spec, pl.BlockSpec((1, 8, rows), lambda h: (h, 0, 0))]
    args = [queries, keys, values, grad_mixed, mixed, logsum]
    out_specs = [row_spec, key_spec, key_spec]
    out_shape = [
        jax.ShapeDtypeStruct((rows, width), jnp.bfloat16),
        jax.ShapeDtypeStruct((count, width), jnp.bfloat16),
        jax.ShapeDtypeStruct((count, width), jnp.bfloat16),
    ]
    scratch = [
        pltpu.VMEM((LANES, count), jnp.bfloat16),
        pltpu.VMEM((LANES, rows), jnp.float32),
        pltpu.VMEM((count, LANES), jnp.float32),
        pltpu.VMEM((count, LANES), jnp.float32),
    ]
    if causal:
        in_specs = [pl.BlockSpec(memory_space=pltpu.SMEM)] + in_specs + [pl.BlockSpec((1, 1, 3 * LANES), lambda h: (h, 0, 0))]
        args = [length] + args + [bias]
        out_specs = out_specs + [pl.BlockSpec((1, LANES, 2 * LANES), lambda h: (h, 0, 0))]
        out_shape = out_shape + [jax.ShapeDtypeStruct((heads, LANES, 2 * LANES), jnp.float32)]
        scratch = scratch + [pltpu.VMEM((LANES, 2 * LANES), jnp.float32)]
    scratch = scratch + [pltpu.VMEM((8, rows), jnp.float32)]
    return pl.pallas_call(
        functools.partial(attend_backward_kernel, causal=causal, head_size=head_size, heads=heads),
        grid=(heads,),
        in_specs=in_specs,
        out_specs=out_specs,
        out_shape=out_shape,
        scratch_shapes=scratch,
        compiler_params=pltpu.CompilerParams(vmem_limit_bytes=60 * 2**20),
        cost_estimate=pl.CostEstimate(
            flops=10 * heads * LANES * rows * count // (2 if causal else 1),
            bytes_accessed=8 * (rows + count) * width,
            transcendentals=heads * rows * count // (2 if causal else 1),
        ),
        name="self_backward" if causal else "cross_backward",
    )(*args)


bounds = np.ceil(16.0 * 8.0 ** (np.arange(1, 16) / 16.0)).astype(np.int32)


def buckets(distance):
    far = 16 + jnp.sum((distance[..., None] >= jnp.asarray(bounds)).astype(jnp.int32), axis=-1)
    return jnp.where(distance < 16, distance, far)


def bias_rows(table):
    count = table.shape[0]
    place = jnp.arange(3 * LANES, dtype=jnp.int32)

    def row(distance, outside):
        onehot = buckets(jnp.clip(distance, 0, 2 * LANES))[None, :] == jnp.arange(count, dtype=jnp.int32)[:, None]
        relative = table - table[count - 1 :]
        values = jnp.sum(jnp.where(onehot[:, None, :], relative[:, :, None], 0.0), axis=0)
        return jnp.where(outside[None], negative, values)[:, None, :]

    forward = row(jnp.where(place < 2 * LANES, LANES - place, 2 * LANES), (place > LANES) & (place < 2 * LANES))
    backward = row(place, place >= 2 * LANES)
    return forward, backward


def matmul_t(left, right):
    return nt(left, right)


def inner_rows(left, right):
    return lax.dot_general(left, right, (((0,), (0,)), ((), ())), preferred_element_type=jnp.float32)


def rms_norm(values, gain):
    scale = lax.rsqrt(jnp.mean(values * values, axis=-1, keepdims=True) + epsilon)
    return values * scale * gain


def rms_back(values, gain, grad_normed):
    scale = lax.rsqrt(jnp.mean(values * values, axis=-1, keepdims=True) + epsilon)
    unit = values * scale
    grad_unit = grad_normed * gain
    grad_gain = jnp.sum(grad_normed * unit, axis=0)
    grad_values = scale * (grad_unit - unit * jnp.mean(grad_unit * unit, axis=-1, keepdims=True))
    return (grad_values, grad_gain)


def activate(gate, upper):
    return jax.nn.gelu(gate, approximate=True) * upper


def per_device(
    tokens, encoder, cotangent, lengths, gains, self_query, self_key, self_value, self_output,
    cross_query, cross_key, cross_value, cross_output, ffn_gate, ffn_up, ffn_down, rel_bias,
):
    both = ("seq", "fsdp")
    seq, fsdp = lax.axis_size("seq"), lax.axis_size("fsdp")
    world = seq * fsdp
    low = jnp.bfloat16
    share = self_query.shape[0]
    width = self_query.shape[1]
    hidden_share = ffn_down.shape[0]
    inner = ffn_gate.shape[1]
    rows = tokens.shape[1]
    group = rel_bias.shape[1]
    group_width = group * HEAD
    padded = -(-group_width // LANES) * LANES
    heads = width // HEAD
    place = lax.axis_index("seq")

    everyone = lax.all_gather(tokens[0], "seq", axis=0, tiled=True)
    encoded = lax.all_gather(encoder[0], "seq", axis=0, tiled=True)

    gain_share = gains.shape[1]
    gain_block = jnp.pad(gains.astype(low).reshape(1, -1), ((0, 7), (0, width - gains.size)))
    pack = jnp.concatenate(
        [w.astype(low) for w in (self_query, self_key, self_value, self_output, cross_query, cross_key, cross_value, cross_output)]
        + [gain_block],
        axis=0,
    )
    packed = lax.all_gather(pack, both, axis=0)
    gate_up = lax.all_gather(jnp.concatenate([ffn_gate.astype(low), ffn_up.astype(low)], axis=1), both, axis=0, tiled=True)
    w_down = lax.all_gather(ffn_down.astype(low), both, axis=0, tiled=True)

    def whole(number):
        return packed[:, number * share : (number + 1) * share].reshape(width, width)

    w_output, c_query, c_key, c_value, c_output = (whole(n) for n in range(3, 8))

    def own(number):
        cut = lax.dynamic_slice_in_dim(whole(number), place * group_width, group_width, 1)
        return jnp.pad(cut, ((0, 0), (0, padded - group_width)))

    w_qkv = jnp.concatenate([own(n) for n in range(3)], axis=1)
    gain_rows = packed[:, 8 * share, : gains.size].reshape(world, 3, gain_share).transpose(1, 0, 2).reshape(3, width).astype(jnp.float32)

    length = lengths[0]
    values_in = tokens[0].astype(jnp.float32)
    normed_all = rms_norm(everyone.astype(jnp.float32), gain_rows[0]).astype(low)
    qkv = nn(normed_all, w_qkv).astype(low)
    base_forward, base_backward = bias_rows(rel_bias)
    own_mixed, own_logsum = attend_forward(qkv, qkv, qkv, group, HEAD, padded, base_forward, lengths)
    mixed = lax.all_to_all(own_mixed[:, :group_width], "seq", split_axis=0, concat_axis=1, tiled=True)
    attended = values_in + nn(mixed, w_output)
    normed_two = rms_norm(attended, gain_rows[1]).astype(low)
    cross_queries = nn(normed_two, c_query).astype(low)
    cross_keys = nn(encoded, c_key).astype(low)
    cross_values = nn(encoded, c_value).astype(low)
    cross_mixed, cross_logsum = attend_forward(cross_queries, cross_keys, cross_values, heads, HEAD)
    crossed = attended + nn(cross_mixed, c_output)
    normed_three = rms_norm(crossed, gain_rows[2]).astype(low)
    both_parts = nn(normed_three, gate_up)
    gate, upper = both_parts[:, :inner], both_parts[:, inner:]
    hidden = activate(gate, upper).astype(low)
    result = crossed + nn(hidden, w_down)

    positions = place * rows + jnp.arange(rows, dtype=jnp.int32)
    grad_out = cotangent[0].astype(jnp.float32) * (positions < length).astype(jnp.float32)[:, None]
    grad_ffn = grad_out.astype(low)
    grad_down = inner_rows(hidden, grad_ffn).astype(low)
    share_down = lax.psum_scatter(grad_down, both, scatter_dimension=0, tiled=True)
    grad_hidden = matmul_t(grad_ffn, w_down)
    _, pullback = jax.vjp(activate, gate, upper)
    grad_gate, grad_upper = pullback(grad_hidden)
    grad_both = jnp.concatenate([grad_gate.astype(low), grad_upper.astype(low)], axis=1)
    grad_gate_up = inner_rows(normed_three, grad_both).astype(low)
    share_gate_up = lax.psum_scatter(grad_gate_up, both, scatter_dimension=0, tiled=True)
    grad_normed_three = matmul_t(grad_both, gate_up)
    norm_part, grad_gain_two = rms_back(crossed, gain_rows[2], grad_normed_three)
    grad_crossed = grad_out + norm_part
    grad_branch = grad_crossed.astype(low)
    grad_coutput = inner_rows(cross_mixed, grad_branch).astype(low)
    grad_cmixed = matmul_t(grad_branch, c_output).astype(low)
    grad_cq, grad_ck, grad_cv = attend_backward(
        cross_queries, cross_keys, cross_values, grad_cmixed, cross_mixed, cross_logsum, heads, HEAD
    )
    grad_cquery = inner_rows(normed_two, grad_cq).astype(low)
    grad_ckey = inner_rows(encoded, grad_ck).astype(low)
    grad_cvalue = inner_rows(encoded, grad_cv).astype(low)
    grad_encoded_part = (matmul_t(grad_ck, c_key) + matmul_t(grad_cv, c_value)).astype(low)
    grad_encoded = lax.psum_scatter(grad_encoded_part, "seq", scatter_dimension=0, tiled=True).astype(jnp.float32)
    norm_part, grad_gain_one = rms_back(attended, gain_rows[1], matmul_t(grad_cq, c_query))
    grad_attended = grad_crossed + norm_part
    grad_self_branch = grad_attended.astype(low)
    grad_output = inner_rows(mixed, grad_self_branch).astype(low)
    grad_mixed = matmul_t(grad_self_branch, w_output).astype(low)
    share_square = lax.psum_scatter(
        jnp.concatenate([grad_output, grad_cquery, grad_ckey, grad_cvalue, grad_coutput], axis=1),
        both, scatter_dimension=0, tiled=True,
    )
    own_grad_mixed = lax.all_to_all(grad_mixed, "seq", split_axis=1, concat_axis=0, tiled=True)
    own_grad_mixed = jnp.pad(own_grad_mixed, ((0, 0), (0, padded - group_width)))
    own_dq, own_dk, own_dv, near = attend_backward(
        qkv, qkv, qkv, own_grad_mixed, own_mixed, own_logsum, group, HEAD, padded, base_backward, lengths
    )
    own_qkv = jnp.concatenate([own_dq, own_dk, own_dv], axis=1)
    grad_normed = lax.psum_scatter(matmul_t(own_qkv, w_qkv).astype(low), "seq", scatter_dimension=0, tiled=True)
    grad_own = inner_rows(normed_all, own_qkv).astype(low)
    grad_own = grad_own.reshape(seq, fsdp, share, 3 * padded).transpose(1, 0, 2, 3)
    grad_own = lax.psum_scatter(grad_own, "fsdp", scatter_dimension=0, tiled=True)[0]
    grad_own = lax.all_to_all(grad_own, "seq", split_axis=0, concat_axis=0, tiled=True)
    grad_own = grad_own.reshape(seq, share, 3, padded)[:, :, :, :group_width].transpose(2, 1, 0, 3).reshape(3, share, width)

    norm_part, grad_gain_zero = rms_back(values_in, gain_rows[0], grad_normed.astype(jnp.float32))
    grad_input = grad_attended + norm_part
    grad_gains = jnp.stack([grad_gain_zero, grad_gain_one, grad_gain_two])
    share_gains = lax.psum_scatter(grad_gains, both, scatter_dimension=1, tiled=True)

    bins = rel_bias.shape[0]
    skew = jnp.pad(near.reshape(group, -1), ((0, 0), (0, LANES))).reshape(group, LANES, 2 * LANES + 1)
    by_distance = jnp.sum(skew[:, :, :LANES], axis=1)
    near_map = (buckets(jnp.arange(LANES, dtype=jnp.int32))[:, None] == jnp.arange(bins - 1, dtype=jnp.int32)[None]).astype(jnp.float32)
    near_sums = jnp.dot(near_map.T, by_distance.T, precision=highest)
    grad_table = jnp.concatenate([near_sums, -jnp.sum(near_sums, axis=0, keepdims=True)], axis=0)
    table_grad = lax.psum(grad_table, "fsdp")

    wide = jnp.float32
    outputs = [share_square[:, n * width : (n + 1) * width].astype(wide) for n in range(5)]
    own_outputs = [grad_own[n].astype(wide) for n in range(3)]
    return (
        result.astype(low)[None], grad_input[None], grad_encoded[None], share_gains,
        *own_outputs, *outputs,
        share_gate_up[:, :inner].astype(wide), share_gate_up[:, inner:].astype(wide), share_down.astype(wide),
        table_grad,
    )


def solution(mesh):
    split = P(("seq", "fsdp"), None)
    rows = P("fsdp", "seq", None)
    gains = P(None, ("seq", "fsdp"))
    return jax.shard_map(
        per_device,
        mesh=mesh,
        in_specs=(rows, rows, rows, P("fsdp"), gains, *([split] * 11), P(None, "seq")),
        out_specs=(rows, rows, rows, gains, *([split] * 11), P(None, "seq")),
        check_vma=False,
    )
```

```python
import functools
import jax
import jax.numpy as jnp
import numpy as np
from jax import lax
from jax.experimental import pallas as pl
from jax.experimental.pallas import tpu as pltpu
from jax.sharding import PartitionSpec as P

LANES = 128
BLOCK = 512
negative = -1e30
epsilon = 1e-06
highest = lax.Precision.HIGHEST
HEAD = 64


def nt(left, right):
    return lax.dot_general(left, right, (((1,), (1,)), ((), ())), preferred_element_type=jnp.float32)


def nn(left, right):
    return jnp.dot(left, right, preferred_element_type=jnp.float32)


def half_mask(head, head_size):
    lane = lax.broadcasted_iota(jnp.int32, (1, LANES), 1)
    per_tile = LANES // head_size
    return (lane // head_size) == (head % per_tile)


def attend_forward_kernel(*refs, causal, head_size):
    if causal:
        length_ref, q_ref, k_ref, v_ref, base_ref, o_ref, lse_ref, s_scr, p_scr, t_scr = refs
        length = length_ref[0]
    else:
        q_ref, k_ref, v_ref, o_ref, lse_ref, s_scr, p_scr = refs
    head = pl.program_id(0)
    first = (head % (LANES // head_size)) == 0
    mask = half_mask(head, head_size)
    rows, keys = q_ref.shape[0], k_ref.shape[0]
    block = min(BLOCK, rows)
    if causal:
        wide = jnp.broadcast_to(base_ref[0], (LANES, 3 * LANES))
        t_scr[...] = pltpu.roll(wide, 0, 1, stride=1, stride_axis=0)[:, : 2 * LANES]
    for number in range(rows // block):
        start = number * block
        queries = jnp.where(mask, q_ref[start : start + block, :], 0)
        total = start + block if causal else keys
        for low in range(0, total, BLOCK):
            high = min(low + BLOCK, total)
            s_scr[:, low:high] = nt(queries, k_ref[low:high, :])
        if causal:
            for part in range(block // LANES):
                at = slice(part * LANES, (part + 1) * LANES)
                column = start + part * LANES
                if column > 0:
                    s_scr[at, column - LANES : column + LANES] += t_scr[...]
                else:
                    s_scr[at, :LANES] += t_scr[:, LANES:]
            for low in range(0, total, BLOCK):
                high = min(low + BLOCK, total)

                @pl.when(length < high)
                def _(low=low, high=high):
                    place = low + lax.broadcasted_iota(jnp.int32, (block, high - low), 1)
                    s_scr[:, low:high] = jnp.where(place < length, s_scr[:, low:high], negative)

        sums = []
        for part in range(block // LANES):
            at = slice(part * LANES, (part + 1) * LANES)
            width = start + (part + 1) * LANES if causal else keys
            scores = s_scr[at, :width]
            largest = jnp.max(scores, axis=1, keepdims=True)
            expos = jnp.exp(scores - largest)
            totals = jnp.sum(expos, axis=1, keepdims=True)
            p_scr[at, :width] = expos.astype(jnp.bfloat16)
            if width < total:
                p_scr[at, width:total] = jnp.zeros((LANES, total - width), jnp.bfloat16)
            logsum = jnp.broadcast_to(largest + jnp.log(totals), (LANES, LANES))
            lse_ref[0, :, start + part * LANES : start + (part + 1) * LANES] = logsum.T[:8]
            sums.append(totals)
        mixed = nn(p_scr[:, :total], v_ref[:total, :])
        mixed = mixed / jnp.concatenate(sums, axis=0)
        before = jnp.where(first, jnp.zeros_like(mixed), o_ref[start : start + block, :].astype(jnp.float32))
        o_ref[start : start + block, :] = jnp.where(mask, mixed, before).astype(jnp.bfloat16)


def attend_forward(queries, keys, values, heads, head_size, padded=0, bias=None, length=None):
    causal = bias is not None
    rows, width = queries.shape
    count = keys.shape[0]
    per_tile = LANES // head_size
    block = min(BLOCK, rows)
    width = padded or width
    tile = lambda h: (0, h // per_tile)
    row_spec = pl.BlockSpec((rows, LANES), tile)
    skip = padded // LANES
    key_specs = [pl.BlockSpec((count, LANES), lambda h, n=n: (0, n * skip + h // per_tile)) for n in (1, 2)]
    in_specs = [row_spec, *key_specs]
    args = [queries, keys, values]
    scratch = [pltpu.VMEM((block, count), jnp.float32), pltpu.VMEM((block, count), jnp.bfloat16)]
    if causal:
        in_specs = [pl.BlockSpec(memory_space=pltpu.SMEM)] + in_specs + [pl.BlockSpec((1, 1, 3 * LANES), lambda h: (h, 0, 0))]
        args = [length] + args + [bias]
        scratch = scratch + [pltpu.VMEM((LANES, 2 * LANES), jnp.float32)]
    return pl.pallas_call(
        functools.partial(attend_forward_kernel, causal=causal, head_size=head_size),
        grid=(heads,),
        in_specs=in_specs,
        out_specs=[row_spec, pl.BlockSpec((1, 8, rows), lambda h: (h, 0, 0))],
        out_shape=[
            jax.ShapeDtypeStruct((rows, width), jnp.bfloat16),
            jax.ShapeDtypeStruct((heads, 8, rows), jnp.float32),
        ],
        scratch_shapes=scratch,
        compiler_params=pltpu.CompilerParams(vmem_limit_bytes=60 * 2**20),
        cost_estimate=pl.CostEstimate(
            flops=4 * heads * LANES * rows * count // (2 if causal else 1),
            bytes_accessed=4 * (rows + count) * width,
            transcendentals=heads * rows * count // (2 if causal else 1),
        ),
        name="self_forward" if causal else "cross_forward",
    )(*args)


def attend_backward_kernel(*refs, causal, head_size, heads):
    if causal:
        (length_ref, q_ref, k_ref, v_ref, do_ref, o_ref, lse_ref, base_ref, dq_ref, dk_ref, dv_ref, near_ref,
         kt_scr, dqt_scr, dk_scr, dv_scr, t_scr, row_scr) = refs
        length = length_ref[0]
    else:
        (q_ref, k_ref, v_ref, do_ref, o_ref, lse_ref, dq_ref, dk_ref, dv_ref,
         kt_scr, dqt_scr, dk_scr, dv_scr, row_scr) = refs
    head = pl.program_id(0)
    per_tile = LANES // head_size
    first = (head % per_tile) == 0
    last = ((head % per_tile) == per_tile - 1) | (head == heads - 1)
    mask = half_mask(head, head_size)
    rows, keys = q_ref.shape[0], k_ref.shape[0]
    block = min(BLOCK, rows)
    key_block = min(BLOCK, keys)

    @pl.when(first)
    def _():
        dqt_scr[...] = jnp.zeros_like(dqt_scr)
        dk_scr[...] = jnp.zeros_like(dk_scr)
        dv_scr[...] = jnp.zeros_like(dv_scr)

    if causal:
        wide = jnp.broadcast_to(base_ref[0], (LANES, 3 * LANES))
        t_scr[...] = pltpu.roll(wide, 0, 1, stride=1, stride_axis=0)[:, : 2 * LANES]
        near_ref[0] = jnp.zeros((LANES, 2 * LANES), jnp.float32)
    for low in range(0, keys, key_block):
        kt_scr[:, low : low + key_block] = jnp.where(mask, k_ref[low : low + key_block, :], 0).T
    for low in range(0, rows, block):
        at = slice(low, low + block)
        product = do_ref[at, :].astype(jnp.float32) * o_ref[at, :].astype(jnp.float32)
        delta = jnp.sum(jnp.where(mask, product, 0.0).T, axis=0, keepdims=True)
        logsum = lse_ref[0, 0:1, at]
        if causal:
            place = low + lax.broadcasted_iota(jnp.int32, (1, block), 1)
            logsum = jnp.where(place < length, logsum, -negative)
        row_scr[0:1, at] = logsum
        row_scr[1:2, at] = delta

    def piece(key_at, row_at, score_fix, near_width):
        queries = jnp.where(mask, q_ref[row_at, :], 0)
        grads = jnp.where(mask, do_ref[row_at, :], 0)
        scores = score_fix(nt(k_ref[key_at, :], queries))
        weights = jnp.exp(scores - row_scr[0:1, row_at])
        grad_weights = nt(v_ref[key_at, :], grads)
        grad_scores = weights * (grad_weights - row_scr[1:2, row_at])
        low_scores = grad_scores.astype(jnp.bfloat16)
        dv_scr[key_at, :] += nn(weights.astype(jnp.bfloat16), grads)
        dk_scr[key_at, :] += nn(low_scores, queries)
        dqt_scr[:, row_at] += nn(kt_scr[:, key_at], low_scores)
        return grad_scores

    if not causal:
        for low in range(0, keys, key_block):
            for at in range(0, rows, block):
                piece(slice(low, low + key_block), slice(at, at + block), lambda s: s, 0)
    else:
        for low in range(0, keys, block):
            for part in range(block // LANES):
                here = low + part * LANES
                width = block - part * LANES
                near = min(2 * LANES, width)

                def fix(scores, near=near):
                    head_part = scores[:, :near] + t_scr[:, :near]
                    if near == scores.shape[1]:
                        return head_part
                    return jnp.concatenate([head_part, scores[:, near:]], axis=1)

                grad = piece(slice(here, here + LANES), slice(here, low + block), fix, near)
                near_ref[0, :, :near] += grad[:, :near]
            for at in range(low + block, rows, block):
                if at == low + block:

                    def fix(scores):
                        top, bottom = scores[: block - LANES], scores[block - LANES :]
                        bottom = jnp.concatenate(
                            [bottom[:, :LANES] + t_scr[:, LANES:], bottom[:, LANES:]], axis=1
                        )
                        return jnp.concatenate([top, bottom], axis=0)
                else:
                    fix = lambda s: s
                grad = piece(slice(low, low + block), slice(at, at + block), fix, 0)
                if at == low + block:
                    near_ref[0, :, LANES:] += grad[block - LANES :, :LANES]

    @pl.when(last)
    def _():
        for low in range(0, rows, block):
            dq_ref[low : low + block, :] = dqt_scr[:, low : low + block].T.astype(jnp.bfloat16)
        dk_ref[...] = dk_scr[...].astype(jnp.bfloat16)
        dv_ref[...] = dv_scr[...].astype(jnp.bfloat16)


def attend_backward(queries, keys, values, grad_mixed, mixed, logsum, heads, head_size, padded=0, bias=None, length=None):
    causal = bias is not None
    rows, width = queries.shape
    count = keys.shape[0]
    per_tile = LANES // head_size
    width = padded or width
    tile = lambda h: (0, h // per_tile)
    row_spec = pl.BlockSpec((rows, LANES), tile)
    key_spec = pl.BlockSpec((count, LANES), tile)
    skip = padded // LANES
    key_specs = [pl.BlockSpec((count, LANES), lambda h, n=n: (0, n * skip + h // per_tile)) for n in (1, 2)]
    in_specs = [row_spec, *key_specs, row_spec, row_spec, pl.BlockSpec((1, 8, rows), lambda h: (h, 0, 0))]
    args = [queries, keys, values, grad_mixed, mixed, logsum]
    out_specs = [row_spec, key_spec, key_spec]
    out_shape = [
        jax.ShapeDtypeStruct((rows, width), jnp.bfloat16),
        jax.ShapeDtypeStruct((count, width), jnp.bfloat16),
        jax.ShapeDtypeStruct((count, width), jnp.bfloat16),
    ]
    scratch = [
        pltpu.VMEM((LANES, count), jnp.bfloat16),
        pltpu.VMEM((LANES, rows), jnp.float32),
        pltpu.VMEM((count, LANES), jnp.float32),
        pltpu.VMEM((count, LANES), jnp.float32),
    ]
    if causal:
        in_specs = [pl.BlockSpec(memory_space=pltpu.SMEM)] + in_specs + [pl.BlockSpec((1, 1, 3 * LANES), lambda h: (h, 0, 0))]
        args = [length] + args + [bias]
        out_specs = out_specs + [pl.BlockSpec((1, LANES, 2 * LANES), lambda h: (h, 0, 0))]
        out_shape = out_shape + [jax.ShapeDtypeStruct((heads, LANES, 2 * LANES), jnp.float32)]
        scratch = scratch + [pltpu.VMEM((LANES, 2 * LANES), jnp.float32)]
    scratch = scratch + [pltpu.VMEM((8, rows), jnp.float32)]
    return pl.pallas_call(
        functools.partial(attend_backward_kernel, causal=causal, head_size=head_size, heads=heads),
        grid=(heads,),
        in_specs=in_specs,
        out_specs=out_specs,
        out_shape=out_shape,
        scratch_shapes=scratch,
        compiler_params=pltpu.CompilerParams(vmem_limit_bytes=60 * 2**20),
        cost_estimate=pl.CostEstimate(
            flops=10 * heads * LANES * rows * count // (2 if causal else 1),
            bytes_accessed=8 * (rows + count) * width,
            transcendentals=heads * rows * count // (2 if causal else 1),
        ),
        name="self_backward" if causal else "cross_backward",
    )(*args)


bounds = np.ceil(16.0 * 8.0 ** (np.arange(1, 16) / 16.0)).astype(np.int32)


def buckets(distance):
    far = 16 + jnp.sum((distance[..., None] >= jnp.asarray(bounds)).astype(jnp.int32), axis=-1)
    return jnp.where(distance < 16, distance, far)


def bias_rows(table):
    count = table.shape[0]
    place = jnp.arange(3 * LANES, dtype=jnp.int32)

    def row(distance, outside):
        onehot = buckets(jnp.clip(distance, 0, 2 * LANES))[None, :] == jnp.arange(count, dtype=jnp.int32)[:, None]
        relative = table - table[count - 1 :]
        values = jnp.sum(jnp.where(onehot[:, None, :], relative[:, :, None], 0.0), axis=0)
        return jnp.where(outside[None], negative, values)[:, None, :]

    forward = row(jnp.where(place < 2 * LANES, LANES - place, 2 * LANES), (place > LANES) & (place < 2 * LANES))
    backward = row(place, place >= 2 * LANES)
    return forward, backward


MESH = pl.DeviceIdType.MESH


def coordinates():
    place, slot = lax.axis_index("seq"), lax.axis_index("fsdp")
    return place // 2, lax.rem(place, 2), slot // 2, lax.rem(slot, 2)


def device(x, c, z, y):
    return (x * 2 + c, z * 2 + y)


def greet(others):
    barrier = pltpu.get_barrier_semaphore()
    for other in others:
        pl.semaphore_signal(barrier, inc=1, device_id=other, device_id_type=MESH)
    pl.semaphore_wait(barrier, len(others))


class Copies:
    def __init__(self, send_sem, recv_sem):
        self.send_sem, self.recv_sem, self.made = send_sem, recv_sem, []

    def send(self, source, target, other):
        number = len(self.made)
        copy = pltpu.make_async_remote_copy(
            src_ref=source, dst_ref=target, send_sem=self.send_sem.at[number], recv_sem=self.recv_sem.at[number],
            device_id=other, device_id_type=MESH,
        )
        copy.start()
        self.made.append(copy)
        return copy

    def finish(self):
        for copy in self.made:
            copy.wait_send()


def gather_kernel(nz, tok, enc, own, squares, gain, everyone, encoded, qkv_out, squares_out, gain_out, send_sem, recv_sem, local_sem):
    x, c, z, y = coordinates()
    flat = device(1 - x, c, z, y), device(x, 1 - c, z, y), device(1 - x, 1 - c, z, y)
    by_x, by_core, diagonal = flat
    by_y = device(x, c, z, 1 - y)
    steps = [lax.rem(z + t, nz) for t in range(nz)]
    backs = [lax.rem(z - t + nz, nz) for t in range(nz)]
    by_z = [device(x, c, steps[t], y) for t in range(nz)]
    greet([*flat, by_y, *by_z[1:]])
    copies = Copies(send_sem, recv_sem)
    local = [
        pltpu.make_async_copy(source, target, local_sem.at[n])
        for n, (source, target) in enumerate(
            [
                (own.at[x, c], qkv_out.at[x, c, z, y]),
                (tok, everyone.at[x, c]),
                (enc, encoded.at[x, c]),
                (squares, squares_out.at[:, x, c, z, y]),
                (gain, gain_out.at[x, c, z, y]),
            ]
        )
    ]
    for copy in local:
        copy.start()
    first = [
        copies.send(own.at[1 - x, c], qkv_out.at[x, c, z, y], by_x),
        copies.send(own.at[x, 1 - c], qkv_out.at[x, c, z, y], by_core),
        copies.send(own.at[1 - x, 1 - c], qkv_out.at[x, c, z, y], diagonal),
    ]
    rows_x = [copies.send(enc, encoded.at[x, c], by_x), copies.send(tok, everyone.at[x, c], by_x)]
    rows_core = [copies.send(enc, encoded.at[x, c], by_core), copies.send(tok, everyone.at[x, c], by_core)]

    def relay(xx, cc, zz, yy, other):
        return [
            copies.send(squares_out.at[:, xx, cc, zz, yy], squares_out.at[:, xx, cc, zz, yy], other),
            copies.send(gain_out.at[xx, cc, zz, yy], gain_out.at[xx, cc, zz, yy], other),
        ]

    def fresh(other):
        return [
            copies.send(squares, squares_out.at[:, x, c, z, y], other),
            copies.send(gain, gain_out.at[x, c, z, y], other),
        ]

    def arrive(pair):
        for copy in pair:
            copy.wait_recv()

    for copy in local:
        copy.wait()
    arrive(first)
    qkv_z = [None] + [copies.send(qkv_out.at[:, :, z, y], qkv_out.at[:, :, z, y], by_z[t]) for t in range(1, nz)]
    qkv_y = [copies.send(qkv_out.at[:, :, z, y], qkv_out.at[:, :, z, y], by_y)]
    squares_z = [None] + [fresh(by_z[t]) for t in range(1, nz)]
    squares_y, squares_x, squares_core = [fresh(by_y)], [fresh(by_x)], [fresh(by_core)]
    for t in range(1, nz):
        qkv_z[t].wait_recv()
        qkv_y.append(copies.send(qkv_out.at[:, :, backs[t], y], qkv_out.at[:, :, backs[t], y], by_y))
    for t in range(1, nz):
        arrive(squares_z[t])
        squares_y.append(relay(x, c, backs[t], y, by_y))
        squares_x.append(relay(x, c, backs[t], y, by_x))
        squares_core.append(relay(x, c, backs[t], y, by_core))
    for copy, target in zip(rows_x, (encoded, everyone)):
        copy.wait_recv()
        rows_core.append(copies.send(target.at[1 - x, c], target.at[1 - x, c], by_core))
    corner = []
    for t in range(nz):
        arrive(squares_x[t])
        if t % 2 == 0:
            corner.append(relay(1 - x, c, backs[t], y, by_y))
        squares_core.append(relay(1 - x, c, backs[t], y, by_core))
        arrive(squares_y[t])
        if t % 2 == 1:
            corner.append(relay(x, c, backs[t], 1 - y, by_x))
        squares_core.append(relay(x, c, backs[t], 1 - y, by_core))
    for t in range(nz):
        arrive(corner[t])
        squares_core.append(relay(1 - x, c, backs[t], 1 - y, by_core))
    for copy in qkv_y + rows_core:
        copy.wait_recv()
    for pair in squares_core:
        arrive(pair)
    copies.finish()


def gather(nz, tok, enc, own, squares, gain):
    count, share, width = squares.shape
    everywhere = (2, 2, nz, 2)
    shapes = [
        jax.ShapeDtypeStruct((2, 2, *tok.shape), tok.dtype),
        jax.ShapeDtypeStruct((2, 2, *enc.shape), enc.dtype),
        jax.ShapeDtypeStruct((*everywhere, share, own.shape[-1]), own.dtype),
        jax.ShapeDtypeStruct((count, *everywhere, share, width), squares.dtype),
        jax.ShapeDtypeStruct((*everywhere, *gain.shape), gain.dtype),
    ]
    total = 3 + 6 + 2 * nz - 1 + 2 * (nz - 1 + 2 * nz + nz + 4 * nz)
    return pl.pallas_call(
        functools.partial(gather_kernel, nz),
        in_specs=[pl.BlockSpec(memory_space=pltpu.VMEM)] * 5,
        out_specs=[pl.BlockSpec(memory_space=pl.ANY)] * 5,
        out_shape=shapes,
        scratch_shapes=[
            pltpu.SemaphoreType.DMA((total,)), pltpu.SemaphoreType.DMA((total,)), pltpu.SemaphoreType.DMA((5,)),
        ],
        compiler_params=pltpu.CompilerParams(collective_id=0, has_side_effects=True, vmem_limit_bytes=8 * 2**20),
        name="gather",
    )(tok, enc, own, squares, gain)


def add_low(target, left, right):
    @pl.loop(0, left.shape[0])
    def _(n):
        target[n] = (left[n].astype(jnp.float32) + right[n].astype(jnp.float32)).astype(target.dtype)


def reduce_kernel(
    nz, count, *refs
):
    squares = refs[:count]
    own, tok, enc, gain, near = refs[count : count + 5]
    out_squares, out_own, out_tok, out_enc, out_gain, out_near = refs[count + 5 : count + 11]
    (sq_a, sq_ra, sq_b, sq_rb, sq_c, sq_rc, sq_rd, own_r, own_a, own_rz, own_f,
     tok_r, tok_a, tok_rx, enc_r, enc_a, enc_rx, gain_r, near_r, send_sem, recv_sem) = refs[count + 11 :]
    x, c, z, y = coordinates()
    flat = device(1 - x, c, z, y), device(x, 1 - c, z, y), device(1 - x, 1 - c, z, y)
    by_x, by_core, diagonal = flat
    by_y = device(x, c, z, 1 - y)
    world = 8 * nz
    place, slot = lax.axis_index("seq"), lax.axis_index("fsdp")
    slots = 2 * nz
    me = place * slots + slot
    steps = [lax.rem(z + t, nz) for t in range(nz)]
    by_z = [device(x, c, steps[t], y) for t in range(nz)]
    barrier = pltpu.get_barrier_semaphore()

    @pl.loop(1, world)
    def _(t):
        other = lax.rem(me + t, world)
        pl.semaphore_signal(barrier, inc=1, device_id=(other // slots, lax.rem(other, slots)), device_id_type=MESH)

    pl.semaphore_wait(barrier, world - 1)
    copies = Copies(send_sem, recv_sem)
    tok_core = copies.send(tok.at[:, 1 - c], tok_r, by_core)
    enc_core = copies.send(enc.at[:, 1 - c], enc_r, by_core)
    own_y = copies.send(own.at[:, :, :, 1 - y], own_r, by_y)
    sq_core = [copies.send(squares[n].at[:, 1 - c], sq_ra.at[n], by_core) for n in range(count)]
    near_all = []
    for t in range(1, slots):
        other = lax.rem(slot + t, slots)
        near_all.append(copies.send(near, near_r.at[t - 1], (place, other)))

    def gain_copy(t):
        other = lax.rem(me + t, world)
        return pltpu.make_async_remote_copy(
            src_ref=gain.at[other], dst_ref=gain_r.at[t - 1], send_sem=send_sem.at[t - 1 + base_gain],
            recv_sem=recv_sem.at[t - 1 + base_gain],
            device_id=(other // slots, lax.rem(other, slots)), device_id_type=MESH,
        )

    base_gain = send_sem.shape[0] - (world - 1)

    @pl.loop(1, world)
    def _(t):
        gain_copy(t).start()

    tok_core.wait_recv()
    for half in range(2):
        add_low(tok_a.at[half], tok.at[half, c], tok_r.at[half])
    tok_x = copies.send(tok_a.at[1 - x], tok_rx, by_x)
    enc_core.wait_recv()
    for half in range(2):
        add_low(enc_a.at[half], enc.at[half, c], enc_r.at[half])
    enc_x = copies.send(enc_a.at[1 - x], enc_rx, by_x)

    sq_y, sq_x, sq_z = [], [], []
    for n in range(count):
        sq_core[n].wait_recv()

        for half in range(2):
            for side in range(2):
                add_low(sq_a.at[n, half, :, side], squares[n].at[half, c, :, side], sq_ra.at[n, half, :, side])
        sq_y.append(copies.send(sq_a.at[n, :, :, 1 - y], sq_rb.at[n], by_y))

    own_y.wait_recv()
    for half in range(2):
        for core in range(2):
            add_low(own_a.at[half, core], own.at[half, core, :, y], own_r.at[half, core])
    own_z = [copies.send(own_a.at[:, :, steps[t]], own_rz.at[t - 1], by_z[t]) for t in range(1, nz)]
    for n in range(count):
        sq_y[n].wait_recv()
        for half in range(2):
            add_low(sq_b.at[n, half], sq_a.at[n, half, :, y], sq_rb.at[n, half])
        sq_x.append(copies.send(sq_b.at[n, 1 - x], sq_rc.at[n], by_x))
    for copy in own_z:
        copy.wait_recv()
    for half in range(2):
        for core in range(2):
            total = own_a[half, core, z].astype(jnp.float32)
            for t in range(nz - 1):
                total += own_rz[t, half, core].astype(jnp.float32)
            own_f[half, core] = total.astype(own_f.dtype)
    own_seq = [
        copies.send(own_f.at[1 - x, c], out_own.at[x, c], by_x),
        copies.send(own_f.at[x, 1 - c], out_own.at[x, c], by_core),
        copies.send(own_f.at[1 - x, 1 - c], out_own.at[x, c], diagonal),
    ]
    out_own[x, c] = own_f[x, c]
    for n in range(count):
        sq_x[n].wait_recv()
        add_low(sq_c.at[n], sq_b.at[n, x], sq_rc.at[n])
        sq_z.append([copies.send(sq_c.at[n, steps[t]], sq_rd.at[n, t - 1], by_z[t]) for t in range(1, nz)])
    tok_x.wait_recv()
    add_low(out_tok, tok_a.at[x], tok_rx)
    enc_x.wait_recv()
    add_low(out_enc, enc_a.at[x], enc_rx)
    for n in range(count):
        for copy in sq_z[n]:
            copy.wait_recv()
        total = sq_c[n, z].astype(jnp.float32)
        for t in range(nz - 1):
            total += sq_rd[n, t].astype(jnp.float32)
        out_squares[n] = total
    for copy in near_all:
        copy.wait_recv()
    total = near[...]
    for t in range(slots - 1):
        total += near_r[t]
    out_near[...] = total
    out_gain[...] = gain[me]

    @pl.loop(1, world)
    def _(t):
        gain_copy(t).wait_recv()
        out_gain[...] += gain_r[t - 1]

    for copy in own_seq:
        copy.wait_recv()
    copies.finish()

    @pl.loop(1, world)
    def _(t):
        gain_copy(t).wait_send()


def reduce(nz, squares, own, tok, enc, gain, near):
    count = len(squares)
    share, width = squares[0].shape[-2:]
    low = jnp.bfloat16
    vmem = lambda *shape: pltpu.VMEM(shape, low)
    tok_slabs, enc_slabs = tok.shape[2:], enc.shape[2:]
    world = 8 * nz
    total = 3 + count + 2 * nz - 1 + 2 + count * 2 + (nz - 1) * (count + 1) + 3 + world - 1
    wide = own.shape[-1]
    return pl.pallas_call(
        functools.partial(reduce_kernel, nz, count),
        in_specs=[pl.BlockSpec(memory_space=pltpu.VMEM)] * (count + 5),
        out_specs=[pl.BlockSpec(memory_space=pltpu.VMEM)] * 6,
        out_shape=[
            jax.ShapeDtypeStruct((count, share, width), jnp.float32),
            jax.ShapeDtypeStruct((2, 2, share, wide), low),
            jax.ShapeDtypeStruct(tok_slabs, jnp.float32),
            jax.ShapeDtypeStruct(enc_slabs, jnp.float32),
            jax.ShapeDtypeStruct(gain.shape[1:], jnp.float32),
            jax.ShapeDtypeStruct(near.shape, jnp.float32),
        ],
        scratch_shapes=[
            vmem(count, 2, nz, 2, share, width), vmem(count, 2, nz, 2, share, width),
            vmem(count, 2, nz, share, width), vmem(count, 2, nz, share, width),
            vmem(count, nz, share, width), vmem(count, nz, share, width),
            vmem(count, nz - 1, share, width),
            vmem(2, 2, nz, share, wide), vmem(2, 2, nz, share, wide), vmem(nz - 1, 2, 2, share, wide), vmem(2, 2, share, wide),
            vmem(2, *tok_slabs), vmem(2, *tok_slabs), vmem(*tok_slabs),
            vmem(2, *enc_slabs), vmem(2, *enc_slabs), vmem(*enc_slabs),
            pltpu.VMEM((world - 1, *gain.shape[1:]), jnp.float32),
            pltpu.VMEM((2 * nz - 1, *near.shape), jnp.float32),
            pltpu.SemaphoreType.DMA((total,)), pltpu.SemaphoreType.DMA((total,)),
        ],
        compiler_params=pltpu.CompilerParams(collective_id=1, has_side_effects=True, vmem_limit_bytes=60 * 2**20),
        name="reduce",
    )(*squares, own, tok, enc, gain, near)


def matmul_t(left, right):
    return nt(left, right)


def inner_rows(left, right):
    return lax.dot_general(left, right, (((0,), (0,)), ((), ())), preferred_element_type=jnp.float32)


def rms_norm(values, gain):
    scale = lax.rsqrt(jnp.mean(values * values, axis=-1, keepdims=True) + epsilon)
    return values * scale * gain


def rms_back(values, gain, grad_normed):
    scale = lax.rsqrt(jnp.mean(values * values, axis=-1, keepdims=True) + epsilon)
    unit = values * scale
    grad_unit = grad_normed * gain
    grad_gain = jnp.sum(grad_normed * unit, axis=0)
    grad_values = scale * (grad_unit - unit * jnp.mean(grad_unit * unit, axis=-1, keepdims=True))
    return (grad_values, grad_gain)


def activate(gate, upper):
    return jax.nn.gelu(gate, approximate=True) * upper


def per_device(
    tokens, encoder, cotangent, lengths, gains, self_query, self_key, self_value, self_output,
    cross_query, cross_key, cross_value, cross_output, ffn_gate, ffn_up, ffn_down, rel_bias,
):
    both = ("seq", "fsdp")
    seq, fsdp = lax.axis_size("seq"), lax.axis_size("fsdp")
    world = seq * fsdp
    low = jnp.bfloat16
    share = self_query.shape[0]
    width = self_query.shape[1]
    hidden_share = ffn_down.shape[0]
    inner = ffn_gate.shape[1]
    rows = tokens.shape[1]
    group = rel_bias.shape[1]
    group_width = group * HEAD
    padded = -(-group_width // LANES) * LANES
    heads = width // HEAD
    place = lax.axis_index("seq")

    aligned = share % 8 == 0
    nz = fsdp // 2
    gain_share = gains.shape[1]
    masters = (self_output, cross_query, cross_key, cross_value, cross_output)
    gate_up = lax.all_gather(jnp.concatenate([ffn_gate.astype(low), ffn_up.astype(low)], axis=1), both, axis=0, tiled=True)
    w_down = lax.all_gather(ffn_down.astype(low), both, axis=0, tiled=True)
    own = jnp.stack([w.astype(low).reshape(share, seq, group_width) for w in (self_query, self_key, self_value)])
    own = jnp.pad(own, ((0, 0), (0, 0), (0, 0), (0, padded - group_width))).transpose(2, 1, 0, 3).reshape(seq, share, 3 * padded)
    squares = jnp.stack([w.astype(low) for w in masters])
    gain_block = gains.astype(low).astype(jnp.float32).reshape(1, -1)
    gain_block = jnp.pad(gain_block, ((0, 7), (0, LANES - gains.size)))
    if aligned:
        everyone, encoded, w_qkv, squares, gain_rows = gather(
            nz, tokens[0], encoder[0], own.reshape(2, 2, share, 3 * padded), squares, gain_block
        )
    else:
        everyone = lax.all_gather(tokens[0], "seq", axis=0)
        encoded = lax.all_gather(encoder[0], "seq", axis=0)
        w_qkv = lax.all_to_all(own, "seq", split_axis=0, concat_axis=0, tiled=True)
        w_qkv = lax.all_gather(w_qkv, "fsdp", axis=1)
        squares = jnp.moveaxis(lax.all_gather(squares, both, axis=0), 1, 0)
        gain_rows = lax.all_gather(gain_block, both, axis=0)
    everyone = everyone.reshape(seq * rows, width)
    encoded = encoded.reshape(-1, width)
    w_qkv = w_qkv.reshape(width, 3 * padded)
    squares = squares.reshape(5, width, width)
    w_output, c_query, c_key, c_value, c_output = (squares[n] for n in range(5))
    gain_rows = gain_rows.reshape(world, 8, LANES)[:, 0, : gains.size]
    gain_rows = gain_rows.reshape(world, 3, gain_share).transpose(1, 0, 2).reshape(3, width)

    length = lengths[0]
    values_in = tokens[0].astype(jnp.float32)
    normed_all = rms_norm(everyone.astype(jnp.float32), gain_rows[0]).astype(low)
    qkv = nn(normed_all, w_qkv).astype(low)
    base_forward, base_backward = bias_rows(rel_bias)
    own_mixed, own_logsum = attend_forward(qkv, qkv, qkv, group, HEAD, padded, base_forward, lengths)
    mixed = lax.all_to_all(own_mixed[:, :group_width], "seq", split_axis=0, concat_axis=1, tiled=True)
    attended = values_in + nn(mixed, w_output)
    normed_two = rms_norm(attended, gain_rows[1]).astype(low)
    cross_queries = nn(normed_two, c_query).astype(low)
    cross_keys = nn(encoded, c_key).astype(low)
    cross_values = nn(encoded, c_value).astype(low)
    cross_mixed, cross_logsum = attend_forward(cross_queries, cross_keys, cross_values, heads, HEAD)
    crossed = attended + nn(cross_mixed, c_output)
    normed_three = rms_norm(crossed, gain_rows[2]).astype(low)
    both_parts = nn(normed_three, gate_up)
    gate, upper = both_parts[:, :inner], both_parts[:, inner:]
    hidden = activate(gate, upper).astype(low)
    result = crossed + nn(hidden, w_down)

    positions = place * rows + jnp.arange(rows, dtype=jnp.int32)
    grad_out = cotangent[0].astype(jnp.float32) * (positions < length).astype(jnp.float32)[:, None]
    grad_ffn = grad_out.astype(low)
    grad_down = inner_rows(hidden, grad_ffn).astype(low)
    share_down = lax.psum_scatter(grad_down, both, scatter_dimension=0, tiled=True)
    grad_hidden = matmul_t(grad_ffn, w_down)
    _, pullback = jax.vjp(activate, gate, upper)
    grad_gate, grad_upper = pullback(grad_hidden)
    grad_both = jnp.concatenate([grad_gate.astype(low), grad_upper.astype(low)], axis=1)
    grad_gate_up = inner_rows(normed_three, grad_both).astype(low)
    share_gate_up = lax.psum_scatter(grad_gate_up, both, scatter_dimension=0, tiled=True)
    grad_normed_three = matmul_t(grad_both, gate_up)
    norm_part, grad_gain_two = rms_back(crossed, gain_rows[2], grad_normed_three)
    grad_crossed = grad_out + norm_part
    grad_branch = grad_crossed.astype(low)
    grad_coutput = inner_rows(cross_mixed, grad_branch).astype(low)
    grad_cmixed = matmul_t(grad_branch, c_output).astype(low)
    grad_cq, grad_ck, grad_cv = attend_backward(
        cross_queries, cross_keys, cross_values, grad_cmixed, cross_mixed, cross_logsum, heads, HEAD
    )
    grad_cquery = inner_rows(normed_two, grad_cq).astype(low)
    grad_ckey = inner_rows(encoded, grad_ck).astype(low)
    grad_cvalue = inner_rows(encoded, grad_cv).astype(low)
    grad_encoded_part = (matmul_t(grad_ck, c_key) + matmul_t(grad_cv, c_value)).astype(low)
    norm_part, grad_gain_one = rms_back(attended, gain_rows[1], matmul_t(grad_cq, c_query))
    grad_attended = grad_crossed + norm_part
    grad_self_branch = grad_attended.astype(low)
    grad_output = inner_rows(mixed, grad_self_branch).astype(low)
    grad_mixed = matmul_t(grad_self_branch, w_output).astype(low)
    own_grad_mixed = lax.all_to_all(grad_mixed, "seq", split_axis=1, concat_axis=0, tiled=True)
    own_grad_mixed = jnp.pad(own_grad_mixed, ((0, 0), (0, padded - group_width)))
    own_dq, own_dk, own_dv, near = attend_backward(
        qkv, qkv, qkv, own_grad_mixed, own_mixed, own_logsum, group, HEAD, padded, base_backward, lengths
    )
    own_qkv = jnp.concatenate([own_dq, own_dk, own_dv], axis=1)
    grad_normed_part = matmul_t(own_qkv, w_qkv)
    values_all = everyone.astype(jnp.float32)
    units_all = values_all * lax.rsqrt(jnp.mean(values_all * values_all, axis=-1, keepdims=True) + epsilon)
    grad_gain_zero = jnp.sum(grad_normed_part * units_all, axis=0)
    grad_normed_part = grad_normed_part.astype(low)
    grad_own = inner_rows(normed_all, own_qkv).astype(low)
    grad_gains = jnp.stack([grad_gain_zero, grad_gain_one, grad_gain_two])
    grad_gains = grad_gains.reshape(3, world, gain_share).transpose(1, 0, 2).reshape(world, 1, 3 * gain_share)
    grad_gains = jnp.pad(grad_gains, ((0, 0), (0, 7), (0, LANES - 3 * gain_share)))
    skew = jnp.pad(near.reshape(group, -1), ((0, 0), (0, LANES))).reshape(group, LANES, 2 * LANES + 1)
    by_distance = jnp.pad(jnp.sum(skew[:, :, :LANES], axis=1), ((0, 8 - group), (0, 0)))
    grad_squares = [grad_output, grad_cquery, grad_ckey, grad_cvalue, grad_coutput]
    if aligned:
        slab = 64
        share_square, grad_own, grad_normed, grad_encoded, share_gains, by_distance = reduce(
            nz,
            [g.reshape(2, 2, nz, 2, share, width) for g in grad_squares],
            grad_own.reshape(2, 2, nz, 2, share, 3 * padded),
            grad_normed_part.reshape(2, 2, -1, slab, width),
            grad_encoded_part.reshape(2, 2, -1, slab, width),
            grad_gains,
            by_distance,
        )
        grad_normed, grad_encoded = grad_normed.reshape(rows, width), grad_encoded.reshape(-1, width)
        grad_own = grad_own.reshape(seq, share, 3 * padded)
    else:
        share_square = lax.psum_scatter(jnp.concatenate(grad_squares, axis=1), both, scatter_dimension=0, tiled=True)
        share_square = share_square.reshape(share, 5, width).transpose(1, 0, 2)
        grad_own = grad_own.reshape(seq, fsdp, share, 3 * padded).transpose(1, 0, 2, 3)
        grad_own = lax.psum_scatter(grad_own, "fsdp", scatter_dimension=0, tiled=True)[0]
        grad_own = lax.all_to_all(grad_own, "seq", split_axis=0, concat_axis=0, tiled=True)
        grad_normed = lax.psum_scatter(grad_normed_part, "seq", scatter_dimension=0, tiled=True).astype(jnp.float32)
        grad_encoded = lax.psum_scatter(grad_encoded_part, "seq", scatter_dimension=0, tiled=True).astype(jnp.float32)
        share_gains = lax.psum_scatter(grad_gains, both, scatter_dimension=0, tiled=True)[0]
        by_distance = lax.psum(by_distance, "fsdp")
    share_gains = share_gains[0, : 3 * gain_share].reshape(3, gain_share)
    grad_own = grad_own.reshape(seq, share, 3, padded)[:, :, :, :group_width].transpose(2, 1, 0, 3).reshape(3, share, width)
    norm_part, _ = rms_back(values_in, gain_rows[0], grad_normed)
    grad_input = grad_attended + norm_part
    bins = rel_bias.shape[0]
    near_map = (buckets(jnp.arange(LANES, dtype=jnp.int32))[:, None] == jnp.arange(bins - 1, dtype=jnp.int32)[None]).astype(jnp.float32)
    near_sums = jnp.dot(near_map.T, by_distance[:group].T, precision=highest)
    table_grad = jnp.concatenate([near_sums, -jnp.sum(near_sums, axis=0, keepdims=True)], axis=0)

    wide = jnp.float32
    outputs = [share_square[n].astype(wide) for n in range(5)]
    own_outputs = [grad_own[n].astype(wide) for n in range(3)]
    return (
        result.astype(low)[None], grad_input[None], grad_encoded[None], share_gains,
        *own_outputs, *outputs,
        share_gate_up[:, :inner].astype(wide), share_gate_up[:, inner:].astype(wide), share_down.astype(wide),
        table_grad,
    )


def solution(mesh):
    split = P(("seq", "fsdp"), None)
    rows = P("fsdp", "seq", None)
    gains = P(None, ("seq", "fsdp"))
    return jax.shard_map(
        per_device,
        mesh=mesh,
        in_specs=(rows, rows, rows, P("fsdp"), gains, *([split] * 11), P(None, "seq")),
        out_specs=(rows, rows, rows, gains, *([split] * 11), P(None, "seq")),
        check_vma=False,
    )
```

```python
import functools

import jax
import jax.numpy as jnp
import numpy as np
from jax import lax
from jax.experimental import pallas as pl
from jax.experimental.pallas import tpu as pltpu
from jax.sharding import PartitionSpec as P

LANES = 128
BLOCK = 512
HEAD = 64
negative = -1e30
epsilon = 1e-06
highest = lax.Precision.HIGHEST
bounds = np.ceil(16.0 * 8.0 ** (np.arange(1, 16) / 16.0)).astype(np.int32)
low = jnp.bfloat16
MESH = pl.DeviceIdType.MESH


def nt(left, right):
    return lax.dot_general(left, right, (((1,), (1,)), ((), ())), preferred_element_type=jnp.float32)


def nn(left, right):
    return jnp.dot(left, right, preferred_element_type=jnp.float32)


def tn(left, right):
    return lax.dot_general(left, right, (((0,), (0,)), ((), ())), preferred_element_type=jnp.float32)


def buckets(distance):
    far = 16 + jnp.sum((distance[..., None] >= jnp.asarray(bounds)).astype(jnp.int32), axis=-1)
    return jnp.where(distance < 16, distance, far)


def bias_rows(table):
    count = table.shape[0]
    place = jnp.arange(3 * LANES, dtype=jnp.int32)
    onehot = buckets(jnp.clip(place, 0, 2 * LANES))[None, :] == jnp.arange(count, dtype=jnp.int32)[:, None]
    relative = table - table[count - 1 :]
    values = jnp.sum(jnp.where(onehot[:, None, :], relative[:, :, None], 0.0), axis=0)
    return jnp.where((place >= 2 * LANES)[None], negative, values)[:, None, :]


def head_place(heads):
    head = pl.program_id(0)
    per_tile = LANES // HEAD
    side = lax.rem(head, per_tile)
    lane = lax.broadcasted_iota(jnp.int32, (1, LANES), 1)
    return head, side == 0, (side == per_tile - 1) | (head == heads - 1), (lane // HEAD) == side


def bias_tiles(base_ref, t_scr):
    wide = jnp.broadcast_to(base_ref[0], (LANES, 3 * LANES))
    t_scr[...] = pltpu.roll(wide, 0, 1, stride=1, stride_axis=0)[:, : 2 * LANES]


def add_near(scores, t_scr):
    near = min(2 * LANES, scores.shape[1])
    fixed = scores[:, :near] + t_scr[:, :near]
    return fixed if near == scores.shape[1] else jnp.concatenate([fixed, scores[:, near:]], axis=1)


def add_corner(scores, t_scr):
    top, bottom = scores[:-LANES], scores[-LANES:]
    bottom = jnp.concatenate([bottom[:, :LANES] + t_scr[:, LANES:], bottom[:, LANES:]], axis=1)
    return jnp.concatenate([top, bottom], axis=0)


def at_step(head, stages, point, points):
    for due, stage in stages:
        if due >= 0 and due % points == point:
            pl.when(head == due // points)(stage)


def at_end(head, heads, stages):
    for due, stage in stages:
        if due < 0:
            pl.when(head == heads - 1)(stage)


FORWARD_POINTS = 4
BACKWARD_POINTS = 10


def attend_forward_kernel(*refs, causal, heads, plan):
    refs = list(refs)
    take = lambda n: [refs.pop(0) for _ in range(n)]
    if causal:
        (length_ref,) = take(1)
    q_ref, k_ref, v_ref = take(3)
    if causal:
        (base_ref,) = take(1)
    given = take(plan.inputs) if plan else []
    o_ref, lse_ref = take(2)
    made = take(plan.outputs) if plan else []
    s_scr, vt_scr, acc_scr, ot_scr = take(4)
    if causal:
        t_scr, mask_scr = take(2)
    stages = plan.stages(given, made, refs) if plan else []
    head, first, last, mask = head_place(heads)
    rows, keys = q_ref.shape[0], k_ref.shape[0]
    block = min(BLOCK, rows)
    if causal:
        bias_tiles(base_ref, t_scr)

        @pl.when(head == 0)
        def _():
            place = lax.broadcasted_iota(jnp.int32, (keys, LANES), 0)
            mask_scr[...] = jnp.where(place < length_ref[0], 0.0, negative)

    for at in range(0, keys, BLOCK):
        vt_scr[:, at : at + BLOCK] = jnp.where(mask, v_ref[at : at + BLOCK, :], 0).T

    def limit(scores, start):
        if start < BLOCK:
            return scores
        part = mask_scr[start : start + scores.shape[0], :]
        return scores + jnp.concatenate([part] * (scores.shape[1] // LANES), axis=1)

    for number in range(rows // block):
        at_step(head, stages, number, FORWARD_POINTS)
        start = number * block
        queries = jnp.where(mask, q_ref[start : start + block, :], 0)
        pieces = [(at, BLOCK, 0) for at in range(0, start if causal else keys, BLOCK)]
        if causal:
            pieces += [(start + part, LANES, part) for part in range(0, block, LANES)]
        largest = jnp.full((1, block), negative, jnp.float32)
        for at, size, skip in pieces:
            scores = nt(k_ref[at : at + size, :], queries[skip:])
            if causal:
                if size == LANES:
                    scores = add_near(scores, t_scr)
                elif at + size == start:
                    scores = add_corner(scores, t_scr)
                scores = limit(scores, at)
            s_scr[at : at + size, skip:] = scores
            top = jnp.maximum(largest[:, skip:], jnp.max(scores, axis=0, keepdims=True))
            largest = top if skip == 0 else jnp.concatenate([largest[:, :skip], top], axis=1)
        totals = jnp.zeros((1, block), jnp.float32)
        acc_scr[...] = jnp.zeros_like(acc_scr)
        for at, size, skip in pieces:
            expos = jnp.exp(s_scr[at : at + size, skip:] - largest[:, skip:])
            more = totals[:, skip:] + jnp.sum(expos, axis=0, keepdims=True)
            totals = more if skip == 0 else jnp.concatenate([totals[:, :skip], more], axis=1)
            acc_scr[:, skip:] += nn(vt_scr[:, at : at + size], expos.astype(low))
        lse_ref[0, :, start : start + block] = jnp.broadcast_to(largest + jnp.log(totals), (8, block))
        mixed = acc_scr[...] / totals
        ot_scr[:, start : start + block] = mixed + jnp.where(first, 0.0, ot_scr[:, start : start + block])

    @pl.when(last)
    def _():
        for at in range(0, rows, block):
            o_ref[at : at + block, :] = ot_scr[:, at : at + block].T.astype(low)

    at_end(head, heads, stages)


def attend_specs(queries, keys, padded):
    rows = queries.shape[0]
    width = padded or queries.shape[1]
    count = keys.shape[0]
    per_tile = LANES // HEAD
    skip = padded // LANES
    row_spec = pl.BlockSpec((rows, LANES), lambda h: (0, h // per_tile))
    key_spec = pl.BlockSpec((count, LANES), lambda h: (0, h // per_tile))
    key_specs = [pl.BlockSpec((count, LANES), lambda h, n=n: (0, n * skip + h // per_tile)) for n in (1, 2)]
    return rows, width, count, row_spec, key_spec, key_specs


def attend_forward(queries, keys, values, heads, padded=0, bias=None, length=None, plan=None, extra=()):
    causal = bias is not None
    rows, width, count, row_spec, _, key_specs = attend_specs(queries, keys, padded)
    block = min(BLOCK, rows)
    in_specs = [row_spec, *key_specs]
    args = [queries, keys, values]
    scratch = [
        pltpu.VMEM((count, block), jnp.float32), pltpu.VMEM((LANES, count), low),
        pltpu.VMEM((LANES, block), jnp.float32), pltpu.VMEM((LANES, rows), jnp.float32),
    ]
    if causal:
        in_specs = [pl.BlockSpec(memory_space=pltpu.SMEM), *in_specs, pl.BlockSpec((1, 1, 3 * LANES), lambda h: (h, 0, 0))]
        args = [length, *args, bias]
        scratch += [pltpu.VMEM((LANES, 2 * LANES), jnp.float32), pltpu.VMEM((count, LANES), jnp.float32)]
    return pl.pallas_call(
        functools.partial(attend_forward_kernel, causal=causal, heads=heads, plan=plan),
        grid=(heads,),
        in_specs=in_specs + (plan.in_specs() if plan else []),
        out_specs=[row_spec, pl.BlockSpec((1, 8, rows), lambda h: (h, 0, 0))] + (plan.out_specs() if plan else []),
        out_shape=[
            jax.ShapeDtypeStruct((rows, width), low),
            jax.ShapeDtypeStruct((heads, 8, rows), jnp.float32),
        ] + (plan.out_shape() if plan else []),
        scratch_shapes=scratch + (plan.scratch() if plan else []),
        compiler_params=plan.params() if plan else pltpu.CompilerParams(vmem_limit_bytes=60 * 2**20),
        cost_estimate=pl.CostEstimate(
            flops=4 * heads * LANES * rows * count // (2 if causal else 1),
            bytes_accessed=4 * (rows + count) * width,
            transcendentals=heads * rows * count // (2 if causal else 1),
        ),
        name="self_forward" if causal else "cross_forward",
    )(*args, *extra)


def attend_backward_kernel(*refs, causal, heads, plan):
    refs = list(refs)
    take = lambda n: [refs.pop(0) for _ in range(n)]
    if causal:
        (length_ref,) = take(1)
    q_ref, k_ref, v_ref, do_ref, o_ref, lse_ref = take(6)
    if causal:
        (base_ref,) = take(1)
    given = take(plan.inputs) if plan else []
    dq_ref, dk_ref, dv_ref = take(3)
    if causal:
        (distance_ref,) = take(1)
    made = take(plan.outputs) if plan else []
    kt_scr, dqt_scr, dk_scr, dv_scr, row_scr = take(5)
    if causal:
        t_scr, near_scr = take(2)
    stages = plan.stages(given, made, refs) if plan else []
    head, first, last, mask = head_place(heads)
    rows, keys = q_ref.shape[0], k_ref.shape[0]
    block = min(BLOCK, rows)
    key_block = min(BLOCK, keys)

    @pl.when(first)
    def _():
        dqt_scr[...] = jnp.zeros_like(dqt_scr)
        dk_scr[...] = jnp.zeros_like(dk_scr)
        dv_scr[...] = jnp.zeros_like(dv_scr)

    if causal:
        bias_tiles(base_ref, t_scr)
        near_scr[...] = jnp.zeros_like(near_scr)
    for at in range(0, keys, key_block):
        kt_scr[:, at : at + key_block] = jnp.where(mask, k_ref[at : at + key_block, :], 0).T
    for start in range(0, rows, block):
        at = slice(start, start + block)
        product = do_ref[at, :].astype(jnp.float32) * o_ref[at, :].astype(jnp.float32)
        delta = jnp.sum(jnp.where(mask, product, 0.0).T, axis=0, keepdims=True)
        logsum = lse_ref[0, 0:1, at]
        if causal:
            place = start + lax.broadcasted_iota(jnp.int32, (1, block), 1)
            logsum = jnp.where(place < length_ref[0], logsum, -negative)
        row_scr[0:1, at] = logsum
        row_scr[1:2, at] = delta

    def piece(key_at, row_at, fix=None):
        queries = jnp.where(mask, q_ref[row_at, :], 0)
        grads = jnp.where(mask, do_ref[row_at, :], 0)
        scores = nt(k_ref[key_at, :], queries)
        if fix is not None:
            scores = fix(scores, t_scr)
        weights = jnp.exp(scores - row_scr[0:1, row_at])
        grad_weights = nt(v_ref[key_at, :], grads)
        grad_scores = weights * (grad_weights - row_scr[1:2, row_at])
        low_scores = grad_scores.astype(low)
        dv_scr[key_at, :] += nn(weights.astype(low), grads)
        dk_scr[key_at, :] += nn(low_scores, queries)
        dqt_scr[:, row_at] += nn(kt_scr[:, key_at], low_scores)
        return grad_scores

    point = 0
    if not causal:
        for start in range(0, keys, key_block):
            for at in range(0, rows, block):
                piece(slice(start, start + key_block), slice(at, at + block))
    else:
        for start in range(0, keys, block):
            at_step(head, stages, point, BACKWARD_POINTS)
            point += 1
            for here in range(start, start + block, LANES):
                grad = piece(slice(here, here + LANES), slice(here, start + block), add_near)
                near = min(2 * LANES, grad.shape[1])
                near_scr[:, :near] += grad[:, :near]
            for at in range(start + block, rows, block):
                at_step(head, stages, point, BACKWARD_POINTS)
                point += 1
                beside = at == start + block
                grad = piece(slice(start, start + block), slice(at, at + block), add_corner if beside else None)
                if beside:
                    near_scr[:, LANES:] += grad[-LANES:, :LANES]
        flip = lax.broadcasted_iota(jnp.int32, (LANES, LANES), 0) + lax.broadcasted_iota(jnp.int32, (LANES, LANES), 1)
        flip = (flip == LANES - 1).astype(jnp.float32)
        turned = lax.dot_general(
            flip, near_scr[...], (((1,), (0,)), ((), ())), precision=highest, preferred_element_type=jnp.float32
        )
        turned = pltpu.roll(turned, 1, 1, stride=1, stride_axis=0)
        sums = jnp.sum(turned[:, LANES:], axis=0, keepdims=True)
        at_row = lax.broadcasted_iota(jnp.int32, (8, LANES), 0) == head
        before = jnp.where(head == 0, 0.0, distance_ref[...])
        distance_ref[...] = jnp.where(at_row, jnp.broadcast_to(sums, (8, LANES)), before)

    @pl.when(last)
    def _():
        for at in range(0, rows, block):
            dq_ref[at : at + block, :] = dqt_scr[:, at : at + block].T.astype(low)
        dk_ref[...] = dk_scr[...].astype(low)
        dv_ref[...] = dv_scr[...].astype(low)

    at_end(head, heads, stages)


def attend_backward(queries, keys, values, grad_mixed, mixed, logsum, heads, padded=0, bias=None, length=None, plan=None, extra=()):
    causal = bias is not None
    rows, width, count, row_spec, key_spec, key_specs = attend_specs(queries, keys, padded)
    in_specs = [row_spec, *key_specs, row_spec, row_spec, pl.BlockSpec((1, 8, rows), lambda h: (h, 0, 0))]
    args = [queries, keys, values, grad_mixed, mixed, logsum]
    out_specs = [row_spec, key_spec, key_spec]
    out_shape = [jax.ShapeDtypeStruct((n, width), low) for n in (rows, count, count)]
    scratch = [
        pltpu.VMEM((LANES, count), low), pltpu.VMEM((LANES, rows), jnp.float32),
        pltpu.VMEM((count, LANES), jnp.float32), pltpu.VMEM((count, LANES), jnp.float32), pltpu.VMEM((8, rows), jnp.float32),
    ]
    if causal:
        in_specs = [pl.BlockSpec(memory_space=pltpu.SMEM), *in_specs, pl.BlockSpec((1, 1, 3 * LANES), lambda h: (h, 0, 0))]
        args = [length, *args, bias]
        out_specs += [pl.BlockSpec((8, LANES), lambda h: (0, 0))]
        out_shape += [jax.ShapeDtypeStruct((8, LANES), jnp.float32)]
        scratch += [pltpu.VMEM((LANES, 2 * LANES), jnp.float32), pltpu.VMEM((LANES, 2 * LANES), jnp.float32)]
    return pl.pallas_call(
        functools.partial(attend_backward_kernel, causal=causal, heads=heads, plan=plan),
        grid=(heads,),
        in_specs=in_specs + (plan.in_specs() if plan else []),
        out_specs=out_specs + (plan.out_specs() if plan else []),
        out_shape=out_shape + (plan.out_shape() if plan else []),
        scratch_shapes=scratch + (plan.scratch() if plan else []),
        compiler_params=plan.params() if plan else pltpu.CompilerParams(vmem_limit_bytes=60 * 2**20),
        cost_estimate=pl.CostEstimate(
            flops=10 * heads * LANES * rows * count // (2 if causal else 1),
            bytes_accessed=8 * (rows + count) * width,
            transcendentals=heads * rows * count // (2 if causal else 1),
        ),
        name="self_backward" if causal else "cross_backward",
    )(*args, *extra)


def coordinates():
    place, slot = lax.axis_index("seq"), lax.axis_index("fsdp")
    return place // 2, lax.rem(place, 2), slot // 2, lax.rem(slot, 2)


def device(x, c, z, y):
    return (x * 2 + c, z * 2 + y)


class Near:
    def __init__(self, nz):
        self.nz = nz
        x, c, z, y = self.x, self.c, self.z, self.y = coordinates()
        self.by_x, self.by_core, self.by_y = device(1 - x, c, z, y), device(x, 1 - c, z, y), device(x, c, z, 1 - y)
        self.diagonal = device(1 - x, 1 - c, z, y)
        self.steps = [lax.rem(z + t, nz) for t in range(nz)]
        self.backs = [lax.rem(z - t + nz, nz) for t in range(nz)]
        self.by_z = [device(x, c, self.steps[t], y) for t in range(nz)]


def greet(others):
    barrier = pltpu.get_barrier_semaphore()
    for other in others:
        pl.semaphore_signal(barrier, inc=1, device_id=other, device_id_type=MESH)
    pl.semaphore_wait(barrier, len(others))


class Copies:
    def __init__(self, send_sem, recv_sem):
        self.send_sem, self.recv_sem, self.made = send_sem, recv_sem, []

    def add(self, source, target, other):
        self.made.append((source, target, other))
        return len(self.made) - 1

    def copy(self, number):
        source, target, other = self.made[number]
        return pltpu.make_async_remote_copy(
            src_ref=source(), dst_ref=target(), send_sem=self.send_sem.at[number], recv_sem=self.recv_sem.at[number],
            device_id=other, device_id_type=MESH,
        )

    def start(self, *numbers):
        for number in numbers:
            self.copy(number).start()

    def arrive(self, *numbers):
        for number in numbers:
            self.copy(number).wait_recv()

    def finish(self):
        for number in range(len(self.made)):
            self.copy(number).wait_send()


def add_low(target, left, right):
    @pl.loop(0, left.shape[0])
    def _(n):
        target[n] = (left[n].astype(jnp.float32) + right[n].astype(jnp.float32)).astype(target.dtype)


def whole(space=pltpu.VMEM):
    return pl.BlockSpec(memory_space=space)


class GatherPlan:
    inputs, outputs = 1, 1

    def __init__(self, nz, count, share, width):
        self.nz, self.count, self.share, self.width = nz, count, share, width
        self.total = 8 * nz - 1

    def in_specs(self):
        return [whole()]

    def out_specs(self):
        return [whole(pl.ANY)]

    def out_shape(self):
        return [jax.ShapeDtypeStruct((self.count, 2, 2, self.nz, 2, self.share, self.width), low)]

    def scratch(self):
        return [pltpu.SemaphoreType.DMA((self.total,)), pltpu.SemaphoreType.DMA((self.total,)), pltpu.SemaphoreType.DMA((1,))]

    def params(self):
        return pltpu.CompilerParams(collective_id=2, has_side_effects=True, vmem_limit_bytes=60 * 2**20)

    def stages(self, given, made, scratch):
        (src,), (out,), (send_sem, recv_sem, local_sem) = given, made, scratch
        nz, my = self.nz, Near(self.nz)
        x, c, z, y, backs = my.x, my.c, my.z, my.y, my.backs
        copies = Copies(send_sem, recv_sem)
        own = lambda: src
        at = lambda xx, cc, zz, yy: lambda: out.at[:, xx, cc, zz, yy]
        mine = at(x, c, z, y)
        by_z = [None] + [copies.add(own, mine, my.by_z[t]) for t in range(1, nz)]
        held = [mine if t == 0 else at(x, c, backs[t], y) for t in range(nz)]
        source = [own if t == 0 else held[t] for t in range(nz)]
        by_y = [copies.add(source[t], held[t], my.by_y) for t in range(nz)]
        by_x = [copies.add(source[t], held[t], my.by_x) for t in range(nz)]
        by_core = [copies.add(source[t], held[t], my.by_core) for t in range(nz)]
        from_x = [at(1 - x, c, backs[t], y) for t in range(nz)]
        from_y = [at(x, c, backs[t], 1 - y) for t in range(nz)]
        far = [at(1 - x, c, backs[t], 1 - y) for t in range(nz)]
        corner = [
            copies.add(from_x[t], from_x[t], my.by_y) if t % 2 == 0 else copies.add(from_y[t], from_y[t], my.by_x)
            for t in range(nz)
        ]
        core_x = [copies.add(from_x[t], from_x[t], my.by_core) for t in range(nz)]
        core_y = [copies.add(from_y[t], from_y[t], my.by_core) for t in range(nz)]
        core_far = [copies.add(far[t], far[t], my.by_core) for t in range(nz)]
        local = lambda: pltpu.make_async_copy(src, mine(), local_sem.at[0])

        def begin():
            greet([my.by_x, my.by_core, my.by_y, *my.by_z[1:]])
            copies.start(*by_z[1:], by_y[0], by_x[0], by_core[0])
            local().start()

        def line(t):
            copies.arrive(by_z[t])
            copies.start(by_y[t], by_x[t], by_core[t])

        def plane(t):
            copies.arrive(by_x[t])
            copies.start(*([corner[t]] if t % 2 == 0 else []), core_x[t])
            copies.arrive(by_y[t])
            copies.start(*([corner[t]] if t % 2 == 1 else []), core_y[t])

        def turn(t):
            copies.arrive(corner[t])
            copies.start(core_far[t])

        def end():
            local().wait()
            copies.arrive(*by_core, *core_x, *core_y, *core_far)
            copies.finish()

        work = [functools.partial(line, t) for t in range(1, nz)]
        work += [functools.partial(plane, t) for t in range(nz)] + [functools.partial(turn, t) for t in range(nz)]
        points = 3 * FORWARD_POINTS - 1
        stages = [(0, begin)]
        for number, stage in enumerate(work):
            stages.append((1 + number * points // (len(work) + 1), stage))
        return stages + [(-1, end)]


class ReducePlan:
    outputs = 2

    def __init__(self, nz, count, share, width, slabs):
        self.nz, self.count, self.share, self.width, self.slabs = nz, count, share, width, slabs
        self.inputs = count + 1
        self.total = count * (nz + 2) + 2

    def in_specs(self):
        return [whole()] * self.inputs

    def out_specs(self):
        return [whole(), whole()]

    def out_shape(self):
        return [
            jax.ShapeDtypeStruct((self.count, self.share, self.width), jnp.float32),
            jax.ShapeDtypeStruct(self.slabs, jnp.float32),
        ]

    def scratch(self):
        nz, tail = self.nz, (self.share, self.width)
        vmem = lambda *shape: pltpu.VMEM((self.count, *shape, *tail), low)
        slabs = [pltpu.VMEM((*lead, *self.slabs), low) for lead in ((2,), (2,), ())]
        sems = [pltpu.SemaphoreType.DMA((self.total,)), pltpu.SemaphoreType.DMA((self.total,))]
        return [vmem(2, 2, nz), vmem(2, nz, 2), vmem(2, nz), vmem(2, nz), vmem(nz), vmem(nz), vmem(nz - 1), *slabs, *sems]

    def params(self):
        return pltpu.CompilerParams(collective_id=3, has_side_effects=True, vmem_limit_bytes=60 * 2**20)

    def stages(self, given, made, scratch):
        squares, enc = given[:-1], given[-1]
        out, out_enc = made
        a, ra, b, rb, d, rd, re, enc_r, enc_a, enc_rx, send_sem, recv_sem = scratch
        nz, my, count = self.nz, Near(self.nz), self.count
        x, c, z, y = my.x, my.c, my.z, my.y
        copies = Copies(send_sem, recv_sem)
        enc_core = copies.add(lambda: enc.at[:, 1 - c], lambda: enc_r, my.by_core)
        core = [copies.add(lambda n=n: squares[n].at[:, 1 - c], lambda n=n: ra.at[n], my.by_core) for n in range(count)]
        enc_x = copies.add(lambda: enc_a.at[1 - x], lambda: enc_rx, my.by_x)
        one, two, three = [], [], []
        for n in range(count):
            y_first = n % 2 == 0
            if y_first:
                one.append(copies.add(lambda n=n: a.at[n, :, 1 - y], lambda n=n: rb.at[n], my.by_y))
                two.append(copies.add(lambda n=n: b.at[n, 1 - x], lambda n=n: rd.at[n], my.by_x))
            else:
                one.append(copies.add(lambda n=n: a.at[n, 1 - x], lambda n=n: rb.at[n], my.by_x))
                two.append(copies.add(lambda n=n: b.at[n, 1 - y], lambda n=n: rd.at[n], my.by_y))
            three.append([
                copies.add(lambda n=n, t=t: d.at[n, my.steps[t]], lambda n=n, t=t: re.at[n, t - 1], my.by_z[t])
                for t in range(1, nz)
            ])

        def begin():
            greet([my.by_x, my.by_core, my.by_y, *my.by_z[1:]])
            copies.start(*core, enc_core)

        def after_core(n):
            copies.arrive(core[n])
            for half in range(2):
                for side in range(2):
                    add_low(a.at[n, half, side], squares[n].at[half, c, :, side], ra.at[n, half, :, side])
            copies.start(one[n])

        def after_one(n):
            copies.arrive(one[n])
            for side in range(2):
                if n % 2 == 0:
                    add_low(b.at[n, side], a.at[n, side, y], rb.at[n, side])
                else:
                    add_low(b.at[n, side], a.at[n, x, side], rb.at[n, side])
            copies.start(two[n])

        def after_two(n):
            copies.arrive(two[n])
            add_low(d.at[n], b.at[n, x if n % 2 == 0 else y], rd.at[n])
            copies.start(*three[n])

        def after_three(n):
            copies.arrive(*three[n])
            total = d[n, z].astype(jnp.float32)
            for t in range(nz - 1):
                total += re[n, t].astype(jnp.float32)
            out[n] = total

        def encoder():
            copies.arrive(enc_core)
            for half in range(2):
                add_low(enc_a.at[half], enc.at[half, c], enc_r.at[half])
            copies.start(enc_x)

        def end():
            copies.arrive(enc_x)
            add_low(out_enc, enc_a.at[x], enc_rx)
            for n in range(count):
                after_three(n)
            copies.finish()

        part = functools.partial
        work = [part(after_core, n) for n in range(count)] + [encoder]
        work += [part(after_one, n) for n in range(count)] + [part(after_two, n) for n in range(count)]
        points = 3 * BACKWARD_POINTS - 2
        stages = [(0, begin)]
        for number, stage in enumerate(work):
            stages.append((2 + number * (points - 2) // len(work), stage))
        return stages + [(-1, end)]


def gather_kernel(nz, tok, enc, own, everyone, encoded, qkv_out, send_sem, recv_sem, local_sem):
    my = Near(nz)
    x, c, z, y, backs = my.x, my.c, my.z, my.y, my.backs
    greet([my.by_x, my.by_core, my.diagonal, my.by_y, *my.by_z[1:]])
    copies = Copies(send_sem, recv_sem)
    local = [
        pltpu.make_async_copy(source, target, local_sem.at[n])
        for n, (source, target) in enumerate(
            [(own.at[x, c], qkv_out.at[x, c, z, y]), (tok, everyone.at[x, c]), (enc, encoded.at[x, c])]
        )
    ]
    for copy in local:
        copy.start()
    mine = lambda: qkv_out.at[x, c, z, y]
    first = [
        copies.add(lambda: own.at[1 - x, c], mine, my.by_x),
        copies.add(lambda: own.at[x, 1 - c], mine, my.by_core),
        copies.add(lambda: own.at[1 - x, 1 - c], mine, my.diagonal),
    ]
    rows = [(tok, everyone), (enc, encoded)]
    rows_x = [copies.add(lambda s=s: s, lambda t=t: t.at[x, c], my.by_x) for s, t in rows]
    rows_core = [copies.add(lambda s=s: s, lambda t=t: t.at[x, c], my.by_core) for s, t in rows]
    rows_far = [copies.add(lambda t=t: t.at[1 - x, c], lambda t=t: t.at[1 - x, c], my.by_core) for s, t in rows]
    line = [lambda t=t: qkv_out.at[:, :, backs[t], y] for t in range(nz)]
    by_z = [None] + [copies.add(line[0], line[0], my.by_z[t]) for t in range(1, nz)]
    by_y = [copies.add(line[t], line[t], my.by_y) for t in range(nz)]
    copies.start(*first, *rows_x, *rows_core)
    for copy in local:
        copy.wait()
    copies.arrive(*first)
    copies.start(*by_z[1:], by_y[0])
    for t in range(1, nz):
        copies.arrive(by_z[t])
        copies.start(by_y[t])
    for n in range(2):
        copies.arrive(rows_x[n])
        copies.start(rows_far[n])
    copies.arrive(*by_y, *rows_core, *rows_far)
    copies.finish()


def gather(nz, tok, enc, own):
    share, wide = own.shape[-2:]
    shapes = [
        jax.ShapeDtypeStruct((2, 2, *tok.shape), tok.dtype),
        jax.ShapeDtypeStruct((2, 2, *enc.shape), enc.dtype),
        jax.ShapeDtypeStruct((2, 2, nz, 2, share, wide), own.dtype),
    ]
    total = 9 + 2 * nz - 1
    return pl.pallas_call(
        functools.partial(gather_kernel, nz),
        in_specs=[whole()] * 3,
        out_specs=[whole(pl.ANY)] * 3,
        out_shape=shapes,
        scratch_shapes=[
            pltpu.SemaphoreType.DMA((total,)), pltpu.SemaphoreType.DMA((total,)), pltpu.SemaphoreType.DMA((3,)),
        ],
        compiler_params=pltpu.CompilerParams(collective_id=0, has_side_effects=True, vmem_limit_bytes=8 * 2**20),
        name="gather",
    )(tok, enc, own)


def reduce_kernel(nz, group_width, square, own, tok, gain, near, out_square, out_q, out_k, out_v, out_tok, out_gain, out_near, *refs):
    (a, ra, b, rb, d, rd, re, own_r, own_a, own_rz, own_f, own_in, tok_r, tok_a, tok_rx, gain_r, near_r,
     send_sem, recv_sem, gain_send, gain_recv) = refs
    my = Near(nz)
    x, c, z, y = my.x, my.c, my.z, my.y
    world, slots = 8 * nz, 2 * nz
    place, slot = lax.axis_index("seq"), lax.axis_index("fsdp")
    me = place * slots + slot
    barrier = pltpu.get_barrier_semaphore()

    @pl.loop(1, world)
    def _(t):
        other = lax.rem(me + t, world)
        pl.semaphore_signal(barrier, inc=1, device_id=(other // slots, lax.rem(other, slots)), device_id_type=MESH)

    pl.semaphore_wait(barrier, world - 1)
    copies = Copies(send_sem, recv_sem)
    add = copies.add
    tok_core = [add(lambda h=h: tok.at[h, 1 - c], lambda h=h: tok_r.at[h], my.by_core) for h in (1 - x, x)]
    own_y = add(lambda: own.at[:, :, :, 1 - y], lambda: own_r, my.by_y)
    core = add(lambda: square.at[:, 1 - c], lambda: ra, my.by_core)
    near_all = [add(lambda: near, lambda t=t: near_r.at[t - 1], (place, lax.rem(slot + t, slots))) for t in range(1, slots)]
    tok_x = add(lambda: tok_a.at[1 - x], lambda: tok_rx, my.by_x)
    one = add(lambda: a.at[:, 1 - y], lambda: rb, my.by_y)
    two = add(lambda: b.at[1 - x], lambda: rd, my.by_x)
    three = [add(lambda t=t: d.at[my.steps[t]], lambda t=t: re.at[t - 1], my.by_z[t]) for t in range(1, nz)]
    own_z = [
        add(lambda t=t: own_a.at[:, :, my.steps[t]], lambda t=t: own_rz.at[t - 1], my.by_z[t]) for t in range(1, nz)
    ]
    landing = lambda: own_in.at[x, c]
    own_seq = [
        add(lambda: own_f.at[1 - x, c], landing, my.by_x),
        add(lambda: own_f.at[x, 1 - c], landing, my.by_core),
        add(lambda: own_f.at[1 - x, 1 - c], landing, my.diagonal),
    ]

    def gain_copy(t):
        other = lax.rem(me + t, world)
        return pltpu.make_async_remote_copy(
            src_ref=gain.at[other], dst_ref=gain_r.at[t - 1], send_sem=gain_send.at[t - 1], recv_sem=gain_recv.at[t - 1],
            device_id=(other // slots, lax.rem(other, slots)), device_id_type=MESH,
        )

    copies.start(own_y, tok_core[0], core, tok_core[1], *near_all)

    @pl.loop(1, world)
    def _(t):
        gain_copy(t).start()

    copies.arrive(tok_core[0])
    add_low(tok_a.at[1 - x], tok.at[1 - x, c], tok_r.at[1 - x])
    copies.start(tok_x)
    copies.arrive(core)
    for half in range(2):
        for side in range(2):
            add_low(a.at[half, side], square.at[half, c, :, side], ra.at[half, :, side])
    copies.start(one)
    copies.arrive(tok_core[1])
    add_low(tok_a.at[x], tok.at[x, c], tok_r.at[x])
    copies.arrive(own_y)
    for half in range(2):
        for side in range(2):
            add_low(own_a.at[half, side], own.at[half, side, :, y], own_r.at[half, side])
    copies.start(*own_z)
    copies.arrive(one)
    for side in range(2):
        add_low(b.at[side], a.at[side, y], rb.at[side])
    copies.start(two)
    copies.arrive(*own_z)
    for half in range(2):
        for side in range(2):
            total = own_a[half, side, z].astype(jnp.float32)
            for t in range(nz - 1):
                total += own_rz[t, half, side].astype(jnp.float32)
            own_f[half, side] = total.astype(low)
    copies.start(*own_seq)
    own_in[x, c] = own_f[x, c]
    copies.arrive(*near_all)
    total = near[...]
    for t in range(slots - 1):
        total += near_r[t]
    out_near[...] = total
    out_gain[...] = gain[me]

    @pl.loop(1, world)
    def _(t):
        gain_copy(t).wait_recv()
        out_gain[...] += gain_r[t - 1]

    copies.arrive(*own_seq)
    padded = own_in.shape[-1] // 3
    for n, out in enumerate((out_q, out_k, out_v)):
        parts = [own_in[s // 2, s % 2, :, n * padded : n * padded + group_width].astype(jnp.float32) for s in range(4)]
        out[...] = jnp.concatenate(parts, axis=1)
    copies.arrive(two)
    add_low(d, b.at[x], rd)
    copies.start(*three)
    copies.arrive(tok_x)
    add_low(out_tok, tok_a.at[x], tok_rx)
    copies.arrive(*three)
    total = d[z].astype(jnp.float32)
    for t in range(nz - 1):
        total += re[t].astype(jnp.float32)
    out_square[...] = total
    copies.finish()

    @pl.loop(1, world)
    def _(t):
        gain_copy(t).wait_send()


def reduce(nz, group_width, square, own, tok, gain, near):
    share, width = square.shape[-2:]
    wide = own.shape[-1]
    vmem = lambda *shape: pltpu.VMEM(shape, low)
    slabs = tok.shape[2:]
    world = 8 * nz
    total = 4 + 2 * nz - 1 + 3 + 2 * (nz - 1) + 3
    f32 = lambda *shape: jax.ShapeDtypeStruct(shape, jnp.float32)
    return pl.pallas_call(
        functools.partial(reduce_kernel, nz, group_width),
        in_specs=[whole()] * 5,
        out_specs=[whole()] * 7,
        out_shape=[f32(share, width)] * 4 + [f32(*slabs), f32(*gain.shape[1:]), f32(*near.shape)],
        scratch_shapes=[
            vmem(2, 2, nz, share, width), vmem(2, nz, 2, share, width), vmem(2, nz, share, width), vmem(2, nz, share, width),
            vmem(nz, share, width), vmem(nz, share, width), vmem(nz - 1, share, width),
            vmem(2, 2, nz, share, wide), vmem(2, 2, nz, share, wide), vmem(nz - 1, 2, 2, share, wide), vmem(2, 2, share, wide),
            vmem(2, 2, share, wide),
            vmem(2, *slabs), vmem(2, *slabs), vmem(*slabs),
            pltpu.VMEM((world - 1, *gain.shape[1:]), jnp.float32), pltpu.VMEM((2 * nz - 1, *near.shape), jnp.float32),
            pltpu.SemaphoreType.DMA((total,)), pltpu.SemaphoreType.DMA((total,)),
            pltpu.SemaphoreType.DMA((world - 1,)), pltpu.SemaphoreType.DMA((world - 1,)),
        ],
        compiler_params=pltpu.CompilerParams(collective_id=1, has_side_effects=True, vmem_limit_bytes=60 * 2**20),
        name="reduce",
    )(square, own, tok, gain, near)


def rms_norm(values, gain):
    scale = lax.rsqrt(jnp.mean(values * values, axis=-1, keepdims=True) + epsilon)
    return values * scale * gain


def rms_back(values, gain, grad_normed):
    scale = lax.rsqrt(jnp.mean(values * values, axis=-1, keepdims=True) + epsilon)
    unit = values * scale
    grad_unit = grad_normed * gain
    grad_gain = jnp.sum(grad_normed * unit, axis=0)
    grad_values = scale * (grad_unit - unit * jnp.mean(grad_unit * unit, axis=-1, keepdims=True))
    return (grad_values, grad_gain)


def activate(gate, upper):
    return jax.nn.gelu(gate, approximate=True) * upper


def per_device(
    tokens, encoder, cotangent, lengths, gains, self_query, self_key, self_value, self_output,
    cross_query, cross_key, cross_value, cross_output, ffn_gate, ffn_up, ffn_down, rel_bias,
):
    both = ("seq", "fsdp")
    seq, fsdp = lax.axis_size("seq"), lax.axis_size("fsdp")
    world = seq * fsdp
    nz = fsdp // 2
    share, width = self_query.shape
    hidden_share = ffn_down.shape[0]
    inner = ffn_gate.shape[1]
    rows = tokens.shape[1]
    group = rel_bias.shape[1]
    group_width = group * HEAD
    padded = -(-group_width // LANES) * LANES
    spare = padded - group_width
    heads = width // HEAD
    place = lax.axis_index("seq")
    aligned = share % 8 == 0

    gate_up = lax.all_gather(jnp.concatenate([ffn_gate.astype(low), ffn_up.astype(low)], axis=1), both, axis=0, tiled=True)
    w_down = lax.all_gather(ffn_down.astype(low), both, axis=0, tiled=True)
    squares = jnp.stack([w.astype(low) for w in (self_output, cross_query, cross_key, cross_value, cross_output)])
    gain_columns = jnp.pad(gains.astype(low).T, ((0, 0), (0, spare - 3)))
    pieces = []
    for s in range(seq):
        for n, w in enumerate((self_query, self_key, self_value)):
            pieces.append(w[:, s * group_width : (s + 1) * group_width].astype(low))
            pieces.append(gain_columns if n == 0 else jnp.zeros((share, spare), low))
    own = jnp.concatenate(pieces, axis=1).reshape(share, seq, 3 * padded).transpose(1, 0, 2)
    if aligned:
        everyone, encoded, w_qkv = gather(nz, tokens[0], encoder[0], own.reshape(2, 2, share, 3 * padded))
    else:
        everyone = lax.all_gather(tokens[0], "seq", axis=0)
        encoded = lax.all_gather(encoder[0], "seq", axis=0)
        w_qkv = lax.all_to_all(own, "seq", split_axis=0, concat_axis=0, tiled=True)
        w_qkv = lax.all_gather(w_qkv, "fsdp", axis=1)
    everyone = everyone.reshape(seq * rows, width)
    encoded = encoded.reshape(-1, width)
    w_qkv = w_qkv.reshape(width, 3 * padded)
    gain_rows = w_qkv[:, group_width : group_width + 3].astype(jnp.float32).T

    length = lengths[0]
    values_in = tokens[0].astype(jnp.float32)
    normed_all = rms_norm(everyone.astype(jnp.float32), gain_rows[0]).astype(low)
    qkv = nn(normed_all, w_qkv).astype(low)
    bias = bias_rows(rel_bias)
    plan = GatherPlan(nz, 5, share, width) if aligned else None
    own_mixed, own_logsum, *gathered = attend_forward(
        qkv, qkv, qkv, group, padded, bias, lengths, plan, (squares,) if aligned else ()
    )
    squares = gathered[0] if aligned else jnp.moveaxis(lax.all_gather(squares, both, axis=0), 1, 0)
    squares = squares.reshape(5, width, width)
    w_output, c_query, c_key, c_value, c_output = (squares[n] for n in range(5))
    mixed = lax.all_to_all(own_mixed[:, :group_width], "seq", split_axis=0, concat_axis=1, tiled=True)
    attended = values_in + nn(mixed, w_output)
    normed_two = rms_norm(attended, gain_rows[1]).astype(low)
    cross_queries = nn(normed_two, c_query).astype(low)
    cross_keys = nn(encoded, c_key).astype(low)
    cross_values = nn(encoded, c_value).astype(low)
    cross_mixed, cross_logsum = attend_forward(cross_queries, cross_keys, cross_values, heads)
    crossed = attended + nn(cross_mixed, c_output)
    normed_three = rms_norm(crossed, gain_rows[2]).astype(low)
    both_parts = nn(normed_three, gate_up)
    gate, upper = both_parts[:, :inner], both_parts[:, inner:]
    hidden = activate(gate, upper).astype(low)
    result = crossed + nn(hidden, w_down)

    positions = place * rows + jnp.arange(rows, dtype=jnp.int32)
    grad_out = cotangent[0].astype(jnp.float32) * (positions < length).astype(jnp.float32)[:, None]
    grad_ffn = grad_out.astype(low)
    grad_hidden = nt(grad_ffn, w_down)
    _, pullback = jax.vjp(activate, gate, upper)
    grad_gate, grad_upper = pullback(grad_hidden)
    grad_both = jnp.concatenate([grad_gate.astype(low), grad_upper.astype(low)], axis=1)
    slabs = -(-hidden_share // share)
    grad_down = tn(hidden, grad_ffn).astype(low).reshape(world, hidden_share, width)
    grad_down = jnp.pad(grad_down, ((0, 0), (0, slabs * share - hidden_share), (0, 0)))
    grad_down = grad_down.reshape(world, slabs, share, width).transpose(0, 2, 1, 3).reshape(world * share, slabs * width)
    packed = jnp.concatenate([tn(normed_three, grad_both).astype(low), grad_down], axis=1)
    share_ffn = lax.psum_scatter(packed, both, scatter_dimension=0, tiled=True)

    grad_normed_three = nt(grad_both, gate_up)
    norm_part, grad_gain_two = rms_back(crossed, gain_rows[2], grad_normed_three)
    grad_crossed = grad_out + norm_part
    grad_branch = grad_crossed.astype(low)
    grad_coutput = tn(cross_mixed, grad_branch).astype(low)
    grad_cmixed = nt(grad_branch, c_output).astype(low)
    grad_cq, grad_ck, grad_cv = attend_backward(
        cross_queries, cross_keys, cross_values, grad_cmixed, cross_mixed, cross_logsum, heads
    )
    grad_cquery = tn(normed_two, grad_cq).astype(low)
    grad_ckey = tn(encoded, grad_ck).astype(low)
    grad_cvalue = tn(encoded, grad_cv).astype(low)
    grad_encoded = (nt(grad_ck, c_key) + nt(grad_cv, c_value)).astype(low)
    norm_part, grad_gain_one = rms_back(attended, gain_rows[1], nt(grad_cq, c_query))
    grad_attended = grad_crossed + norm_part
    grad_self_branch = grad_attended.astype(low)
    grad_output = tn(mixed, grad_self_branch).astype(low)
    grad_mixed = nt(grad_self_branch, w_output).astype(low)
    own_grad_mixed = lax.all_to_all(grad_mixed, "seq", split_axis=1, concat_axis=0, tiled=True)
    own_grad_mixed = jnp.pad(own_grad_mixed, ((0, 0), (0, padded - group_width)))
    slab = 64
    chunked = lambda g: g.reshape(2, 2, nz, 2, share, g.shape[-1])
    by_place = lambda g: g.reshape(2, 2, -1, slab, width)
    early = [grad_cquery, grad_ckey, grad_cvalue, grad_coutput]
    plan, extra = None, ()
    if aligned:
        extra = (*[chunked(g) for g in early], by_place(grad_encoded))
        plan = ReducePlan(nz, len(early), share, width, extra[-1].shape[2:])
    own_dq, own_dk, own_dv, by_distance, *sums = attend_backward(
        qkv, qkv, qkv, own_grad_mixed, own_mixed, own_logsum, group, padded, bias, lengths, plan, extra
    )
    own_qkv = jnp.concatenate([own_dq, own_dk, own_dv], axis=1)
    grad_normed_part = nt(own_qkv, w_qkv)
    values_all = everyone.astype(jnp.float32)
    units_all = values_all * lax.rsqrt(jnp.mean(values_all * values_all, axis=-1, keepdims=True) + epsilon)
    grad_gain_zero = jnp.sum(grad_normed_part * units_all, axis=0)
    grad_normed_part = grad_normed_part.astype(low)
    grad_own = tn(normed_all, own_qkv).astype(low)
    grad_gains = jnp.stack([grad_gain_zero, grad_gain_one, grad_gain_two])
    grad_gains = grad_gains.reshape(3, world, share).transpose(1, 0, 2).reshape(world, 1, 3 * share)
    grad_gains = jnp.pad(grad_gains, ((0, 0), (0, 7), (0, LANES - 3 * share)))
    wide = jnp.float32
    if aligned:
        share_output, *share_own, grad_normed, share_gains, by_distance = reduce(
            nz, group_width, chunked(grad_output), chunked(grad_own), by_place(grad_normed_part), grad_gains, by_distance
        )
        share_early, grad_encoded = sums
        share_squares = [share_output, *(share_early[n] for n in range(4))]
        grad_normed, grad_encoded = grad_normed.reshape(rows, width), grad_encoded.reshape(-1, width)
    else:
        scatter = lambda g, axes: lax.psum_scatter(g, axes, scatter_dimension=0, tiled=True)
        share_squares = scatter(jnp.concatenate([grad_output, *early], axis=1), both).astype(wide)
        share_squares = [share_squares[:, n * width : (n + 1) * width] for n in range(5)]
        grad_own = scatter(grad_own.reshape(seq, fsdp, share, 3 * padded).transpose(1, 0, 2, 3), "fsdp")[0]
        grad_own = lax.all_to_all(grad_own, "seq", split_axis=0, concat_axis=0, tiled=True).astype(wide)
        grad_own = grad_own.reshape(seq, share, 3, padded)[:, :, :, :group_width].transpose(2, 1, 0, 3).reshape(3, share, width)
        share_own = [grad_own[n] for n in range(3)]
        grad_normed = scatter(grad_normed_part, "seq").astype(wide)
        grad_encoded = scatter(grad_encoded, "seq").astype(wide)
        share_gains = scatter(grad_gains, both)[0]
        by_distance = lax.psum(by_distance, "fsdp")
    share_gains = share_gains[0, : 3 * share].reshape(3, share)
    norm_part, _ = rms_back(values_in, gain_rows[0], grad_normed)
    grad_input = grad_attended + norm_part
    bins = rel_bias.shape[0]
    near_map = (buckets(jnp.arange(LANES, dtype=jnp.int32))[:, None] == jnp.arange(bins - 1, dtype=jnp.int32)[None]).astype(wide)
    near_sums = jnp.dot(near_map.T, by_distance[:group].T, precision=highest)
    table_grad = jnp.concatenate([near_sums, -jnp.sum(near_sums, axis=0, keepdims=True)], axis=0)
    share_ffn = share_ffn.astype(wide)
    share_down = share_ffn[:, 2 * inner :].reshape(share, slabs, width).transpose(1, 0, 2).reshape(slabs * share, width)
    return (
        result.astype(low)[None], grad_input[None], grad_encoded[None], share_gains, *share_own, *share_squares,
        share_ffn[:, :inner], share_ffn[:, inner : 2 * inner], share_down[:hidden_share], table_grad,
    )


def solution(mesh):
    split = P(("seq", "fsdp"), None)
    rows = P("fsdp", "seq", None)
    gains = P(None, ("seq", "fsdp"))
    return jax.shard_map(
        per_device,
        mesh=mesh,
        in_specs=(rows, rows, rows, P("fsdp"), gains, *([split] * 11), P(None, "seq")),
        out_specs=(rows, rows, rows, gains, *([split] * 11), P(None, "seq")),
        check_vma=False,
    )
```

```python
import functools

import jax
import jax.numpy as jnp
import numpy as np
from jax import lax
from jax.experimental import pallas as pl
from jax.experimental.pallas import tpu as pltpu
from jax.sharding import PartitionSpec as P

LANES = 128
BLOCK = 512
HEAD = 64
negative = -1e30
epsilon = 1e-06
highest = lax.Precision.HIGHEST
bounds = np.ceil(16.0 * 8.0 ** (np.arange(1, 16) / 16.0)).astype(np.int32)
low = jnp.bfloat16
MESH = pl.DeviceIdType.MESH


def nt(left, right):
    return lax.dot_general(left, right, (((1,), (1,)), ((), ())), preferred_element_type=jnp.float32)


def nn(left, right):
    return jnp.dot(left, right, preferred_element_type=jnp.float32)


def tn(left, right):
    return lax.dot_general(left, right, (((0,), (0,)), ((), ())), preferred_element_type=jnp.float32)


def buckets(distance):
    far = 16 + jnp.sum((distance[..., None] >= jnp.asarray(bounds)).astype(jnp.int32), axis=-1)
    return jnp.where(distance < 16, distance, far)


def bias_rows(table):
    count = table.shape[0]
    place = jnp.arange(3 * LANES, dtype=jnp.int32)
    onehot = buckets(jnp.clip(place, 0, 2 * LANES))[None, :] == jnp.arange(count, dtype=jnp.int32)[:, None]
    relative = table - table[count - 1 :]
    values = jnp.sum(jnp.where(onehot[:, None, :], relative[:, :, None], 0.0), axis=0)
    return jnp.where((place >= 2 * LANES)[None], negative, values)[:, None, :]


def head_place(heads):
    head = pl.program_id(0)
    per_tile = LANES // HEAD
    side = lax.rem(head, per_tile)
    lane = lax.broadcasted_iota(jnp.int32, (1, LANES), 1)
    return head, side == 0, (side == per_tile - 1) | (head == heads - 1), (lane // HEAD) == side


def bias_tiles(base_ref, t_scr):
    wide = jnp.broadcast_to(base_ref[0], (LANES, 3 * LANES))
    t_scr[...] = pltpu.roll(wide, 0, 1, stride=1, stride_axis=0)[:, : 2 * LANES]


def add_near(scores, t_scr):
    near = min(2 * LANES, scores.shape[1])
    fixed = scores[:, :near] + t_scr[:, :near]
    return fixed if near == scores.shape[1] else jnp.concatenate([fixed, scores[:, near:]], axis=1)


def add_corner(scores, t_scr):
    top, bottom = scores[:-LANES], scores[-LANES:]
    bottom = jnp.concatenate([bottom[:, :LANES] + t_scr[:, LANES:], bottom[:, LANES:]], axis=1)
    return jnp.concatenate([top, bottom], axis=0)


def at_step(head, stages, point, points):
    for due, stage in stages:
        if due >= 0 and due % points == point:
            pl.when(head == due // points)(stage)


def at_end(head, heads, stages):
    for due, stage in stages:
        if due < 0:
            pl.when(head == heads - 1)(stage)


FORWARD_POINTS = 4
BACKWARD_POINTS = 10


def attend_forward_kernel(*refs, causal, heads, plan):
    refs = list(refs)
    take = lambda n: [refs.pop(0) for _ in range(n)]
    if causal:
        (length_ref,) = take(1)
    q_ref, k_ref, v_ref = take(3)
    if causal:
        (base_ref,) = take(1)
    given = take(plan.inputs) if plan else []
    o_ref, lse_ref = take(2)
    made = take(plan.outputs) if plan else []
    s_scr, vt_scr, acc_scr, ot_scr = take(4)
    if causal:
        t_scr, mask_scr = take(2)
    stages = plan.stages(given, made, refs) if plan else []
    head, first, last, mask = head_place(heads)
    rows, keys = q_ref.shape[0], k_ref.shape[0]
    block = min(BLOCK, rows)
    if causal:
        bias_tiles(base_ref, t_scr)

        @pl.when(head == 0)
        def _():
            place = lax.broadcasted_iota(jnp.int32, (keys, LANES), 0)
            mask_scr[...] = jnp.where(place < length_ref[0], 0.0, negative)

    for at in range(0, keys, BLOCK):
        vt_scr[:, at : at + BLOCK] = jnp.where(mask, v_ref[at : at + BLOCK, :], 0).T

    def limit(scores, start):
        if start < BLOCK:
            return scores
        part = mask_scr[start : start + scores.shape[0], :]
        return scores + jnp.concatenate([part] * (scores.shape[1] // LANES), axis=1)

    for number in range(rows // block):
        at_step(head, stages, number, FORWARD_POINTS)
        start = number * block
        queries = jnp.where(mask, q_ref[start : start + block, :], 0)
        pieces = [(at, BLOCK, 0) for at in range(0, start if causal else keys, BLOCK)]
        if causal:
            pieces += [(start + part, LANES, part) for part in range(0, block, LANES)]
        largest = jnp.full((1, block), negative, jnp.float32)
        for at, size, skip in pieces:
            scores = nt(k_ref[at : at + size, :], queries[skip:])
            if causal:
                if size == LANES:
                    scores = add_near(scores, t_scr)
                elif at + size == start:
                    scores = add_corner(scores, t_scr)
                scores = limit(scores, at)
            s_scr[at : at + size, skip:] = scores
            top = jnp.maximum(largest[:, skip:], jnp.max(scores, axis=0, keepdims=True))
            largest = top if skip == 0 else jnp.concatenate([largest[:, :skip], top], axis=1)
        totals = jnp.zeros((1, block), jnp.float32)
        acc_scr[...] = jnp.zeros_like(acc_scr)
        for at, size, skip in pieces:
            expos = jnp.exp(s_scr[at : at + size, skip:] - largest[:, skip:])
            more = totals[:, skip:] + jnp.sum(expos, axis=0, keepdims=True)
            totals = more if skip == 0 else jnp.concatenate([totals[:, :skip], more], axis=1)
            acc_scr[:, skip:] += nn(vt_scr[:, at : at + size], expos.astype(low))
        lse_ref[0, :, start : start + block] = jnp.broadcast_to(largest + jnp.log(totals), (8, block))
        mixed = acc_scr[...] / totals
        ot_scr[:, start : start + block] = mixed + jnp.where(first, 0.0, ot_scr[:, start : start + block])

    @pl.when(last)
    def _():
        for at in range(0, rows, block):
            o_ref[at : at + block, :] = ot_scr[:, at : at + block].T.astype(low)

    at_end(head, heads, stages)


def attend_specs(queries, keys, padded):
    rows = queries.shape[0]
    width = padded or queries.shape[1]
    count = keys.shape[0]
    per_tile = LANES // HEAD
    skip = padded // LANES
    row_spec = pl.BlockSpec((rows, LANES), lambda h: (0, h // per_tile))
    key_spec = pl.BlockSpec((count, LANES), lambda h: (0, h // per_tile))
    key_specs = [pl.BlockSpec((count, LANES), lambda h, n=n: (0, n * skip + h // per_tile)) for n in (1, 2)]
    return rows, width, count, row_spec, key_spec, key_specs


def attend_forward(queries, keys, values, heads, padded=0, bias=None, length=None, plan=None, extra=()):
    causal = bias is not None
    rows, width, count, row_spec, _, key_specs = attend_specs(queries, keys, padded)
    block = min(BLOCK, rows)
    in_specs = [row_spec, *key_specs]
    args = [queries, keys, values]
    scratch = [
        pltpu.VMEM((count, block), jnp.float32), pltpu.VMEM((LANES, count), low),
        pltpu.VMEM((LANES, block), jnp.float32), pltpu.VMEM((LANES, rows), jnp.float32),
    ]
    if causal:
        in_specs = [pl.BlockSpec(memory_space=pltpu.SMEM), *in_specs, pl.BlockSpec((1, 1, 3 * LANES), lambda h: (h, 0, 0))]
        args = [length, *args, bias]
        scratch += [pltpu.VMEM((LANES, 2 * LANES), jnp.float32), pltpu.VMEM((count, LANES), jnp.float32)]
    return pl.pallas_call(
        functools.partial(attend_forward_kernel, causal=causal, heads=heads, plan=plan),
        grid=(heads,),
        in_specs=in_specs + (plan.in_specs() if plan else []),
        out_specs=[row_spec, pl.BlockSpec((1, 8, rows), lambda h: (h, 0, 0))] + (plan.out_specs() if plan else []),
        out_shape=[
            jax.ShapeDtypeStruct((rows, width), low),
            jax.ShapeDtypeStruct((heads, 8, rows), jnp.float32),
        ] + (plan.out_shape() if plan else []),
        scratch_shapes=scratch + (plan.scratch() if plan else []),
        compiler_params=plan.params() if plan else pltpu.CompilerParams(vmem_limit_bytes=60 * 2**20),
        cost_estimate=pl.CostEstimate(
            flops=4 * heads * LANES * rows * count // (2 if causal else 1),
            bytes_accessed=4 * (rows + count) * width,
            transcendentals=heads * rows * count // (2 if causal else 1),
        ),
        name="self_forward" if causal else "cross_forward",
    )(*args, *extra)


def attend_backward_kernel(*refs, causal, heads, plan):
    refs = list(refs)
    take = lambda n: [refs.pop(0) for _ in range(n)]
    if causal:
        (length_ref,) = take(1)
    q_ref, k_ref, v_ref, do_ref, o_ref, lse_ref = take(6)
    if causal:
        (base_ref,) = take(1)
    given = take(plan.inputs) if plan else []
    dq_ref, dk_ref, dv_ref = take(3)
    if causal:
        (distance_ref,) = take(1)
    made = take(plan.outputs) if plan else []
    kt_scr, dqt_scr, dk_scr, dv_scr, row_scr = take(5)
    if causal:
        t_scr, near_scr = take(2)
    stages = plan.stages(given, made, refs) if plan else []
    head, first, last, mask = head_place(heads)
    rows, keys = q_ref.shape[0], k_ref.shape[0]
    block = min(BLOCK, rows)
    key_block = min(BLOCK, keys)

    @pl.when(first)
    def _():
        dqt_scr[...] = jnp.zeros_like(dqt_scr)
        dk_scr[...] = jnp.zeros_like(dk_scr)
        dv_scr[...] = jnp.zeros_like(dv_scr)

    if causal:
        bias_tiles(base_ref, t_scr)
        near_scr[...] = jnp.zeros_like(near_scr)
    for at in range(0, keys, key_block):
        kt_scr[:, at : at + key_block] = jnp.where(mask, k_ref[at : at + key_block, :], 0).T
    for start in range(0, rows, block):
        at = slice(start, start + block)
        product = do_ref[at, :].astype(jnp.float32) * o_ref[at, :].astype(jnp.float32)
        delta = jnp.sum(jnp.where(mask, product, 0.0).T, axis=0, keepdims=True)
        logsum = lse_ref[0, 0:1, at]
        if causal:
            place = start + lax.broadcasted_iota(jnp.int32, (1, block), 1)
            logsum = jnp.where(place < length_ref[0], logsum, -negative)
        row_scr[0:1, at] = logsum
        row_scr[1:2, at] = delta

    def piece(key_at, row_at, fix=None):
        queries = jnp.where(mask, q_ref[row_at, :], 0)
        grads = jnp.where(mask, do_ref[row_at, :], 0)
        scores = nt(k_ref[key_at, :], queries)
        if fix is not None:
            scores = fix(scores, t_scr)
        weights = jnp.exp(scores - row_scr[0:1, row_at])
        grad_weights = nt(v_ref[key_at, :], grads)
        grad_scores = weights * (grad_weights - row_scr[1:2, row_at])
        low_scores = grad_scores.astype(low)
        dv_scr[key_at, :] += nn(weights.astype(low), grads)
        dk_scr[key_at, :] += nn(low_scores, queries)
        dqt_scr[:, row_at] += nn(kt_scr[:, key_at], low_scores)
        return grad_scores

    point = 0
    if not causal:
        at_step(head, stages, 0, 1)
        for start in range(0, keys, key_block):
            for at in range(0, rows, block):
                piece(slice(start, start + key_block), slice(at, at + block))
    else:
        for start in range(0, keys, block):
            at_step(head, stages, point, BACKWARD_POINTS)
            point += 1
            for here in range(start, start + block, LANES):
                grad = piece(slice(here, here + LANES), slice(here, start + block), add_near)
                near = min(2 * LANES, grad.shape[1])
                near_scr[:, :near] += grad[:, :near]
            for at in range(start + block, rows, block):
                at_step(head, stages, point, BACKWARD_POINTS)
                point += 1
                beside = at == start + block
                grad = piece(slice(start, start + block), slice(at, at + block), add_corner if beside else None)
                if beside:
                    near_scr[:, LANES:] += grad[-LANES:, :LANES]
        flip = lax.broadcasted_iota(jnp.int32, (LANES, LANES), 0) + lax.broadcasted_iota(jnp.int32, (LANES, LANES), 1)
        flip = (flip == LANES - 1).astype(jnp.float32)
        turned = lax.dot_general(
            flip, near_scr[...], (((1,), (0,)), ((), ())), precision=highest, preferred_element_type=jnp.float32
        )
        turned = pltpu.roll(turned, 1, 1, stride=1, stride_axis=0)
        sums = jnp.sum(turned[:, LANES:], axis=0, keepdims=True)
        at_row = lax.broadcasted_iota(jnp.int32, (8, LANES), 0) == head
        before = jnp.where(head == 0, 0.0, distance_ref[...])
        distance_ref[...] = jnp.where(at_row, jnp.broadcast_to(sums, (8, LANES)), before)

    @pl.when(last)
    def _():
        for at in range(0, rows, block):
            dq_ref[at : at + block, :] = dqt_scr[:, at : at + block].T.astype(low)
        dk_ref[...] = dk_scr[...].astype(low)
        dv_ref[...] = dv_scr[...].astype(low)

    at_end(head, heads, stages)


def attend_backward(queries, keys, values, grad_mixed, mixed, logsum, heads, padded=0, bias=None, length=None, plan=None, extra=()):
    causal = bias is not None
    rows, width, count, row_spec, key_spec, key_specs = attend_specs(queries, keys, padded)
    in_specs = [row_spec, *key_specs, row_spec, row_spec, pl.BlockSpec((1, 8, rows), lambda h: (h, 0, 0))]
    args = [queries, keys, values, grad_mixed, mixed, logsum]
    out_specs = [row_spec, key_spec, key_spec]
    out_shape = [jax.ShapeDtypeStruct((n, width), low) for n in (rows, count, count)]
    scratch = [
        pltpu.VMEM((LANES, count), low), pltpu.VMEM((LANES, rows), jnp.float32),
        pltpu.VMEM((count, LANES), jnp.float32), pltpu.VMEM((count, LANES), jnp.float32), pltpu.VMEM((8, rows), jnp.float32),
    ]
    if causal:
        in_specs = [pl.BlockSpec(memory_space=pltpu.SMEM), *in_specs, pl.BlockSpec((1, 1, 3 * LANES), lambda h: (h, 0, 0))]
        args = [length, *args, bias]
        out_specs += [pl.BlockSpec((8, LANES), lambda h: (0, 0))]
        out_shape += [jax.ShapeDtypeStruct((8, LANES), jnp.float32)]
        scratch += [pltpu.VMEM((LANES, 2 * LANES), jnp.float32), pltpu.VMEM((LANES, 2 * LANES), jnp.float32)]
    return pl.pallas_call(
        functools.partial(attend_backward_kernel, causal=causal, heads=heads, plan=plan),
        grid=(heads,),
        in_specs=in_specs + (plan.in_specs() if plan else []),
        out_specs=out_specs + (plan.out_specs() if plan else []),
        out_shape=out_shape + (plan.out_shape() if plan else []),
        scratch_shapes=scratch + (plan.scratch() if plan else []),
        compiler_params=plan.params() if plan else pltpu.CompilerParams(vmem_limit_bytes=60 * 2**20),
        cost_estimate=pl.CostEstimate(
            flops=10 * heads * LANES * rows * count // (2 if causal else 1),
            bytes_accessed=8 * (rows + count) * width,
            transcendentals=heads * rows * count // (2 if causal else 1),
        ),
        name="self_backward" if causal else "cross_backward",
    )(*args, *extra)


def scale_of(values):
    return lax.rsqrt(jnp.mean(values * values, axis=-1, keepdims=True) + epsilon)


def project_kernel(gain_lane, x_ref, w_ref, qkv_ref, normed_ref, gains_ref):
    @pl.when(pl.program_id(0) == 0)
    def _():
        tile = gain_lane // LANES * LANES
        turned = w_ref[:, tile : tile + LANES].astype(jnp.float32).T
        first = gain_lane - tile
        gains_ref[...] = turned[first : first + 8]

    values = x_ref[...].astype(jnp.float32)
    normed = (values * scale_of(values) * gains_ref[0:1, :]).astype(low)
    normed_ref[...] = normed
    qkv_ref[...] = nn(normed, w_ref[...]).astype(low)


def project(everyone, w_qkv, gain_lane):
    count, width = everyone.shape
    wide = w_qkv.shape[1]
    block = min(BLOCK, count)
    rows = lambda n: pl.BlockSpec((block, n), lambda i: (i, 0))
    return pl.pallas_call(
        functools.partial(project_kernel, gain_lane),
        grid=(count // block,),
        in_specs=[rows(width), pl.BlockSpec((width, wide), lambda i: (0, 0))],
        out_specs=[rows(wide), rows(width), pl.BlockSpec((8, width), lambda i: (0, 0))],
        out_shape=[
            jax.ShapeDtypeStruct((count, wide), low), jax.ShapeDtypeStruct((count, width), low),
            jax.ShapeDtypeStruct((8, width), jnp.float32),
        ],
        compiler_params=pltpu.CompilerParams(vmem_limit_bytes=40 * 2**20),
        name="project",
    )(everyone, w_qkv)


def unproject_kernel(x_ref, normed_ref, w_ref, dq_ref, dk_ref, dv_ref, part_ref, own_ref, gain_ref, own_scr):
    step = pl.program_id(0)
    padded = dq_ref.shape[1]
    grads = [r[...] for r in (dq_ref, dk_ref, dv_ref)]
    part = sum(nt(g, w_ref[:, n * padded : (n + 1) * padded]) for n, g in enumerate(grads))
    values = x_ref[...].astype(jnp.float32)
    share = jnp.sum(part * (values * scale_of(values)), axis=0, keepdims=True)
    part_ref[...] = part.astype(low)
    turned = normed_ref[...].T

    @pl.when(step == 0)
    def _():
        gain_ref[...] = jnp.zeros_like(gain_ref)
        own_scr[...] = jnp.zeros_like(own_scr)

    gain_ref[...] += jnp.broadcast_to(share, gain_ref.shape)
    for n, g in enumerate(grads):
        own_scr[:, n * padded : (n + 1) * padded] += nn(turned, g)

    @pl.when(step == pl.num_programs(0) - 1)
    def _():
        own_ref[...] = own_scr[...].astype(low)


def unproject(everyone, normed, w_qkv, dq, dk, dv):
    count, width = everyone.shape
    wide, padded = w_qkv.shape[1], dq.shape[1]
    block = min(BLOCK, count)
    rows = lambda n: pl.BlockSpec((block, n), lambda i: (i, 0))
    fixed = lambda a, b: pl.BlockSpec((a, b), lambda i: (0, 0))
    return pl.pallas_call(
        unproject_kernel,
        grid=(count // block,),
        in_specs=[rows(width), rows(width), fixed(width, wide), rows(padded), rows(padded), rows(padded)],
        out_specs=[rows(width), fixed(width, wide), fixed(8, width)],
        out_shape=[
            jax.ShapeDtypeStruct((count, width), low), jax.ShapeDtypeStruct((width, wide), low),
            jax.ShapeDtypeStruct((8, width), jnp.float32),
        ],
        scratch_shapes=[pltpu.VMEM((width, wide), jnp.float32)],
        compiler_params=pltpu.CompilerParams(vmem_limit_bytes=50 * 2**20),
        name="unproject",
    )(everyone, normed, w_qkv, dq, dk, dv)


slope = float(np.sqrt(2.0 / np.pi))
cubic = 0.044715


def middle_kernel(
    slabs, scalars, x1_ref, mixed_ref, co_ref, gains_ref, cot_ref, gate_ref, up_ref, down_ref,
    out_ref, dx_ref, dm_ref, co_grad_ref, gain_ref, packed,
    x2_scr, n3_scr, n3t_scr, df_scr, result_scr, dn_scr, gate_buf, up_buf, down_buf, sem,
):
    step, steps = pl.program_id(0), pl.num_programs(0)
    rows, width = x1_ref.shape
    block = gate_ref.shape[1]
    world, share = packed.shape[:2]
    inner = block * steps
    owners = down_buf.shape[1]
    hidden_share = block // owners

    @pl.when(step == 0)
    def _():
        x2 = x1_ref[...] + nn(mixed_ref[...], co_ref[...])
        x2_scr[...] = x2
        normed = (x2 * scale_of(x2) * gains_ref[2:3, :]).astype(low)
        n3_scr[...] = normed
        n3t_scr[...] = normed.T
        place = scalars[1] + lax.broadcasted_iota(jnp.int32, (rows, 1), 0)
        df_scr[...] = jnp.where(place < scalars[0], cot_ref[...], 0)
        result_scr[...] = x2
        dn_scr[...] = jnp.zeros_like(dn_scr)
        down_buf[...] = jnp.zeros_like(down_buf)

    normed, df = n3_scr[...], df_scr[...]
    gate, upper = nn(normed, gate_ref[...]), nn(normed, up_ref[...])
    bent = jnp.tanh(slope * (gate + cubic * (gate * gate * gate)))
    half = 0.5 * (1.0 + bent)
    active = gate * half
    hidden = (active * upper).astype(low)
    result_scr[...] += nn(hidden, down_ref[...])
    grad_hidden = nt(df, down_ref[...])
    rise = half + (0.5 * gate) * ((1.0 - bent * bent) * (slope + (3.0 * cubic * slope) * (gate * gate)))
    grad_gate = (grad_hidden * upper * rise).astype(low)
    grad_upper = (grad_hidden * active).astype(low)
    dn_scr[...] += nt(grad_gate, gate_ref[...]) + nt(grad_upper, up_ref[...])
    slot = lax.rem(step, 2)

    def sends(at, which):
        first = pl.multiple_of(at * block, LANES)
        yield pltpu.make_async_copy(gate_buf.at[which], packed.at[:, :, pl.ds(first, block)], sem.at[which, 0])
        yield pltpu.make_async_copy(up_buf.at[which], packed.at[:, :, pl.ds(pl.multiple_of(inner + at * block, LANES), block)], sem.at[which, 1])
        for k in range(slabs):
            column = 2 * inner + k * width
            yield pltpu.make_async_copy(
                down_buf.at[which, :, k], packed.at[pl.ds(at * owners, owners), :, column : column + width], sem.at[which, 2 + k]
            )

    @pl.when(step >= 2)
    def _():
        for copy in sends(step - 2, slot):
            copy.wait()

    turned = n3t_scr[...]
    gate_buf[slot] = nn(turned, grad_gate).reshape(world, share, block).astype(low)
    up_buf[slot] = nn(turned, grad_upper).reshape(world, share, block).astype(low)
    grad_down = tn(hidden, df)
    for o in range(owners):
        for k in range(slabs):
            size = min(share, hidden_share - k * share)
            start = o * hidden_share + k * share
            down_buf[slot, o, k, :size] = grad_down[start : start + size].astype(low)
    for copy in sends(step, slot):
        copy.start()

    @pl.when(step == steps - 1)
    def _():
        out_ref[...] = result_scr[...].astype(low)
        x2, grad_normed = x2_scr[...], dn_scr[...]
        scale = scale_of(x2)
        unit = x2 * scale
        grad_unit = grad_normed * gains_ref[2:3, :]
        gain_ref[...] = jnp.broadcast_to(jnp.sum(grad_normed * unit, axis=0, keepdims=True), gain_ref.shape)
        back = scale * (grad_unit - unit * jnp.mean(grad_unit * unit, axis=-1, keepdims=True))
        dx = df.astype(jnp.float32) + back
        dx_ref[...] = dx
        branch = dx.astype(low)
        dm_ref[...] = nt(branch, co_ref[...]).astype(low)
        co_grad_ref[...] = tn(mixed_ref[...], branch).astype(low)
        if steps > 1:
            for copy in sends(step - 1, 1 - slot):
                copy.wait()
        for copy in sends(step, slot):
            copy.wait()


def middle(scalars, x1, mixed, c_output, gains, cotangent, gate_up, w_down, world):
    rows, width = x1.shape
    inner = w_down.shape[0]
    block = min(BLOCK, inner)
    steps = inner // block
    share, hidden_share = width // world, inner // world
    slabs = -(-hidden_share // share)
    owners = block // hidden_share
    fixed = lambda *shape: pl.BlockSpec(shape, lambda j: (0,) * len(shape))
    f32 = jnp.float32
    return pl.pallas_call(
        functools.partial(middle_kernel, slabs),
        grid=(steps,),
        in_specs=[
            pl.BlockSpec(memory_space=pltpu.SMEM), fixed(rows, width), fixed(rows, width), fixed(width, width),
            fixed(8, width), fixed(rows, width),
            pl.BlockSpec((width, block), lambda j: (0, j)), pl.BlockSpec((width, block), lambda j: (0, steps + j)),
            pl.BlockSpec((block, width), lambda j: (j, 0)),
        ],
        out_specs=[
            fixed(rows, width), fixed(rows, width), fixed(rows, width), fixed(width, width), fixed(8, width),
            pl.BlockSpec(memory_space=pl.ANY),
        ],
        out_shape=[
            jax.ShapeDtypeStruct((rows, width), low), jax.ShapeDtypeStruct((rows, width), f32),
            jax.ShapeDtypeStruct((rows, width), low), jax.ShapeDtypeStruct((width, width), low),
            jax.ShapeDtypeStruct((8, width), f32),
            jax.ShapeDtypeStruct((world, share, 2 * inner + slabs * width), low),
        ],
        scratch_shapes=[
            pltpu.VMEM((rows, width), f32), pltpu.VMEM((rows, width), low), pltpu.VMEM((width, rows), low),
            pltpu.VMEM((rows, width), low), pltpu.VMEM((rows, width), f32), pltpu.VMEM((rows, width), f32),
            pltpu.VMEM((2, world, share, block), low), pltpu.VMEM((2, world, share, block), low),
            pltpu.VMEM((2, owners, slabs, share, width), low), pltpu.SemaphoreType.DMA((2, 2 + slabs)),
        ],
        compiler_params=pltpu.CompilerParams(vmem_limit_bytes=62 * 2**20),
        cost_estimate=pl.CostEstimate(
            flops=2 * rows * width * (9 * inner + 3 * width), transcendentals=rows * inner, bytes_accessed=26 * width * inner // 4
        ),
        name="middle",
    )(scalars, x1, mixed, c_output, gains, cotangent, gate_up, gate_up, w_down)


def coordinates():
    place, slot = lax.axis_index("seq"), lax.axis_index("fsdp")
    return place // 2, lax.rem(place, 2), slot // 2, lax.rem(slot, 2)


def device(x, c, z, y):
    return (x * 2 + c, z * 2 + y)


class Near:
    def __init__(self, nz):
        self.nz = nz
        x, c, z, y = self.x, self.c, self.z, self.y = coordinates()
        self.by_x, self.by_core, self.by_y = device(1 - x, c, z, y), device(x, 1 - c, z, y), device(x, c, z, 1 - y)
        self.diagonal = device(1 - x, 1 - c, z, y)
        self.steps = [lax.rem(z + t, nz) for t in range(nz)]
        self.backs = [lax.rem(z - t + nz, nz) for t in range(nz)]
        self.by_z = [device(x, c, self.steps[t], y) for t in range(nz)]


def greet(others):
    barrier = pltpu.get_barrier_semaphore()
    for other in others:
        pl.semaphore_signal(barrier, inc=1, device_id=other, device_id_type=MESH)
    pl.semaphore_wait(barrier, len(others))


class Copies:
    def __init__(self, send_sem, recv_sem):
        self.send_sem, self.recv_sem, self.made = send_sem, recv_sem, []

    def add(self, source, target, other):
        self.made.append((source, target, other))
        return len(self.made) - 1

    def copy(self, number):
        source, target, other = self.made[number]
        return pltpu.make_async_remote_copy(
            src_ref=source(), dst_ref=target(), send_sem=self.send_sem.at[number], recv_sem=self.recv_sem.at[number],
            device_id=other, device_id_type=MESH,
        )

    def start(self, *numbers):
        for number in numbers:
            self.copy(number).start()

    def arrive(self, *numbers):
        for number in numbers:
            self.copy(number).wait_recv()

    def finish(self):
        for number in range(len(self.made)):
            self.copy(number).wait_send()


def add_low(target, left, right):
    count = left.shape[0]
    unroll = 4 if count % 4 == 0 else 1

    @pl.loop(0, count // unroll)
    def _(n):
        for k in range(unroll):
            at = n * unroll + k
            if target.dtype == low:
                target[at] = left[at] + right[at]
            else:
                target[at] = left[at].astype(target.dtype) + right[at].astype(target.dtype)


def whole(space=pltpu.VMEM):
    return pl.BlockSpec(memory_space=space)


class GatherPlan:
    inputs, outputs = 1, 1

    def __init__(self, nz, count, share, width):
        self.nz, self.count, self.share, self.width = nz, count, share, width
        self.total = 8 * nz - 1

    def in_specs(self):
        return [whole()]

    def out_specs(self):
        return [whole(pl.ANY)]

    def out_shape(self):
        return [jax.ShapeDtypeStruct((self.count, 2, 2, self.nz, 2, self.share, self.width), low)]

    def scratch(self):
        return [pltpu.SemaphoreType.DMA((self.total,)), pltpu.SemaphoreType.DMA((self.total,)), pltpu.SemaphoreType.DMA((1,))]

    def params(self):
        return pltpu.CompilerParams(collective_id=2, has_side_effects=True, vmem_limit_bytes=60 * 2**20)

    def stages(self, given, made, scratch):
        (src,), (out,), (send_sem, recv_sem, local_sem) = given, made, scratch
        nz, my = self.nz, Near(self.nz)
        x, c, z, y, backs = my.x, my.c, my.z, my.y, my.backs
        copies = Copies(send_sem, recv_sem)
        own = lambda: src
        at = lambda xx, cc, zz, yy: lambda: out.at[:, xx, cc, zz, yy]
        mine = at(x, c, z, y)
        by_z = [None] + [copies.add(own, mine, my.by_z[t]) for t in range(1, nz)]
        held = [mine if t == 0 else at(x, c, backs[t], y) for t in range(nz)]
        source = [own if t == 0 else held[t] for t in range(nz)]
        by_y = [copies.add(source[t], held[t], my.by_y) for t in range(nz)]
        by_x = [copies.add(source[t], held[t], my.by_x) for t in range(nz)]
        by_core = [copies.add(source[t], held[t], my.by_core) for t in range(nz)]
        from_x = [at(1 - x, c, backs[t], y) for t in range(nz)]
        from_y = [at(x, c, backs[t], 1 - y) for t in range(nz)]
        far = [at(1 - x, c, backs[t], 1 - y) for t in range(nz)]
        corner = [
            copies.add(from_x[t], from_x[t], my.by_y) if t % 2 == 0 else copies.add(from_y[t], from_y[t], my.by_x)
            for t in range(nz)
        ]
        core_x = [copies.add(from_x[t], from_x[t], my.by_core) for t in range(nz)]
        core_y = [copies.add(from_y[t], from_y[t], my.by_core) for t in range(nz)]
        core_far = [copies.add(far[t], far[t], my.by_core) for t in range(nz)]
        local = lambda: pltpu.make_async_copy(src, mine(), local_sem.at[0])

        def begin():
            greet([my.by_x, my.by_core, my.by_y, *my.by_z[1:]])
            copies.start(*by_z[1:], by_y[0], by_x[0], by_core[0])
            local().start()

        def line(t):
            copies.arrive(by_z[t])
            copies.start(by_y[t], by_x[t], by_core[t])

        def plane(t):
            copies.arrive(by_x[t])
            copies.start(*([corner[t]] if t % 2 == 0 else []), core_x[t])
            copies.arrive(by_y[t])
            copies.start(*([corner[t]] if t % 2 == 1 else []), core_y[t])

        def turn(t):
            copies.arrive(corner[t])
            copies.start(core_far[t])

        def end():
            local().wait()
            copies.arrive(*by_core, *core_x, *core_y, *core_far)
            copies.finish()

        work = [functools.partial(line, t) for t in range(1, nz)]
        work += [functools.partial(plane, t) for t in range(nz)] + [functools.partial(turn, t) for t in range(nz)]
        points = 3 * FORWARD_POINTS - 1
        stages = [(0, begin)]
        for number, stage in enumerate(work):
            stages.append((1 + number * points // (len(work) + 1), stage))
        return stages + [(-1, end)]


class ReducePlan:
    def __init__(self, nz, count, share, width, number, points, slabs=None):
        self.nz, self.count, self.share, self.width, self.slabs = nz, count, share, width, slabs
        self.number, self.points = number, points
        self.inputs = count + (slabs is not None)
        self.outputs = 1 + (slabs is not None)
        self.total = count * (nz + 1) + count + 2 * (slabs is not None)

    def in_specs(self):
        return [whole()] * self.inputs

    def out_specs(self):
        return [whole()] * self.outputs

    def out_shape(self):
        shapes = [jax.ShapeDtypeStruct((self.count, self.share, self.width), jnp.float32)]
        return shapes + ([jax.ShapeDtypeStruct(self.slabs, jnp.float32)] if self.slabs else [])

    def scratch(self):
        nz, tail = self.nz, (self.share, self.width)
        vmem = lambda *shape: pltpu.VMEM((self.count, *shape, *tail), low)
        slabs = [pltpu.VMEM((*lead, *self.slabs), low) for lead in ((2,), (2,), ())] if self.slabs else []
        sems = [pltpu.SemaphoreType.DMA((self.total,)), pltpu.SemaphoreType.DMA((self.total,))]
        return [vmem(2, 2, nz), vmem(2, nz, 2), vmem(2, nz), vmem(2, nz), vmem(nz), vmem(nz), vmem(nz - 1), *slabs, *sems]

    def params(self):
        return pltpu.CompilerParams(collective_id=self.number, has_side_effects=True, vmem_limit_bytes=60 * 2**20)

    def stages(self, given, made, scratch):
        squares, out, beside = given[: self.count], made[0], self.slabs is not None
        a, ra, b, rb, d, rd, re = scratch[:7]
        send_sem, recv_sem = scratch[-2:]
        if beside:
            enc, out_enc, (enc_r, enc_a, enc_rx) = given[-1], made[1], scratch[7:10]
        nz, my, count = self.nz, Near(self.nz), self.count
        x, c, z, y = my.x, my.c, my.z, my.y
        copies = Copies(send_sem, recv_sem)
        if beside:
            enc_core = copies.add(lambda: enc.at[:, 1 - c], lambda: enc_r, my.by_core)
            enc_x = copies.add(lambda: enc_a.at[1 - x], lambda: enc_rx, my.by_x)
        core = [copies.add(lambda n=n: squares[n].at[:, 1 - c], lambda n=n: ra.at[n], my.by_core) for n in range(count)]
        one, two, three = [], [], []
        for n in range(count):
            y_first = n % 2 == 0
            if y_first:
                one.append(copies.add(lambda n=n: a.at[n, :, 1 - y], lambda n=n: rb.at[n], my.by_y))
                two.append(copies.add(lambda n=n: b.at[n, 1 - x], lambda n=n: rd.at[n], my.by_x))
            else:
                one.append(copies.add(lambda n=n: a.at[n, 1 - x], lambda n=n: rb.at[n], my.by_x))
                two.append(copies.add(lambda n=n: b.at[n, 1 - y], lambda n=n: rd.at[n], my.by_y))
            three.append([
                copies.add(lambda n=n, t=t: d.at[n, my.steps[t]], lambda n=n, t=t: re.at[n, t - 1], my.by_z[t])
                for t in range(1, nz)
            ])

        def begin():
            greet([my.by_x, my.by_core, my.by_y, *my.by_z[1:]])
            copies.start(*core, *([enc_core] if beside else []))

        def after_core(n):
            copies.arrive(core[n])
            for half in range(2):
                for side in range(2):
                    add_low(a.at[n, half, side], squares[n].at[half, c, :, side], ra.at[n, half, :, side])
            copies.start(one[n])

        def after_one(n):
            copies.arrive(one[n])
            for side in range(2):
                if n % 2 == 0:
                    add_low(b.at[n, side], a.at[n, side, y], rb.at[n, side])
                else:
                    add_low(b.at[n, side], a.at[n, x, side], rb.at[n, side])
            copies.start(two[n])

        def after_two(n):
            copies.arrive(two[n])
            add_low(d.at[n], b.at[n, x if n % 2 == 0 else y], rd.at[n])
            copies.start(*three[n])

        def after_three(n):
            copies.arrive(*three[n])
            total = d[n, z].astype(jnp.float32)
            for t in range(nz - 1):
                total += re[n, t].astype(jnp.float32)
            out[n] = total

        def encoder():
            copies.arrive(enc_core)
            for half in range(2):
                add_low(enc_a.at[half], enc.at[half, c], enc_r.at[half])
            copies.start(enc_x)

        def end():
            if beside:
                copies.arrive(enc_x)
                add_low(out_enc, enc_a.at[x], enc_rx)
            for n in range(count):
                after_three(n)
            copies.finish()

        part = functools.partial
        work = [part(after_core, n) for n in range(count)] + ([encoder] if beside else [])
        work += [part(after_one, n) for n in range(count)] + [part(after_two, n) for n in range(count)]
        first, last = self.points // 12, self.points - 1 - self.points // 12
        stages = [(0, begin)]
        for number, stage in enumerate(work):
            stages.append((first + number * (last - first) // max(len(work) - 1, 1), stage))
        return stages + [(-1, end)]


def gather_kernel(nz, tok, enc, own, everyone, encoded, qkv_out, send_sem, recv_sem, local_sem):
    my = Near(nz)
    x, c, z, y, backs = my.x, my.c, my.z, my.y, my.backs
    greet([my.by_x, my.by_core, my.diagonal, my.by_y, *my.by_z[1:]])
    copies = Copies(send_sem, recv_sem)
    local = [
        pltpu.make_async_copy(source, target, local_sem.at[n])
        for n, (source, target) in enumerate(
            [(own.at[x, c], qkv_out.at[x, c, z, y]), (tok, everyone.at[x, c]), (enc, encoded.at[x, c])]
        )
    ]
    for copy in local:
        copy.start()
    mine = lambda: qkv_out.at[x, c, z, y]
    first = [
        copies.add(lambda: own.at[1 - x, c], mine, my.by_x),
        copies.add(lambda: own.at[x, 1 - c], mine, my.by_core),
        copies.add(lambda: own.at[1 - x, 1 - c], mine, my.diagonal),
    ]
    rows = [(tok, everyone), (enc, encoded)]
    rows_x = [copies.add(lambda s=s: s, lambda t=t: t.at[x, c], my.by_x) for s, t in rows]
    rows_core = [copies.add(lambda s=s: s, lambda t=t: t.at[x, c], my.by_core) for s, t in rows]
    rows_far = [copies.add(lambda t=t: t.at[1 - x, c], lambda t=t: t.at[1 - x, c], my.by_core) for s, t in rows]
    line = [lambda t=t: qkv_out.at[:, :, backs[t], y] for t in range(nz)]
    by_z = [None] + [copies.add(line[0], line[0], my.by_z[t]) for t in range(1, nz)]
    by_y = [copies.add(line[t], line[t], my.by_y) for t in range(nz)]
    copies.start(*first, *rows_x, *rows_core)
    for copy in local:
        copy.wait()
    copies.arrive(*first)
    copies.start(*by_z[1:], by_y[0])
    for t in range(1, nz):
        copies.arrive(by_z[t])
        copies.start(by_y[t])
    for n in range(2):
        copies.arrive(rows_x[n])
        copies.start(rows_far[n])
    copies.arrive(*by_y, *rows_core, *rows_far)
    copies.finish()


def gather(nz, tok, enc, own):
    share, wide = own.shape[-2:]
    shapes = [
        jax.ShapeDtypeStruct((2, 2, *tok.shape), tok.dtype),
        jax.ShapeDtypeStruct((2, 2, *enc.shape), enc.dtype),
        jax.ShapeDtypeStruct((2, 2, nz, 2, share, wide), own.dtype),
    ]
    total = 9 + 2 * nz - 1
    return pl.pallas_call(
        functools.partial(gather_kernel, nz),
        in_specs=[whole()] * 3,
        out_specs=[whole(pl.ANY)] * 3,
        out_shape=shapes,
        scratch_shapes=[
            pltpu.SemaphoreType.DMA((total,)), pltpu.SemaphoreType.DMA((total,)), pltpu.SemaphoreType.DMA((3,)),
        ],
        compiler_params=pltpu.CompilerParams(collective_id=0, has_side_effects=True, vmem_limit_bytes=8 * 2**20),
        name="gather",
    )(tok, enc, own)


def reduce_kernel(nz, group_width, square, own, tok, gain, near, out_square, out_q, out_k, out_v, out_tok, out_gain, out_near, *refs):
    (a, ra, b, rb, d, rd, re, own_r, own_a, own_rz, own_f, own_in, tok_r, tok_a, tok_rx, gain_r, near_r,
     send_sem, recv_sem, gain_send, gain_recv) = refs
    my = Near(nz)
    x, c, z, y = my.x, my.c, my.z, my.y
    world, slots = 8 * nz, 2 * nz
    place, slot = lax.axis_index("seq"), lax.axis_index("fsdp")
    me = place * slots + slot
    barrier = pltpu.get_barrier_semaphore()

    @pl.loop(1, world)
    def _(t):
        other = lax.rem(me + t, world)
        pl.semaphore_signal(barrier, inc=1, device_id=(other // slots, lax.rem(other, slots)), device_id_type=MESH)

    pl.semaphore_wait(barrier, world - 1)
    copies = Copies(send_sem, recv_sem)
    add = copies.add
    half = tok.shape[2] // 2
    padded = own.shape[-1] // 3
    cut = lambda p: slice(p * half, (p + 1) * half)
    own_cut = lambda n: slice(n * padded, (n + 1) * padded)
    tok_core = [
        add(lambda h=h, p=p: tok.at[h, 1 - c, cut(p)], lambda h=h, p=p: tok_r.at[h, cut(p)], my.by_core)
        for h in (1 - x, x) for p in range(2)
    ]
    own_y = [
        add(lambda n=n: own.at[:, :, :, 1 - y, :, own_cut(n)], lambda n=n: own_r.at[n], my.by_y) for n in range(3)
    ]
    core = add(lambda: square.at[:, 1 - c], lambda: ra, my.by_core)
    near_all = [add(lambda: near, lambda t=t: near_r.at[t - 1], (place, lax.rem(slot + t, slots))) for t in range(1, slots)]
    tok_x = [add(lambda p=p: tok_a.at[1 - x, cut(p)], lambda p=p: tok_rx.at[cut(p)], my.by_x) for p in range(2)]
    one = add(lambda: a.at[:, 1 - y], lambda: rb, my.by_y)
    two = add(lambda: b.at[1 - x], lambda: rd, my.by_x)
    three = [add(lambda t=t: d.at[my.steps[t]], lambda t=t: re.at[t - 1], my.by_z[t]) for t in range(1, nz)]
    own_z = [
        [add(lambda n=n, t=t: own_a.at[n, :, :, my.steps[t]], lambda n=n, t=t: own_rz.at[n, t - 1], my.by_z[t]) for t in range(1, nz)]
        for n in range(3)
    ]
    landing = lambda: own_in.at[:, x, c]
    own_seq = [
        add(lambda: own_f.at[:, 1 - x, c], landing, my.by_x),
        add(lambda: own_f.at[:, x, 1 - c], landing, my.by_core),
        add(lambda: own_f.at[:, 1 - x, 1 - c], landing, my.diagonal),
    ]

    def gain_copy(t):
        other = lax.rem(me + t, world)
        return pltpu.make_async_remote_copy(
            src_ref=gain.at[other], dst_ref=gain_r.at[t - 1], send_sem=gain_send.at[t - 1], recv_sem=gain_recv.at[t - 1],
            device_id=(other // slots, lax.rem(other, slots)), device_id_type=MESH,
        )

    copies.start(own_y[0], *tok_core[:2], own_y[1], core, *tok_core[2:], own_y[2], *near_all)

    @pl.loop(1, world)
    def _(t):
        gain_copy(t).start()

    def tok_sum(h, p):
        add_low(tok_a.at[h, cut(p)], tok.at[h, c, cut(p)], tok_r.at[h, cut(p)])

    for p in range(2):
        copies.arrive(tok_core[p])
        tok_sum(1 - x, p)
        copies.start(tok_x[p])
    copies.arrive(core)
    for h in range(2):
        for side in range(2):
            add_low(a.at[h, side], square.at[h, c, :, side], ra.at[h, :, side])
    copies.start(one)

    def own_sum(n):
        copies.arrive(own_y[n])
        for h in range(2):
            for side in range(2):
                for k in range(nz):
                    own_a[n, h, side, k] = own[h, side, k, y, :, own_cut(n)] + own_r[n, h, side, k]
        copies.start(*own_z[n])

    own_sum(0)
    for p in range(2):
        copies.arrive(tok_core[2 + p])
        tok_sum(x, p)
    own_sum(1)
    own_sum(2)
    copies.arrive(one)
    for side in range(2):
        add_low(b.at[side], a.at[side, y], rb.at[side])
    copies.start(two)
    for n in range(3):
        copies.arrive(*own_z[n])
        for h in range(2):
            for side in range(2):
                total = own_a[n, h, side, z].astype(jnp.float32)
                for t in range(nz - 1):
                    total += own_rz[n, t, h, side].astype(jnp.float32)
                own_f[n, h, side] = total.astype(low)
    copies.start(*own_seq)
    own_in[:, x, c] = own_f[:, x, c]
    copies.arrive(two)
    add_low(d, b.at[x], rd)
    copies.start(*three)
    copies.arrive(*near_all)
    total = near[...]
    for t in range(slots - 1):
        total += near_r[t]
    out_near[...] = total
    out_gain[...] = gain[me]

    @pl.loop(1, world)
    def _(t):
        gain_copy(t).wait_recv()
        out_gain[...] += gain_r[t - 1]

    for p in range(2):
        copies.arrive(tok_x[p])
        add_low(out_tok.at[cut(p)], tok_a.at[x, cut(p)], tok_rx.at[cut(p)])
    copies.arrive(*own_seq)
    for n, out in enumerate((out_q, out_k, out_v)):
        parts = [own_in[n, s // 2, s % 2, :, :group_width].astype(jnp.float32) for s in range(4)]
        out[...] = jnp.concatenate(parts, axis=1)
    copies.arrive(*three)
    total = d[z].astype(jnp.float32)
    for t in range(nz - 1):
        total += re[t].astype(jnp.float32)
    out_square[...] = total
    copies.finish()

    @pl.loop(1, world)
    def _(t):
        gain_copy(t).wait_send()


def reduce(nz, group_width, square, own, tok, gain, near):
    share, width = square.shape[-2:]
    wide = own.shape[-1]
    vmem = lambda *shape: pltpu.VMEM(shape, low)
    slabs = tok.shape[2:]
    world = 8 * nz
    padded = wide // 3
    total = 4 + 3 + 1 + 2 * nz - 1 + 2 + 2 + nz - 1 + 3 * (nz - 1) + 3
    f32 = lambda *shape: jax.ShapeDtypeStruct(shape, jnp.float32)
    return pl.pallas_call(
        functools.partial(reduce_kernel, nz, group_width),
        in_specs=[whole()] * 5,
        out_specs=[whole()] * 7,
        out_shape=[f32(share, width)] * 4 + [f32(*slabs), f32(*gain.shape[1:]), f32(*near.shape)],
        scratch_shapes=[
            vmem(2, 2, nz, share, width), vmem(2, nz, 2, share, width), vmem(2, nz, share, width), vmem(2, nz, share, width),
            vmem(nz, share, width), vmem(nz, share, width), vmem(nz - 1, share, width),
            vmem(3, 2, 2, nz, share, padded), vmem(3, 2, 2, nz, share, padded), vmem(3, nz - 1, 2, 2, share, padded),
            vmem(3, 2, 2, share, padded), vmem(3, 2, 2, share, padded),
            vmem(2, *slabs), vmem(2, *slabs), vmem(*slabs),
            pltpu.VMEM((world - 1, *gain.shape[1:]), jnp.float32), pltpu.VMEM((2 * nz - 1, *near.shape), jnp.float32),
            pltpu.SemaphoreType.DMA((total,)), pltpu.SemaphoreType.DMA((total,)),
            pltpu.SemaphoreType.DMA((world - 1,)), pltpu.SemaphoreType.DMA((world - 1,)),
        ],
        compiler_params=pltpu.CompilerParams(collective_id=1, has_side_effects=True, vmem_limit_bytes=60 * 2**20),
        name="reduce",
    )(square, own, tok, gain, near)


def rms_norm(values, gain):
    scale = lax.rsqrt(jnp.mean(values * values, axis=-1, keepdims=True) + epsilon)
    return values * scale * gain


def rms_back(values, gain, grad_normed):
    scale = lax.rsqrt(jnp.mean(values * values, axis=-1, keepdims=True) + epsilon)
    unit = values * scale
    grad_unit = grad_normed * gain
    grad_gain = jnp.sum(grad_normed * unit, axis=0)
    grad_values = scale * (grad_unit - unit * jnp.mean(grad_unit * unit, axis=-1, keepdims=True))
    return (grad_values, grad_gain)


def activate(gate, upper):
    return jax.nn.gelu(gate, approximate=True) * upper


def per_device(
    tokens, encoder, cotangent, lengths, gains, self_query, self_key, self_value, self_output,
    cross_query, cross_key, cross_value, cross_output, ffn_gate, ffn_up, ffn_down, rel_bias,
):
    both = ("seq", "fsdp")
    seq, fsdp = lax.axis_size("seq"), lax.axis_size("fsdp")
    world = seq * fsdp
    nz = fsdp // 2
    share, width = self_query.shape
    hidden_share = ffn_down.shape[0]
    inner = ffn_gate.shape[1]
    rows = tokens.shape[1]
    group = rel_bias.shape[1]
    group_width = group * HEAD
    padded = -(-group_width // LANES) * LANES
    spare = padded - group_width
    heads = width // HEAD
    place = lax.axis_index("seq")
    aligned = share % 8 == 0

    gate_up = lax.all_gather(jnp.concatenate([ffn_gate.astype(low), ffn_up.astype(low)], axis=1), both, axis=0, tiled=True)
    w_down = lax.all_gather(ffn_down.astype(low), both, axis=0, tiled=True)
    squares = jnp.stack([w.astype(low) for w in (self_output, cross_query, cross_key, cross_value, cross_output)])
    gain_columns = jnp.pad(gains.astype(low).T, ((0, 0), (0, spare - 3)))
    pieces = []
    for s in range(seq):
        for n, w in enumerate((self_query, self_key, self_value)):
            pieces.append(w[:, s * group_width : (s + 1) * group_width].astype(low))
            pieces.append(gain_columns if n == 0 else jnp.zeros((share, spare), low))
    own = jnp.concatenate(pieces, axis=1).reshape(share, seq, 3 * padded).transpose(1, 0, 2)
    if aligned:
        everyone, encoded, w_qkv = gather(nz, tokens[0], encoder[0], own.reshape(2, 2, share, 3 * padded))
    else:
        everyone = lax.all_gather(tokens[0], "seq", axis=0)
        encoded = lax.all_gather(encoder[0], "seq", axis=0)
        w_qkv = lax.all_to_all(own, "seq", split_axis=0, concat_axis=0, tiled=True)
        w_qkv = lax.all_gather(w_qkv, "fsdp", axis=1)
    everyone = everyone.reshape(seq * rows, width)
    encoded = encoded.reshape(-1, width)
    w_qkv = w_qkv.reshape(width, 3 * padded)
    length = lengths[0]
    values_in = tokens[0].astype(jnp.float32)
    qkv, normed_all, gain_rows = project(everyone, w_qkv, group_width)
    bias = bias_rows(rel_bias)
    plan = GatherPlan(nz, 5, share, width) if aligned else None
    own_mixed, own_logsum, *gathered = attend_forward(
        qkv, qkv, qkv, group, padded, bias, lengths, plan, (squares,) if aligned else ()
    )
    squares = gathered[0] if aligned else jnp.moveaxis(lax.all_gather(squares, both, axis=0), 1, 0)
    squares = squares.reshape(5, width, width)
    w_output, c_query, c_key, c_value, c_output = (squares[n] for n in range(5))
    mixed = lax.all_to_all(own_mixed[:, :group_width], "seq", split_axis=0, concat_axis=1, tiled=True)
    attended = values_in + nn(mixed, w_output)
    normed_two = rms_norm(attended, gain_rows[1]).astype(low)
    cross_queries = nn(normed_two, c_query).astype(low)
    cross_keys = nn(encoded, c_key).astype(low)
    cross_values = nn(encoded, c_value).astype(low)
    cross_mixed, cross_logsum = attend_forward(cross_queries, cross_keys, cross_values, heads)
    slabs = -(-hidden_share // share)
    if aligned:
        scalars = jnp.stack([length, place * rows])
        result, grad_crossed, grad_cmixed, grad_coutput, gain_two, packed = middle(
            scalars, attended, cross_mixed, c_output, gain_rows, cotangent[0], gate_up, w_down, world
        )
        grad_gain_two = gain_two[0]
        packed = packed.reshape(width, -1)
    else:
        crossed = attended + nn(cross_mixed, c_output)
        normed_three = rms_norm(crossed, gain_rows[2]).astype(low)
        both_parts = nn(normed_three, gate_up)
        gate, upper = both_parts[:, :inner], both_parts[:, inner:]
        hidden = activate(gate, upper).astype(low)
        result = (crossed + nn(hidden, w_down)).astype(low)

        positions = place * rows + jnp.arange(rows, dtype=jnp.int32)
        grad_out = cotangent[0].astype(jnp.float32) * (positions < length).astype(jnp.float32)[:, None]
        grad_ffn = grad_out.astype(low)
        grad_hidden = nt(grad_ffn, w_down)
        _, pullback = jax.vjp(activate, gate, upper)
        grad_gate, grad_upper = pullback(grad_hidden)
        grad_both = jnp.concatenate([grad_gate.astype(low), grad_upper.astype(low)], axis=1)
        grad_down = tn(hidden, grad_ffn).astype(low).reshape(world, hidden_share, width)
        grad_down = jnp.pad(grad_down, ((0, 0), (0, slabs * share - hidden_share), (0, 0)))
        grad_down = grad_down.reshape(world, slabs, share, width).transpose(0, 2, 1, 3).reshape(world * share, slabs * width)
        packed = jnp.concatenate([tn(normed_three, grad_both).astype(low), grad_down], axis=1)

        grad_normed_three = nt(grad_both, gate_up)
        norm_part, grad_gain_two = rms_back(crossed, gain_rows[2], grad_normed_three)
        grad_crossed = grad_out + norm_part
        grad_branch = grad_crossed.astype(low)
        grad_coutput = tn(cross_mixed, grad_branch).astype(low)
        grad_cmixed = nt(grad_branch, c_output).astype(low)
    share_ffn = lax.psum_scatter(packed, both, scatter_dimension=0, tiled=True)
    slab = 64
    chunked = lambda g: g.reshape(2, 2, nz, 2, share, g.shape[-1])
    by_place = lambda g: g.reshape(2, 2, -1, slab, width)
    plan = ReducePlan(nz, 1, share, width, 4, heads) if aligned else None
    grad_cq, grad_ck, grad_cv, *first_sums = attend_backward(
        cross_queries, cross_keys, cross_values, grad_cmixed, cross_mixed, cross_logsum, heads,
        plan=plan, extra=(chunked(grad_coutput),) if aligned else (),
    )
    grad_cquery = tn(normed_two, grad_cq).astype(low)
    grad_ckey = tn(encoded, grad_ck).astype(low)
    grad_cvalue = tn(encoded, grad_cv).astype(low)
    grad_encoded = (nt(grad_ck, c_key) + nt(grad_cv, c_value)).astype(low)
    norm_part, grad_gain_one = rms_back(attended, gain_rows[1], nt(grad_cq, c_query))
    grad_attended = grad_crossed + norm_part
    grad_self_branch = grad_attended.astype(low)
    grad_output = tn(mixed, grad_self_branch).astype(low)
    grad_mixed = nt(grad_self_branch, w_output).astype(low)
    own_grad_mixed = lax.all_to_all(grad_mixed, "seq", split_axis=1, concat_axis=0, tiled=True)
    own_grad_mixed = jnp.pad(own_grad_mixed, ((0, 0), (0, padded - group_width)))
    early = [grad_cquery, grad_ckey, grad_cvalue]
    plan, extra = None, ()
    if aligned:
        extra = (*[chunked(g) for g in early], by_place(grad_encoded))
        plan = ReducePlan(nz, len(early), share, width, 3, 3 * BACKWARD_POINTS, extra[-1].shape[2:])
    own_dq, own_dk, own_dv, by_distance, *sums = attend_backward(
        qkv, qkv, qkv, own_grad_mixed, own_mixed, own_logsum, group, padded, bias, lengths, plan, extra
    )
    grad_normed_part, grad_own, gain_zero = unproject(everyone, normed_all, w_qkv, own_dq, own_dk, own_dv)
    grad_gain_zero = gain_zero[0]
    grad_gains = jnp.stack([grad_gain_zero, grad_gain_one, grad_gain_two])
    grad_gains = grad_gains.reshape(3, world, share).transpose(1, 0, 2).reshape(world, 1, 3 * share)
    grad_gains = jnp.pad(grad_gains, ((0, 0), (0, 7), (0, LANES - 3 * share)))
    wide = jnp.float32
    if aligned:
        share_output, *share_own, grad_normed, share_gains, by_distance = reduce(
            nz, group_width, chunked(grad_output), chunked(grad_own), by_place(grad_normed_part), grad_gains, by_distance
        )
        share_early, grad_encoded = sums
        share_squares = [share_output, *(share_early[n] for n in range(3)), first_sums[0][0]]
        grad_normed, grad_encoded = grad_normed.reshape(rows, width), grad_encoded.reshape(-1, width)
    else:
        scatter = lambda g, axes: lax.psum_scatter(g, axes, scatter_dimension=0, tiled=True)
        share_squares = scatter(jnp.concatenate([grad_output, *early, grad_coutput], axis=1), both).astype(wide)
        share_squares = [share_squares[:, n * width : (n + 1) * width] for n in range(5)]
        grad_own = scatter(grad_own.reshape(seq, fsdp, share, 3 * padded).transpose(1, 0, 2, 3), "fsdp")[0]
        grad_own = lax.all_to_all(grad_own, "seq", split_axis=0, concat_axis=0, tiled=True).astype(wide)
        grad_own = grad_own.reshape(seq, share, 3, padded)[:, :, :, :group_width].transpose(2, 1, 0, 3).reshape(3, share, width)
        share_own = [grad_own[n] for n in range(3)]
        grad_normed = scatter(grad_normed_part, "seq").astype(wide)
        grad_encoded = scatter(grad_encoded, "seq").astype(wide)
        share_gains = scatter(grad_gains, both)[0]
        by_distance = lax.psum(by_distance, "fsdp")
    share_gains = share_gains[0, : 3 * share].reshape(3, share)
    norm_part, _ = rms_back(values_in, gain_rows[0], grad_normed)
    grad_input = grad_attended + norm_part
    bins = rel_bias.shape[0]
    near_map = (buckets(jnp.arange(LANES, dtype=jnp.int32))[:, None] == jnp.arange(bins - 1, dtype=jnp.int32)[None]).astype(wide)
    near_sums = jnp.dot(near_map.T, by_distance[:group].T, precision=highest)
    table_grad = jnp.concatenate([near_sums, -jnp.sum(near_sums, axis=0, keepdims=True)], axis=0)
    share_ffn = share_ffn.astype(wide)
    share_down = share_ffn[:, 2 * inner :].reshape(share, slabs, width).transpose(1, 0, 2).reshape(slabs * share, width)
    return (
        result[None], grad_input[None], grad_encoded[None], share_gains, *share_own, *share_squares,
        share_ffn[:, :inner], share_ffn[:, inner : 2 * inner], share_down[:hidden_share], table_grad,
    )


def solution(mesh):
    split = P(("seq", "fsdp"), None)
    rows = P("fsdp", "seq", None)
    gains = P(None, ("seq", "fsdp"))
    return jax.shard_map(
        per_device,
        mesh=mesh,
        in_specs=(rows, rows, rows, P("fsdp"), gains, *([split] * 11), P(None, "seq")),
        out_specs=(rows, rows, rows, gains, *([split] * 11), P(None, "seq")),
        check_vma=False,
    )
```

```python
import functools

import jax
import jax.numpy as jnp
import numpy as np
from jax import lax
from jax.experimental import pallas as pl
from jax.experimental.pallas import tpu as pltpu
from jax.sharding import PartitionSpec as P

LANES = 128
BLOCK = 512
HEAD = 64
negative = -1e30
epsilon = 1e-06
highest = lax.Precision.HIGHEST
bounds = np.ceil(16.0 * 8.0 ** (np.arange(1, 16) / 16.0)).astype(np.int32)
low = jnp.bfloat16
MESH = pl.DeviceIdType.MESH


def nt(left, right):
    return lax.dot_general(left, right, (((1,), (1,)), ((), ())), preferred_element_type=jnp.float32)


def nn(left, right):
    return jnp.dot(left, right, preferred_element_type=jnp.float32)


def tn(left, right):
    return lax.dot_general(left, right, (((0,), (0,)), ((), ())), preferred_element_type=jnp.float32)


def buckets(distance):
    far = 16 + jnp.sum((distance[..., None] >= jnp.asarray(bounds)).astype(jnp.int32), axis=-1)
    return jnp.where(distance < 16, distance, far)


def bias_rows(table):
    count = table.shape[0]
    place = jnp.arange(3 * LANES, dtype=jnp.int32)
    onehot = buckets(jnp.clip(place, 0, 2 * LANES))[None, :] == jnp.arange(count, dtype=jnp.int32)[:, None]
    relative = table - table[count - 1 :]
    values = jnp.sum(jnp.where(onehot[:, None, :], relative[:, :, None], 0.0), axis=0)
    return jnp.where((place >= 2 * LANES)[None], negative, values)[:, None, :]


def head_place(heads):
    head = pl.program_id(0)
    per_tile = LANES // HEAD
    side = lax.rem(head, per_tile)
    lane = lax.broadcasted_iota(jnp.int32, (1, LANES), 1)
    return head, side == 0, (side == per_tile - 1) | (head == heads - 1), (lane // HEAD) == side


def bias_tiles(base_ref, t_scr):
    wide = jnp.broadcast_to(base_ref[0], (LANES, 3 * LANES))
    t_scr[...] = pltpu.roll(wide, 0, 1, stride=1, stride_axis=0)[:, : 2 * LANES]


def add_near(scores, t_scr):
    near = min(2 * LANES, scores.shape[1])
    fixed = scores[:, :near] + t_scr[:, :near]
    return fixed if near == scores.shape[1] else jnp.concatenate([fixed, scores[:, near:]], axis=1)


def add_corner(scores, t_scr):
    top, bottom = scores[:-LANES], scores[-LANES:]
    bottom = jnp.concatenate([bottom[:, :LANES] + t_scr[:, LANES:], bottom[:, LANES:]], axis=1)
    return jnp.concatenate([top, bottom], axis=0)


def at_step(head, stages, point, points):
    for due, stage in stages:
        if due >= 0 and due % points == point:
            pl.when(head == due // points)(stage)


def at_end(head, heads, stages):
    for due, stage in stages:
        if due < 0:
            pl.when(head == heads - 1)(stage)


FORWARD_POINTS = 4
BACKWARD_POINTS = 10


def attend_forward_kernel(*refs, causal, heads, plan):
    refs = list(refs)
    take = lambda n: [refs.pop(0) for _ in range(n)]
    if causal:
        (length_ref,) = take(1)
    q_ref, k_ref, v_ref = take(3)
    if causal:
        (base_ref,) = take(1)
    given = take(plan.inputs) if plan else []
    o_ref, lse_ref = take(2)
    made = take(plan.outputs) if plan else []
    s_scr, vt_scr, acc_scr, ot_scr = take(4)
    if causal:
        t_scr, mask_scr = take(2)
    stages = plan.stages(given, made, refs) if plan else []
    head, first, last, mask = head_place(heads)
    rows, keys = q_ref.shape[0], k_ref.shape[0]
    block = min(BLOCK, rows)
    if causal:
        bias_tiles(base_ref, t_scr)

        @pl.when(head == 0)
        def _():
            place = lax.broadcasted_iota(jnp.int32, (keys, LANES), 0)
            mask_scr[...] = jnp.where(place < length_ref[0], 0.0, negative)

    for at in range(0, keys, BLOCK):
        vt_scr[:, at : at + BLOCK] = jnp.where(mask, v_ref[at : at + BLOCK, :], 0).T

    def limit(scores, start):
        if start < BLOCK:
            return scores
        part = mask_scr[start : start + scores.shape[0], :]
        return scores + jnp.concatenate([part] * (scores.shape[1] // LANES), axis=1)

    for number in range(rows // block):
        at_step(head, stages, number, FORWARD_POINTS)
        start = number * block
        queries = jnp.where(mask, q_ref[start : start + block, :], 0)
        pieces = [(at, BLOCK, 0) for at in range(0, start if causal else keys, BLOCK)]
        if causal:
            pieces += [(start + part, LANES, part) for part in range(0, block, LANES)]
        largest = jnp.full((1, block), negative, jnp.float32)
        for at, size, skip in pieces:
            scores = nt(k_ref[at : at + size, :], queries[skip:])
            if causal:
                if size == LANES:
                    scores = add_near(scores, t_scr)
                elif at + size == start:
                    scores = add_corner(scores, t_scr)
                scores = limit(scores, at)
            s_scr[at : at + size, skip:] = scores
            top = jnp.maximum(largest[:, skip:], jnp.max(scores, axis=0, keepdims=True))
            largest = top if skip == 0 else jnp.concatenate([largest[:, :skip], top], axis=1)
        totals = jnp.zeros((1, block), jnp.float32)
        acc_scr[...] = jnp.zeros_like(acc_scr)
        for at, size, skip in pieces:
            expos = jnp.exp(s_scr[at : at + size, skip:] - largest[:, skip:])
            more = totals[:, skip:] + jnp.sum(expos, axis=0, keepdims=True)
            totals = more if skip == 0 else jnp.concatenate([totals[:, :skip], more], axis=1)
            acc_scr[:, skip:] += nn(vt_scr[:, at : at + size], expos.astype(low))
        lse_ref[0, :, start : start + block] = jnp.broadcast_to(largest + jnp.log(totals), (8, block))
        mixed = acc_scr[...] / totals
        ot_scr[:, start : start + block] = mixed + jnp.where(first, 0.0, ot_scr[:, start : start + block])

    @pl.when(last)
    def _():
        for at in range(0, rows, block):
            o_ref[at : at + block, :] = ot_scr[:, at : at + block].T.astype(low)

    at_end(head, heads, stages)


def attend_specs(queries, keys, padded):
    rows = queries.shape[0]
    width = padded or queries.shape[1]
    count = keys.shape[0]
    per_tile = LANES // HEAD
    skip = padded // LANES
    row_spec = pl.BlockSpec((rows, LANES), lambda h: (0, h // per_tile))
    key_spec = pl.BlockSpec((count, LANES), lambda h: (0, h // per_tile))
    key_specs = [pl.BlockSpec((count, LANES), lambda h, n=n: (0, n * skip + h // per_tile)) for n in (1, 2)]
    return rows, width, count, row_spec, key_spec, key_specs


def attend_forward(queries, keys, values, heads, padded=0, bias=None, length=None, plan=None, extra=()):
    causal = bias is not None
    rows, width, count, row_spec, _, key_specs = attend_specs(queries, keys, padded)
    block = min(BLOCK, rows)
    in_specs = [row_spec, *key_specs]
    args = [queries, keys, values]
    scratch = [
        pltpu.VMEM((count, block), jnp.float32), pltpu.VMEM((LANES, count), low),
        pltpu.VMEM((LANES, block), jnp.float32), pltpu.VMEM((LANES, rows), jnp.float32),
    ]
    if causal:
        in_specs = [pl.BlockSpec(memory_space=pltpu.SMEM), *in_specs, pl.BlockSpec((1, 1, 3 * LANES), lambda h: (h, 0, 0))]
        args = [length, *args, bias]
        scratch += [pltpu.VMEM((LANES, 2 * LANES), jnp.float32), pltpu.VMEM((count, LANES), jnp.float32)]
    return pl.pallas_call(
        functools.partial(attend_forward_kernel, causal=causal, heads=heads, plan=plan),
        grid=(heads,),
        in_specs=in_specs + (plan.in_specs() if plan else []),
        out_specs=[row_spec, pl.BlockSpec((1, 8, rows), lambda h: (h, 0, 0))] + (plan.out_specs() if plan else []),
        out_shape=[
            jax.ShapeDtypeStruct((rows, width), low),
            jax.ShapeDtypeStruct((heads, 8, rows), jnp.float32),
        ] + (plan.out_shape() if plan else []),
        scratch_shapes=scratch + (plan.scratch() if plan else []),
        compiler_params=plan.params() if plan else pltpu.CompilerParams(vmem_limit_bytes=62 * 2**20),
        cost_estimate=pl.CostEstimate(
            flops=4 * heads * LANES * rows * count // (2 if causal else 1),
            bytes_accessed=4 * (rows + count) * width,
            transcendentals=heads * rows * count // (2 if causal else 1),
        ),
        name="self_forward" if causal else "cross_forward",
    )(*args, *extra)


def attend_backward_kernel(*refs, causal, heads, plan):
    refs = list(refs)
    take = lambda n: [refs.pop(0) for _ in range(n)]
    if causal:
        (length_ref,) = take(1)
    q_ref, k_ref, v_ref, do_ref, o_ref, lse_ref = take(6)
    if causal:
        (base_ref,) = take(1)
    given = take(plan.inputs) if plan else []
    dq_ref, dk_ref, dv_ref = take(3)
    if causal:
        (distance_ref,) = take(1)
    made = take(plan.outputs) if plan else []
    kt_scr, dqt_scr, dk_scr, dv_scr, row_scr = take(5)
    if causal:
        t_scr, near_scr = take(2)
    stages = plan.stages(given, made, refs) if plan else []
    head, first, last, mask = head_place(heads)
    rows, keys = q_ref.shape[0], k_ref.shape[0]
    block = min(BLOCK, rows)
    key_block = min(BLOCK, keys)

    @pl.when(first)
    def _():
        dqt_scr[...] = jnp.zeros_like(dqt_scr)
        dk_scr[...] = jnp.zeros_like(dk_scr)
        dv_scr[...] = jnp.zeros_like(dv_scr)

    if causal:
        bias_tiles(base_ref, t_scr)
        near_scr[...] = jnp.zeros_like(near_scr)
    for at in range(0, keys, key_block):
        kt_scr[:, at : at + key_block] = jnp.where(mask, k_ref[at : at + key_block, :], 0).T
    for start in range(0, rows, block):
        at = slice(start, start + block)
        product = do_ref[at, :].astype(jnp.float32) * o_ref[at, :].astype(jnp.float32)
        delta = jnp.sum(jnp.where(mask, product, 0.0).T, axis=0, keepdims=True)
        logsum = lse_ref[0, 0:1, at]
        if causal:
            place = start + lax.broadcasted_iota(jnp.int32, (1, block), 1)
            logsum = jnp.where(place < length_ref[0], logsum, -negative)
        row_scr[0:1, at] = logsum
        row_scr[1:2, at] = delta

    def piece(key_at, row_at, fix=None):
        queries = jnp.where(mask, q_ref[row_at, :], 0)
        grads = jnp.where(mask, do_ref[row_at, :], 0)
        scores = nt(k_ref[key_at, :], queries)
        if fix is not None:
            scores = fix(scores, t_scr)
        weights = jnp.exp(scores - row_scr[0:1, row_at])
        grad_weights = nt(v_ref[key_at, :], grads)
        grad_scores = weights * (grad_weights - row_scr[1:2, row_at])
        low_scores = grad_scores.astype(low)
        dv_scr[key_at, :] += nn(weights.astype(low), grads)
        dk_scr[key_at, :] += nn(low_scores, queries)
        dqt_scr[:, row_at] += nn(kt_scr[:, key_at], low_scores)
        return grad_scores

    point = 0
    if not causal:
        at_step(head, stages, 0, 1)
        for start in range(0, keys, key_block):
            for at in range(0, rows, block):
                piece(slice(start, start + key_block), slice(at, at + block))
    else:
        for start in range(0, keys, block):
            at_step(head, stages, point, BACKWARD_POINTS)
            point += 1
            for here in range(start, start + block, LANES):
                grad = piece(slice(here, here + LANES), slice(here, start + block), add_near)
                near = min(2 * LANES, grad.shape[1])
                near_scr[:, :near] += grad[:, :near]
            for at in range(start + block, rows, block):
                at_step(head, stages, point, BACKWARD_POINTS)
                point += 1
                beside = at == start + block
                grad = piece(slice(start, start + block), slice(at, at + block), add_corner if beside else None)
                if beside:
                    near_scr[:, LANES:] += grad[-LANES:, :LANES]
        flip = lax.broadcasted_iota(jnp.int32, (LANES, LANES), 0) + lax.broadcasted_iota(jnp.int32, (LANES, LANES), 1)
        flip = (flip == LANES - 1).astype(jnp.float32)
        turned = lax.dot_general(
            flip, near_scr[...], (((1,), (0,)), ((), ())), precision=highest, preferred_element_type=jnp.float32
        )
        turned = pltpu.roll(turned, 1, 1, stride=1, stride_axis=0)
        sums = jnp.sum(turned[:, LANES:], axis=0, keepdims=True)
        at_row = lax.broadcasted_iota(jnp.int32, (8, LANES), 0) == head
        before = jnp.where(head == 0, 0.0, distance_ref[...])
        distance_ref[...] = jnp.where(at_row, jnp.broadcast_to(sums, (8, LANES)), before)

    @pl.when(last)
    def _():
        for at in range(0, rows, block):
            dq_ref[at : at + block, :] = dqt_scr[:, at : at + block].T.astype(low)
        dk_ref[...] = dk_scr[...].astype(low)
        dv_ref[...] = dv_scr[...].astype(low)

    at_end(head, heads, stages)


def attend_backward(queries, keys, values, grad_mixed, mixed, logsum, heads, padded=0, bias=None, length=None, plan=None, extra=()):
    causal = bias is not None
    rows, width, count, row_spec, key_spec, key_specs = attend_specs(queries, keys, padded)
    in_specs = [row_spec, *key_specs, row_spec, row_spec, pl.BlockSpec((1, 8, rows), lambda h: (h, 0, 0))]
    args = [queries, keys, values, grad_mixed, mixed, logsum]
    out_specs = [row_spec, key_spec, key_spec]
    out_shape = [jax.ShapeDtypeStruct((n, width), low) for n in (rows, count, count)]
    scratch = [
        pltpu.VMEM((LANES, count), low), pltpu.VMEM((LANES, rows), jnp.float32),
        pltpu.VMEM((count, LANES), jnp.float32), pltpu.VMEM((count, LANES), jnp.float32), pltpu.VMEM((8, rows), jnp.float32),
    ]
    if causal:
        in_specs = [pl.BlockSpec(memory_space=pltpu.SMEM), *in_specs, pl.BlockSpec((1, 1, 3 * LANES), lambda h: (h, 0, 0))]
        args = [length, *args, bias]
        out_specs += [pl.BlockSpec((8, LANES), lambda h: (0, 0))]
        out_shape += [jax.ShapeDtypeStruct((8, LANES), jnp.float32)]
        scratch += [pltpu.VMEM((LANES, 2 * LANES), jnp.float32), pltpu.VMEM((LANES, 2 * LANES), jnp.float32)]
    return pl.pallas_call(
        functools.partial(attend_backward_kernel, causal=causal, heads=heads, plan=plan),
        grid=(heads,),
        in_specs=in_specs + (plan.in_specs() if plan else []),
        out_specs=out_specs + (plan.out_specs() if plan else []),
        out_shape=out_shape + (plan.out_shape() if plan else []),
        scratch_shapes=scratch + (plan.scratch() if plan else []),
        compiler_params=plan.params() if plan else pltpu.CompilerParams(vmem_limit_bytes=62 * 2**20),
        cost_estimate=pl.CostEstimate(
            flops=10 * heads * LANES * rows * count // (2 if causal else 1),
            bytes_accessed=8 * (rows + count) * width,
            transcendentals=heads * rows * count // (2 if causal else 1),
        ),
        name="self_backward" if causal else "cross_backward",
    )(*args, *extra)


def scale_of(values):
    return lax.rsqrt(jnp.mean(values * values, axis=-1, keepdims=True) + epsilon)


def project_kernel(gain_lane, x_ref, w_ref, qkv_ref, normed_ref, gains_ref):
    @pl.when(pl.program_id(0) == 0)
    def _():
        tile = gain_lane // LANES * LANES
        turned = w_ref[:, tile : tile + LANES].astype(jnp.float32).T
        first = gain_lane - tile
        gains_ref[...] = turned[first : first + 8]

    values = x_ref[...].astype(jnp.float32)
    normed = (values * scale_of(values) * gains_ref[0:1, :]).astype(low)
    normed_ref[...] = normed
    qkv_ref[...] = nn(normed, w_ref[...]).astype(low)


def project(everyone, w_qkv, gain_lane):
    count, width = everyone.shape
    wide = w_qkv.shape[1]
    block = min(BLOCK, count)
    rows = lambda n: pl.BlockSpec((block, n), lambda i: (i, 0))
    return pl.pallas_call(
        functools.partial(project_kernel, gain_lane),
        grid=(count // block,),
        in_specs=[rows(width), pl.BlockSpec((width, wide), lambda i: (0, 0))],
        out_specs=[rows(wide), rows(width), pl.BlockSpec((8, width), lambda i: (0, 0))],
        out_shape=[
            jax.ShapeDtypeStruct((count, wide), low), jax.ShapeDtypeStruct((count, width), low),
            jax.ShapeDtypeStruct((8, width), jnp.float32),
        ],
        compiler_params=pltpu.CompilerParams(vmem_limit_bytes=62 * 2**20),
        name="project",
    )(everyone, w_qkv)


def unproject_kernel(x_ref, normed_ref, w_ref, dq_ref, dk_ref, dv_ref, part_ref, own_ref, gain_ref, own_scr):
    step = pl.program_id(0)
    padded = dq_ref.shape[1]
    grads = [r[...] for r in (dq_ref, dk_ref, dv_ref)]
    part = sum(nt(g, w_ref[:, n * padded : (n + 1) * padded]) for n, g in enumerate(grads))
    values = x_ref[...].astype(jnp.float32)
    share = jnp.sum(part * (values * scale_of(values)), axis=0, keepdims=True)
    part_ref[...] = part.astype(low)
    turned = normed_ref[...].T

    @pl.when(step == 0)
    def _():
        gain_ref[...] = jnp.zeros_like(gain_ref)
        own_scr[...] = jnp.zeros_like(own_scr)

    gain_ref[...] += jnp.broadcast_to(share, gain_ref.shape)
    for n, g in enumerate(grads):
        own_scr[:, n * padded : (n + 1) * padded] += nn(turned, g)

    @pl.when(step == pl.num_programs(0) - 1)
    def _():
        own_ref[...] = own_scr[...].astype(low)


def unproject(everyone, normed, w_qkv, dq, dk, dv):
    count, width = everyone.shape
    wide, padded = w_qkv.shape[1], dq.shape[1]
    block = min(BLOCK, count)
    rows = lambda n: pl.BlockSpec((block, n), lambda i: (i, 0))
    fixed = lambda a, b: pl.BlockSpec((a, b), lambda i: (0, 0))
    return pl.pallas_call(
        unproject_kernel,
        grid=(count // block,),
        in_specs=[rows(width), rows(width), fixed(width, wide), rows(padded), rows(padded), rows(padded)],
        out_specs=[rows(width), fixed(width, wide), fixed(8, width)],
        out_shape=[
            jax.ShapeDtypeStruct((count, width), low), jax.ShapeDtypeStruct((width, wide), low),
            jax.ShapeDtypeStruct((8, width), jnp.float32),
        ],
        scratch_shapes=[pltpu.VMEM((width, wide), jnp.float32)],
        compiler_params=pltpu.CompilerParams(vmem_limit_bytes=62 * 2**20),
        name="unproject",
    )(everyone, normed, w_qkv, dq, dk, dv)


slope = float(np.sqrt(2.0 / np.pi))
cubic = 0.044715


def middle_kernel(
    slabs, scalars, x1_ref, mixed_ref, co_ref, gains_ref, cot_ref, gate_ref, up_ref, *refs
):
    slab_refs, refs = refs[:slabs], refs[slabs:]
    out_ref, dx_ref, dm_ref, co_grad_ref, gain_ref, packed = refs[:6]
    x2_scr, n3_scr, n3t_scr, df_scr, result_scr, dn_scr, down_ref, gate_buf, up_buf, down_buf, sem = refs[6:]
    step, steps = pl.program_id(0), pl.num_programs(0)
    rows, width = x1_ref.shape
    block = gate_ref.shape[1]
    world, share = packed.shape[:2]
    inner = block * steps
    owners = down_buf.shape[1]
    hidden_share = block // owners

    @pl.when(step == 0)
    def _():
        x2 = x1_ref[...] + nn(mixed_ref[...], co_ref[...])
        x2_scr[...] = x2
        normed = (x2 * scale_of(x2) * gains_ref[2:3, :]).astype(low)
        n3_scr[...] = normed
        n3t_scr[...] = normed.T
        place = scalars[1] + lax.broadcasted_iota(jnp.int32, (rows, 1), 0)
        df_scr[...] = jnp.where(place < scalars[0], cot_ref[...], 0)
        result_scr[...] = x2
        dn_scr[...] = jnp.zeros_like(dn_scr)
        down_buf[...] = jnp.zeros_like(down_buf)

    for o in range(owners):
        for k in range(slabs):
            size = min(share, hidden_share - k * share)
            start = o * hidden_share + k * share
            down_ref[start : start + size] = slab_refs[k][o, :size]

    normed, df = n3_scr[...], df_scr[...]
    gate, upper = nn(normed, gate_ref[...]), nn(normed, up_ref[...])
    bent = jnp.tanh(slope * (gate + cubic * (gate * gate * gate)))
    half = 0.5 * (1.0 + bent)
    active = gate * half
    hidden = (active * upper).astype(low)
    result_scr[...] += nn(hidden, down_ref[...])
    grad_hidden = nt(df, down_ref[...])
    rise = half + (0.5 * gate) * ((1.0 - bent * bent) * (slope + (3.0 * cubic * slope) * (gate * gate)))
    grad_gate = (grad_hidden * upper * rise).astype(low)
    grad_upper = (grad_hidden * active).astype(low)
    dn_scr[...] += nt(grad_gate, gate_ref[...]) + nt(grad_upper, up_ref[...])
    slot = lax.rem(step, 2)

    def sends(at, which):
        first = pl.multiple_of(at * block, LANES)
        yield pltpu.make_async_copy(gate_buf.at[which], packed.at[:, :, pl.ds(first, block)], sem.at[which, 0])
        yield pltpu.make_async_copy(up_buf.at[which], packed.at[:, :, pl.ds(pl.multiple_of(inner + at * block, LANES), block)], sem.at[which, 1])
        for k in range(slabs):
            column = 2 * inner + k * width
            yield pltpu.make_async_copy(
                down_buf.at[which, :, k], packed.at[pl.ds(at * owners, owners), :, column : column + width], sem.at[which, 2 + k]
            )

    @pl.when(step >= 2)
    def _():
        for copy in sends(step - 2, slot):
            copy.wait()

    turned = n3t_scr[...]
    gate_buf[slot] = nn(turned, grad_gate).reshape(world, share, block).astype(low)
    up_buf[slot] = nn(turned, grad_upper).reshape(world, share, block).astype(low)
    grad_down = tn(hidden, df)
    for o in range(owners):
        for k in range(slabs):
            size = min(share, hidden_share - k * share)
            start = o * hidden_share + k * share
            down_buf[slot, o, k, :size] = grad_down[start : start + size].astype(low)
    for copy in sends(step, slot):
        copy.start()

    @pl.when(step == steps - 1)
    def _():
        out_ref[...] = result_scr[...].astype(low)
        x2, grad_normed = x2_scr[...], dn_scr[...]
        scale = scale_of(x2)
        unit = x2 * scale
        grad_unit = grad_normed * gains_ref[2:3, :]
        gain_ref[...] = jnp.broadcast_to(jnp.sum(grad_normed * unit, axis=0, keepdims=True), gain_ref.shape)
        back = scale * (grad_unit - unit * jnp.mean(grad_unit * unit, axis=-1, keepdims=True))
        dx = df.astype(jnp.float32) + back
        dx_ref[...] = dx
        branch = dx.astype(low)
        dm_ref[...] = nt(branch, co_ref[...]).astype(low)
        co_grad_ref[...] = tn(mixed_ref[...], branch).astype(low)
        if steps > 1:
            for copy in sends(step - 1, 1 - slot):
                copy.wait()
        for copy in sends(step, slot):
            copy.wait()


def middle(scalars, x1, mixed, gains, cotangent, weights, inner, world):
    rows, width = x1.shape
    block = min(BLOCK, inner)
    steps = inner // block
    share, hidden_share = width // world, inner // world
    slabs = -(-hidden_share // share)
    owners = block // hidden_share
    ahead = (1 + slabs) * width // block
    fixed = lambda *shape: pl.BlockSpec(shape, lambda j: (0,) * len(shape))
    f32 = jnp.float32
    return pl.pallas_call(
        functools.partial(middle_kernel, slabs),
        grid=(steps,),
        in_specs=[
            pl.BlockSpec(memory_space=pltpu.SMEM), fixed(rows, width), fixed(rows, width), fixed(width, width),
            fixed(8, width), fixed(rows, width),
            pl.BlockSpec((width, block), lambda j: (0, ahead + j)), pl.BlockSpec((width, block), lambda j: (0, ahead + steps + j)),
            *[pl.BlockSpec((owners, share, width), lambda j, k=k: (j, 0, 1 + k)) for k in range(slabs)],
        ],
        out_specs=[
            fixed(rows, width), fixed(rows, width), fixed(rows, width), fixed(width, width), fixed(8, width),
            pl.BlockSpec(memory_space=pl.ANY),
        ],
        out_shape=[
            jax.ShapeDtypeStruct((rows, width), low), jax.ShapeDtypeStruct((rows, width), f32),
            jax.ShapeDtypeStruct((rows, width), low), jax.ShapeDtypeStruct((width, width), low),
            jax.ShapeDtypeStruct((8, width), f32),
            jax.ShapeDtypeStruct((world, share, 2 * inner + slabs * width), low),
        ],
        scratch_shapes=[
            pltpu.VMEM((rows, width), f32), pltpu.VMEM((rows, width), low), pltpu.VMEM((width, rows), low),
            pltpu.VMEM((rows, width), low), pltpu.VMEM((rows, width), f32), pltpu.VMEM((rows, width), f32),
            pltpu.VMEM((block, width), low),
            pltpu.VMEM((2, world, share, block), low), pltpu.VMEM((2, world, share, block), low),
            pltpu.VMEM((2, owners, slabs, share, width), low), pltpu.SemaphoreType.DMA((2, 2 + slabs)),
        ],
        compiler_params=pltpu.CompilerParams(vmem_limit_bytes=62 * 2**20),
        cost_estimate=pl.CostEstimate(
            flops=2 * rows * width * (9 * inner + 3 * width), transcendentals=rows * inner, bytes_accessed=26 * width * inner // 4
        ),
        name="middle",
    )(scalars, x1, mixed, weights, gains, cotangent, weights, weights, *[weights.reshape(world, share, -1)] * slabs)


def encode_kernel(enc_ref, w_ref, key_ref, value_ref):
    for n, out in enumerate((key_ref, value_ref)):
        out[...] = nn(enc_ref[...], w_ref[n]).astype(low)


def encode(encoded, squares):
    count, width = encoded.shape
    part = width // 3
    columns = pl.BlockSpec((count, part), lambda j: (0, j))
    return pl.pallas_call(
        encode_kernel,
        grid=(3,),
        in_specs=[pl.BlockSpec((count, width), lambda j: (0, 0)), pl.BlockSpec((2, width, part), lambda j: (1, 0, j))],
        out_specs=[columns] * 2,
        out_shape=[jax.ShapeDtypeStruct((count, width), low)] * 2,
        compiler_params=pltpu.CompilerParams(vmem_limit_bytes=62 * 2**20),
        cost_estimate=pl.CostEstimate(flops=4 * count * width * width, transcendentals=0, bytes_accessed=8 * width * width),
        name="encode",
    )(encoded, squares)


def enter_kernel(group_width, x_ref, mixed_ref, w_ref, gains_ref, attended_ref, normed_ref, query_ref):
    total = x_ref[...].astype(jnp.float32)
    for s in range(mixed_ref.shape[0]):
        total += nn(mixed_ref[s, :, :group_width], w_ref[0, s * group_width : (s + 1) * group_width])
    attended_ref[...] = total
    normed = (total * scale_of(total) * gains_ref[1:2, :]).astype(low)
    normed_ref[...] = normed
    query_ref[...] = nn(normed, w_ref[1]).astype(low)


def enter(tokens, mixed, squares, gains, group_width):
    rows, width = tokens.shape
    seq, _, padded = mixed.shape
    block = min(256, rows)
    by_rows = pl.BlockSpec((block, width), lambda i: (i, 0))
    return pl.pallas_call(
        functools.partial(enter_kernel, group_width),
        grid=(rows // block,),
        in_specs=[
            by_rows, pl.BlockSpec((seq, block, padded), lambda i: (0, i, 0)), pl.BlockSpec((2, width, width), lambda i: (0, 0, 0)),
            pl.BlockSpec((8, width), lambda i: (0, 0)),
        ],
        out_specs=[by_rows] * 3,
        out_shape=[jax.ShapeDtypeStruct((rows, width), t) for t in (jnp.float32, low, low)],
        compiler_params=pltpu.CompilerParams(vmem_limit_bytes=62 * 2**20),
        cost_estimate=pl.CostEstimate(flops=4 * rows * width * width, transcendentals=0, bytes_accessed=12 * width * width),
        name="enter",
    )(tokens, mixed, squares, gains)


def leave_kernel(group_width, grad_ref, w_ref, attended_ref, gains_ref, dx_ref, total_ref, branch_ref, dm_ref, gain_ref):
    @pl.when(pl.program_id(0) == 0)
    def _():
        gain_ref[...] = jnp.zeros_like(gain_ref)

    grad_normed = nt(grad_ref[...], w_ref[1])
    values = attended_ref[...]
    scale = scale_of(values)
    unit = values * scale
    grad_unit = grad_normed * gains_ref[1:2, :]
    gain_ref[...] += jnp.broadcast_to(jnp.sum(grad_normed * unit, axis=0, keepdims=True), gain_ref.shape)
    total = dx_ref[...] + scale * (grad_unit - unit * jnp.mean(grad_unit * unit, axis=-1, keepdims=True))
    total_ref[...] = total
    branch = total.astype(low)
    branch_ref[...] = branch
    for s in range(dm_ref.shape[0]):
        dm_ref[s, :, :group_width] = nt(branch, w_ref[0, s * group_width : (s + 1) * group_width]).astype(low)
        if dm_ref.shape[2] > group_width:
            dm_ref[s, :, group_width:] = jnp.zeros((branch.shape[0], dm_ref.shape[2] - group_width), low)


def leave(grad_queries, squares, attended, gains, grad_crossed, seq, group_width, padded):
    rows, width = grad_queries.shape
    block = min(256, rows)
    by_rows = pl.BlockSpec((block, width), lambda i: (i, 0))
    fixed = pl.BlockSpec((8, width), lambda i: (0, 0))
    return pl.pallas_call(
        functools.partial(leave_kernel, group_width),
        grid=(rows // block,),
        in_specs=[by_rows, pl.BlockSpec((2, width, width), lambda i: (0, 0, 0)), by_rows, fixed, by_rows],
        out_specs=[by_rows, by_rows, pl.BlockSpec((seq, block, padded), lambda i: (0, i, 0)), fixed],
        out_shape=[
            jax.ShapeDtypeStruct((rows, width), jnp.float32), jax.ShapeDtypeStruct((rows, width), low),
            jax.ShapeDtypeStruct((seq, rows, padded), low), jax.ShapeDtypeStruct((8, width), jnp.float32),
        ],
        compiler_params=pltpu.CompilerParams(vmem_limit_bytes=62 * 2**20),
        cost_estimate=pl.CostEstimate(flops=4 * rows * width * width, transcendentals=0, bytes_accessed=16 * width * width),
        name="leave",
    )(grad_queries, squares, attended, gains, grad_crossed)


def square_terms_kernel(group_width, normed, grad_q, encoded, grad_k, grad_v, w_ref, mixed, branch, q_out, k_out, v_out, o_out, e_out, *scratch):
    normed_t, encoded_t, mixed_t, total = scratch
    step = pl.program_id(0)

    @pl.when(step == 0)
    def _():
        normed_t[...] = normed[...].T
        encoded_t[...] = encoded[...].T
        for s in range(mixed.shape[0]):
            mixed_t[s * group_width : (s + 1) * group_width] = mixed[s].T[:group_width]
        total[...] = jnp.zeros_like(total)

    q_out[...] = nn(normed_t[...], grad_q[...]).astype(low)
    k_out[...] = nn(encoded_t[...], grad_k[...]).astype(low)
    v_out[...] = nn(encoded_t[...], grad_v[...]).astype(low)
    o_out[...] = nn(mixed_t[...], branch[...]).astype(low)
    total[...] += nt(grad_k[...], w_ref[0]) + nt(grad_v[...], w_ref[1])

    @pl.when(step == pl.num_programs(0) - 1)
    def _():
        e_out[...] = total[...].astype(low)


def square_terms(normed, grad_q, encoded, grad_k, grad_v, squares, mixed, branch, group_width):
    rows, width = normed.shape
    count = encoded.shape[0]
    part = width // 3
    fixed = lambda v: pl.BlockSpec(v.shape, lambda j: (0,) * v.ndim)
    columns = lambda n: pl.BlockSpec((n, part), lambda j: (0, j))
    return pl.pallas_call(
        functools.partial(square_terms_kernel, group_width),
        grid=(3,),
        in_specs=[
            fixed(normed), columns(rows), fixed(encoded), columns(count), columns(count),
            pl.BlockSpec((2, width, part), lambda j: (1, 0, j)), fixed(mixed), columns(rows),
        ],
        out_specs=[columns(width)] * 4 + [fixed(encoded)],
        out_shape=[jax.ShapeDtypeStruct((width, width), low)] * 4 + [jax.ShapeDtypeStruct((count, width), low)],
        scratch_shapes=[
            pltpu.VMEM((width, rows), low), pltpu.VMEM((width, count), low), pltpu.VMEM((width, rows), low),
            pltpu.VMEM((count, width), jnp.float32),
        ],
        compiler_params=pltpu.CompilerParams(vmem_limit_bytes=62 * 2**20),
        cost_estimate=pl.CostEstimate(flops=12 * rows * width * width, transcendentals=0, bytes_accessed=24 * width * width),
        name="square_terms",
    )(normed, grad_q, encoded, grad_k, grad_v, squares, mixed, branch)


def coordinates():
    place, slot = lax.axis_index("seq"), lax.axis_index("fsdp")
    return place // 2, lax.rem(place, 2), slot // 2, lax.rem(slot, 2)


def device(x, c, z, y):
    return (x * 2 + c, z * 2 + y)


class Near:
    def __init__(self, nz):
        self.nz = nz
        x, c, z, y = self.x, self.c, self.z, self.y = coordinates()
        self.by_x, self.by_core, self.by_y = device(1 - x, c, z, y), device(x, 1 - c, z, y), device(x, c, z, 1 - y)
        self.diagonal = device(1 - x, 1 - c, z, y)
        self.steps = [lax.rem(z + t, nz) for t in range(nz)]
        self.backs = [lax.rem(z - t + nz, nz) for t in range(nz)]
        self.by_z = [device(x, c, self.steps[t], y) for t in range(nz)]


def greet(others):
    barrier = pltpu.get_barrier_semaphore()
    for other in others:
        pl.semaphore_signal(barrier, inc=1, device_id=other, device_id_type=MESH)
    pl.semaphore_wait(barrier, len(others))


class Copies:
    def __init__(self, send_sem, recv_sem):
        self.send_sem, self.recv_sem, self.made = send_sem, recv_sem, []

    def add(self, source, target, other):
        self.made.append((source, target, other))
        return len(self.made) - 1

    def copy(self, number):
        source, target, other = self.made[number]
        return pltpu.make_async_remote_copy(
            src_ref=source(), dst_ref=target(), send_sem=self.send_sem.at[number], recv_sem=self.recv_sem.at[number],
            device_id=other, device_id_type=MESH,
        )

    def start(self, *numbers):
        for number in numbers:
            self.copy(number).start()

    def arrive(self, *numbers):
        for number in numbers:
            self.copy(number).wait_recv()

    def finish(self):
        for number in range(len(self.made)):
            self.copy(number).wait_send()


def add_low(target, left, right):
    count = left.shape[0]
    unroll = 4 if count % 4 == 0 else 1

    @pl.loop(0, count // unroll)
    def _(n):
        for k in range(unroll):
            at = n * unroll + k
            if target.dtype == low:
                target[at] = left[at] + right[at]
            else:
                target[at] = left[at].astype(target.dtype) + right[at].astype(target.dtype)


def whole(space=pltpu.VMEM):
    return pl.BlockSpec(memory_space=space)


class GatherPlan:
    inputs, outputs = 1, 1

    def __init__(self, nz, count, share, width):
        self.nz, self.count, self.share, self.width = nz, count, share, width
        self.total = 8 * nz - 1

    def in_specs(self):
        return [whole()]

    def out_specs(self):
        return [whole(pl.ANY)]

    def out_shape(self):
        return [jax.ShapeDtypeStruct((self.count, 2, 2, self.nz, 2, self.share, self.width), low)]

    def scratch(self):
        return [pltpu.SemaphoreType.DMA((self.total,)), pltpu.SemaphoreType.DMA((self.total,)), pltpu.SemaphoreType.DMA((1,))]

    def params(self):
        return pltpu.CompilerParams(collective_id=2, has_side_effects=True, vmem_limit_bytes=62 * 2**20)

    def stages(self, given, made, scratch):
        (src,), (out,), (send_sem, recv_sem, local_sem) = given, made, scratch
        nz, my = self.nz, Near(self.nz)
        x, c, z, y, backs = my.x, my.c, my.z, my.y, my.backs
        copies = Copies(send_sem, recv_sem)
        own = lambda: src
        at = lambda xx, cc, zz, yy: lambda: out.at[:, xx, cc, zz, yy]
        mine = at(x, c, z, y)
        by_z = [None] + [copies.add(own, mine, my.by_z[t]) for t in range(1, nz)]
        held = [mine if t == 0 else at(x, c, backs[t], y) for t in range(nz)]
        source = [own if t == 0 else held[t] for t in range(nz)]
        by_y = [copies.add(source[t], held[t], my.by_y) for t in range(nz)]
        by_x = [copies.add(source[t], held[t], my.by_x) for t in range(nz)]
        by_core = [copies.add(source[t], held[t], my.by_core) for t in range(nz)]
        from_x = [at(1 - x, c, backs[t], y) for t in range(nz)]
        from_y = [at(x, c, backs[t], 1 - y) for t in range(nz)]
        far = [at(1 - x, c, backs[t], 1 - y) for t in range(nz)]
        corner = [
            copies.add(from_x[t], from_x[t], my.by_y) if t % 2 == 0 else copies.add(from_y[t], from_y[t], my.by_x)
            for t in range(nz)
        ]
        core_x = [copies.add(from_x[t], from_x[t], my.by_core) for t in range(nz)]
        core_y = [copies.add(from_y[t], from_y[t], my.by_core) for t in range(nz)]
        core_far = [copies.add(far[t], far[t], my.by_core) for t in range(nz)]
        local = lambda: pltpu.make_async_copy(src, mine(), local_sem.at[0])

        def begin():
            greet([my.by_x, my.by_core, my.by_y, *my.by_z[1:]])
            copies.start(*by_z[1:], by_y[0], by_x[0], by_core[0])
            local().start()

        def line(t):
            copies.arrive(by_z[t])
            copies.start(by_y[t], by_x[t], by_core[t])

        def plane(t):
            copies.arrive(by_x[t])
            copies.start(*([corner[t]] if t % 2 == 0 else []), core_x[t])
            copies.arrive(by_y[t])
            copies.start(*([corner[t]] if t % 2 == 1 else []), core_y[t])

        def turn(t):
            copies.arrive(corner[t])
            copies.start(core_far[t])

        def end():
            local().wait()
            copies.arrive(*by_core, *core_x, *core_y, *core_far)
            copies.finish()

        work = [functools.partial(line, t) for t in range(1, nz)]
        work += [functools.partial(plane, t) for t in range(nz)] + [functools.partial(turn, t) for t in range(nz)]
        points = 3 * FORWARD_POINTS - 1
        stages = [(0, begin)]
        for number, stage in enumerate(work):
            stages.append((1 + number * points // (len(work) + 1), stage))
        return stages + [(-1, end)]


class ReducePlan:
    def __init__(self, nz, count, share, width, number, points, slabs=None):
        self.nz, self.count, self.share, self.width, self.slabs = nz, count, share, width, slabs
        self.number, self.points = number, points
        self.inputs = count + (slabs is not None)
        self.outputs = 1 + (slabs is not None)
        self.total = count * (nz + 1) + count + 2 * (slabs is not None)

    def in_specs(self):
        return [whole()] * self.inputs

    def out_specs(self):
        return [whole()] * self.outputs

    def out_shape(self):
        shapes = [jax.ShapeDtypeStruct((self.count, self.share, self.width), jnp.float32)]
        return shapes + ([jax.ShapeDtypeStruct(self.slabs, jnp.float32)] if self.slabs else [])

    def scratch(self):
        nz, tail = self.nz, (self.share, self.width)
        vmem = lambda *shape: pltpu.VMEM((self.count, *shape, *tail), low)
        slabs = [pltpu.VMEM((*lead, *self.slabs), low) for lead in ((2,), (2,), ())] if self.slabs else []
        sems = [pltpu.SemaphoreType.DMA((self.total,)), pltpu.SemaphoreType.DMA((self.total,))]
        return [vmem(2, 2, nz), vmem(2, nz, 2), vmem(2, nz), vmem(2, nz), vmem(nz), vmem(nz), vmem(nz - 1), *slabs, *sems]

    def params(self):
        return pltpu.CompilerParams(collective_id=self.number, has_side_effects=True, vmem_limit_bytes=62 * 2**20)

    def stages(self, given, made, scratch):
        squares, out, beside = given[: self.count], made[0], self.slabs is not None
        a, ra, b, rb, d, rd, re = scratch[:7]
        send_sem, recv_sem = scratch[-2:]
        if beside:
            enc, out_enc, (enc_r, enc_a, enc_rx) = given[-1], made[1], scratch[7:10]
        nz, my, count = self.nz, Near(self.nz), self.count
        x, c, z, y = my.x, my.c, my.z, my.y
        copies = Copies(send_sem, recv_sem)
        if beside:
            enc_core = copies.add(lambda: enc.at[:, 1 - c], lambda: enc_r, my.by_core)
            enc_x = copies.add(lambda: enc_a.at[1 - x], lambda: enc_rx, my.by_x)
        core = [copies.add(lambda n=n: squares[n].at[:, 1 - c], lambda n=n: ra.at[n], my.by_core) for n in range(count)]
        one, two, three = [], [], []
        for n in range(count):
            y_first = n % 2 == 0
            if y_first:
                one.append(copies.add(lambda n=n: a.at[n, :, 1 - y], lambda n=n: rb.at[n], my.by_y))
                two.append(copies.add(lambda n=n: b.at[n, 1 - x], lambda n=n: rd.at[n], my.by_x))
            else:
                one.append(copies.add(lambda n=n: a.at[n, 1 - x], lambda n=n: rb.at[n], my.by_x))
                two.append(copies.add(lambda n=n: b.at[n, 1 - y], lambda n=n: rd.at[n], my.by_y))
            three.append([
                copies.add(lambda n=n, t=t: d.at[n, my.steps[t]], lambda n=n, t=t: re.at[n, t - 1], my.by_z[t])
                for t in range(1, nz)
            ])

        def begin():
            greet([my.by_x, my.by_core, my.by_y, *my.by_z[1:]])
            copies.start(*core, *([enc_core] if beside else []))

        def after_core(n):
            copies.arrive(core[n])
            for half in range(2):
                for side in range(2):
                    add_low(a.at[n, half, side], squares[n].at[half, c, :, side], ra.at[n, half, :, side])
            copies.start(one[n])

        def after_one(n):
            copies.arrive(one[n])
            for side in range(2):
                if n % 2 == 0:
                    add_low(b.at[n, side], a.at[n, side, y], rb.at[n, side])
                else:
                    add_low(b.at[n, side], a.at[n, x, side], rb.at[n, side])
            copies.start(two[n])

        def after_two(n):
            copies.arrive(two[n])
            add_low(d.at[n], b.at[n, x if n % 2 == 0 else y], rd.at[n])
            copies.start(*three[n])

        def after_three(n):
            copies.arrive(*three[n])
            total = d[n, z].astype(jnp.float32)
            for t in range(nz - 1):
                total += re[n, t].astype(jnp.float32)
            out[n] = total

        def encoder():
            copies.arrive(enc_core)
            for half in range(2):
                add_low(enc_a.at[half], enc.at[half, c], enc_r.at[half])
            copies.start(enc_x)

        def end():
            if beside:
                copies.arrive(enc_x)
                add_low(out_enc, enc_a.at[x], enc_rx)
            for n in range(count):
                after_three(n)
            copies.finish()

        part = functools.partial
        work = [part(after_core, n) for n in range(count)] + ([encoder] if beside else [])
        work += [part(after_one, n) for n in range(count)] + [part(after_two, n) for n in range(count)]
        first, last = self.points // 12, self.points - 1 - self.points // 12
        stages = [(0, begin)]
        for number, stage in enumerate(work):
            stages.append((first + number * (last - first) // max(len(work) - 1, 1), stage))
        return stages + [(-1, end)]


def gather_kernel(nz, tok, enc, own, everyone, encoded, qkv_out, send_sem, recv_sem, local_sem):
    my = Near(nz)
    x, c, z, y, backs = my.x, my.c, my.z, my.y, my.backs
    greet([my.by_x, my.by_core, my.diagonal, my.by_y, *my.by_z[1:]])
    copies = Copies(send_sem, recv_sem)
    local = [
        pltpu.make_async_copy(source, target, local_sem.at[n])
        for n, (source, target) in enumerate(
            [(own.at[x, c], qkv_out.at[x, c, z, y]), (tok, everyone.at[x, c]), (enc, encoded.at[x, c])]
        )
    ]
    for copy in local:
        copy.start()
    mine = lambda: qkv_out.at[x, c, z, y]
    first = [
        copies.add(lambda: own.at[1 - x, c], mine, my.by_x),
        copies.add(lambda: own.at[x, 1 - c], mine, my.by_core),
        copies.add(lambda: own.at[1 - x, 1 - c], mine, my.diagonal),
    ]
    rows = [(tok, everyone), (enc, encoded)]
    rows_x = [copies.add(lambda s=s: s, lambda t=t: t.at[x, c], my.by_x) for s, t in rows]
    rows_core = [copies.add(lambda s=s: s, lambda t=t: t.at[x, c], my.by_core) for s, t in rows]
    rows_far = [copies.add(lambda t=t: t.at[1 - x, c], lambda t=t: t.at[1 - x, c], my.by_core) for s, t in rows]
    line = [lambda t=t: qkv_out.at[:, :, backs[t], y] for t in range(nz)]
    by_z = [None] + [copies.add(line[0], line[0], my.by_z[t]) for t in range(1, nz)]
    by_y = [copies.add(line[t], line[t], my.by_y) for t in range(nz)]
    copies.start(*first, *rows_x, *rows_core)
    for copy in local:
        copy.wait()
    copies.arrive(*first)
    copies.start(*by_z[1:], by_y[0])
    for t in range(1, nz):
        copies.arrive(by_z[t])
        copies.start(by_y[t])
    for n in range(2):
        copies.arrive(rows_x[n])
        copies.start(rows_far[n])
    copies.arrive(*by_y, *rows_core, *rows_far)
    copies.finish()


def gather(nz, tok, enc, own):
    share, wide = own.shape[-2:]
    shapes = [
        jax.ShapeDtypeStruct((2, 2, *tok.shape), tok.dtype),
        jax.ShapeDtypeStruct((2, 2, *enc.shape), enc.dtype),
        jax.ShapeDtypeStruct((2, 2, nz, 2, share, wide), own.dtype),
    ]
    total = 9 + 2 * nz - 1
    return pl.pallas_call(
        functools.partial(gather_kernel, nz),
        in_specs=[whole()] * 3,
        out_specs=[whole(pl.ANY)] * 3,
        out_shape=shapes,
        scratch_shapes=[
            pltpu.SemaphoreType.DMA((total,)), pltpu.SemaphoreType.DMA((total,)), pltpu.SemaphoreType.DMA((3,)),
        ],
        compiler_params=pltpu.CompilerParams(collective_id=0, has_side_effects=True, vmem_limit_bytes=62 * 2**20),
        name="gather",
    )(tok, enc, own)


def reduce_kernel(nz, group_width, square, own, tok, gain, near, out_square, out_q, out_k, out_v, out_tok, out_gain, out_near, *refs):
    (a, ra, b, rb, d, rd, re, own_r, own_a, own_rz, own_f, own_in, tok_r, tok_a, tok_rx, gain_r, near_r,
     send_sem, recv_sem, gain_send, gain_recv) = refs
    my = Near(nz)
    x, c, z, y = my.x, my.c, my.z, my.y
    world, slots = 8 * nz, 2 * nz
    place, slot = lax.axis_index("seq"), lax.axis_index("fsdp")
    me = place * slots + slot
    barrier = pltpu.get_barrier_semaphore()

    @pl.loop(1, world)
    def _(t):
        other = lax.rem(me + t, world)
        pl.semaphore_signal(barrier, inc=1, device_id=(other // slots, lax.rem(other, slots)), device_id_type=MESH)

    pl.semaphore_wait(barrier, world - 1)
    copies = Copies(send_sem, recv_sem)
    add = copies.add
    half = tok.shape[2] // 2
    padded = own.shape[-1] // 3
    cut = lambda p: slice(p * half, (p + 1) * half)
    own_cut = lambda n: slice(n * padded, (n + 1) * padded)
    tok_core = [
        add(lambda h=h, p=p: tok.at[h, 1 - c, cut(p)], lambda h=h, p=p: tok_r.at[h, cut(p)], my.by_core)
        for h in (1 - x, x) for p in range(2)
    ]
    own_y = [
        add(lambda n=n: own.at[:, :, :, 1 - y, :, own_cut(n)], lambda n=n: own_r.at[n], my.by_y) for n in range(3)
    ]
    core = add(lambda: square.at[:, 1 - c], lambda: ra, my.by_core)
    near_all = [add(lambda: near, lambda t=t: near_r.at[t - 1], (place, lax.rem(slot + t, slots))) for t in range(1, slots)]
    tok_x = [add(lambda p=p: tok_a.at[1 - x, cut(p)], lambda p=p: tok_rx.at[cut(p)], my.by_x) for p in range(2)]
    one = add(lambda: a.at[:, 1 - y], lambda: rb, my.by_y)
    two = add(lambda: b.at[1 - x], lambda: rd, my.by_x)
    three = [add(lambda t=t: d.at[my.steps[t]], lambda t=t: re.at[t - 1], my.by_z[t]) for t in range(1, nz)]
    own_z = [
        [add(lambda n=n, t=t: own_a.at[n, :, :, my.steps[t]], lambda n=n, t=t: own_rz.at[n, t - 1], my.by_z[t]) for t in range(1, nz)]
        for n in range(3)
    ]
    landing = lambda: own_in.at[:, x, c]
    own_seq = [
        add(lambda: own_f.at[:, 1 - x, c], landing, my.by_x),
        add(lambda: own_f.at[:, x, 1 - c], landing, my.by_core),
        add(lambda: own_f.at[:, 1 - x, 1 - c], landing, my.diagonal),
    ]

    def gain_copy(t):
        other = lax.rem(me + t, world)
        return pltpu.make_async_remote_copy(
            src_ref=gain.at[other], dst_ref=gain_r.at[t - 1], send_sem=gain_send.at[t - 1], recv_sem=gain_recv.at[t - 1],
            device_id=(other // slots, lax.rem(other, slots)), device_id_type=MESH,
        )

    copies.start(own_y[0], *tok_core[:2], own_y[1], core, *tok_core[2:], own_y[2], *near_all)

    @pl.loop(1, world)
    def _(t):
        gain_copy(t).start()

    def tok_sum(h, p):
        add_low(tok_a.at[h, cut(p)], tok.at[h, c, cut(p)], tok_r.at[h, cut(p)])

    for p in range(2):
        copies.arrive(tok_core[p])
        tok_sum(1 - x, p)
        copies.start(tok_x[p])
    copies.arrive(core)
    for h in range(2):
        for side in range(2):
            add_low(a.at[h, side], square.at[h, c, :, side], ra.at[h, :, side])
    copies.start(one)

    def own_sum(n):
        copies.arrive(own_y[n])
        for h in range(2):
            for side in range(2):
                for k in range(nz):
                    own_a[n, h, side, k] = own[h, side, k, y, :, own_cut(n)] + own_r[n, h, side, k]
        copies.start(*own_z[n])

    own_sum(0)
    for p in range(2):
        copies.arrive(tok_core[2 + p])
        tok_sum(x, p)
    own_sum(1)
    own_sum(2)
    copies.arrive(one)
    for side in range(2):
        add_low(b.at[side], a.at[side, y], rb.at[side])
    copies.start(two)
    for n in range(3):
        copies.arrive(*own_z[n])
        for h in range(2):
            for side in range(2):
                total = own_a[n, h, side, z].astype(jnp.float32)
                for t in range(nz - 1):
                    total += own_rz[n, t, h, side].astype(jnp.float32)
                own_f[n, h, side] = total.astype(low)
    copies.start(*own_seq)
    own_in[:, x, c] = own_f[:, x, c]
    copies.arrive(two)
    add_low(d, b.at[x], rd)
    copies.start(*three)
    copies.arrive(*near_all)
    total = near[...]
    for t in range(slots - 1):
        total += near_r[t]
    out_near[...] = total
    out_gain[...] = gain[me]

    @pl.loop(1, world)
    def _(t):
        gain_copy(t).wait_recv()
        out_gain[...] += gain_r[t - 1]

    for p in range(2):
        copies.arrive(tok_x[p])
        add_low(out_tok.at[cut(p)], tok_a.at[x, cut(p)], tok_rx.at[cut(p)])
    copies.arrive(*own_seq)
    for n, out in enumerate((out_q, out_k, out_v)):
        parts = [own_in[n, s // 2, s % 2, :, :group_width].astype(jnp.float32) for s in range(4)]
        out[...] = jnp.concatenate(parts, axis=1)
    copies.arrive(*three)
    total = d[z].astype(jnp.float32)
    for t in range(nz - 1):
        total += re[t].astype(jnp.float32)
    out_square[...] = total
    copies.finish()

    @pl.loop(1, world)
    def _(t):
        gain_copy(t).wait_send()


def reduce(nz, group_width, square, own, tok, gain, near):
    share, width = square.shape[-2:]
    wide = own.shape[-1]
    vmem = lambda *shape: pltpu.VMEM(shape, low)
    slabs = tok.shape[2:]
    world = 8 * nz
    padded = wide // 3
    total = 4 + 3 + 1 + 2 * nz - 1 + 2 + 2 + nz - 1 + 3 * (nz - 1) + 3
    f32 = lambda *shape: jax.ShapeDtypeStruct(shape, jnp.float32)
    return pl.pallas_call(
        functools.partial(reduce_kernel, nz, group_width),
        in_specs=[whole()] * 5,
        out_specs=[whole()] * 7,
        out_shape=[f32(share, width)] * 4 + [f32(*slabs), f32(*gain.shape[1:]), f32(*near.shape)],
        scratch_shapes=[
            vmem(2, 2, nz, share, width), vmem(2, nz, 2, share, width), vmem(2, nz, share, width), vmem(2, nz, share, width),
            vmem(nz, share, width), vmem(nz, share, width), vmem(nz - 1, share, width),
            vmem(3, 2, 2, nz, share, padded), vmem(3, 2, 2, nz, share, padded), vmem(3, nz - 1, 2, 2, share, padded),
            vmem(3, 2, 2, share, padded), vmem(3, 2, 2, share, padded),
            vmem(2, *slabs), vmem(2, *slabs), vmem(*slabs),
            pltpu.VMEM((world - 1, *gain.shape[1:]), jnp.float32), pltpu.VMEM((2 * nz - 1, *near.shape), jnp.float32),
            pltpu.SemaphoreType.DMA((total,)), pltpu.SemaphoreType.DMA((total,)),
            pltpu.SemaphoreType.DMA((world - 1,)), pltpu.SemaphoreType.DMA((world - 1,)),
        ],
        compiler_params=pltpu.CompilerParams(collective_id=1, has_side_effects=True, vmem_limit_bytes=62 * 2**20),
        name="reduce",
    )(square, own, tok, gain, near)


def rms_norm(values, gain):
    scale = lax.rsqrt(jnp.mean(values * values, axis=-1, keepdims=True) + epsilon)
    return values * scale * gain


def rms_back(values, gain, grad_normed):
    scale = lax.rsqrt(jnp.mean(values * values, axis=-1, keepdims=True) + epsilon)
    unit = values * scale
    grad_unit = grad_normed * gain
    grad_gain = jnp.sum(grad_normed * unit, axis=0)
    grad_values = scale * (grad_unit - unit * jnp.mean(grad_unit * unit, axis=-1, keepdims=True))
    return (grad_values, grad_gain)


def activate(gate, upper):
    return jax.nn.gelu(gate, approximate=True) * upper


def per_device(
    tokens, encoder, cotangent, lengths, gains, self_query, self_key, self_value, self_output,
    cross_query, cross_key, cross_value, cross_output, ffn_gate, ffn_up, ffn_down, rel_bias,
):
    both = ("seq", "fsdp")
    seq, fsdp = lax.axis_size("seq"), lax.axis_size("fsdp")
    world = seq * fsdp
    nz = fsdp // 2
    share, width = self_query.shape
    hidden_share = ffn_down.shape[0]
    inner = ffn_gate.shape[1]
    rows = tokens.shape[1]
    group = rel_bias.shape[1]
    group_width = group * HEAD
    padded = -(-group_width // LANES) * LANES
    spare = padded - group_width
    heads = width // HEAD
    place = lax.axis_index("seq")
    aligned = share % 8 == 0

    slabs = -(-hidden_share // share)
    squares = jnp.stack([w.astype(low) for w in (self_output, cross_query, cross_key, cross_value)])
    if aligned:
        down = jnp.pad(ffn_down.astype(low), ((0, slabs * share - hidden_share), (0, 0))).reshape(slabs, share, width)
        wide_share = [cross_output.astype(low), *[down[k] for k in range(slabs)], ffn_gate.astype(low), ffn_up.astype(low)]
        wide_weights = lax.all_gather(jnp.concatenate(wide_share, axis=1), both, axis=0, tiled=True)
    else:
        gate_up = lax.all_gather(jnp.concatenate([ffn_gate.astype(low), ffn_up.astype(low)], axis=1), both, axis=0, tiled=True)
        w_down = lax.all_gather(ffn_down.astype(low), both, axis=0, tiled=True)
        c_output = lax.all_gather(cross_output.astype(low), both, axis=0, tiled=True)
    gain_columns = jnp.pad(gains.astype(low).T, ((0, 0), (0, spare - 3)))
    pieces = []
    for s in range(seq):
        for n, w in enumerate((self_query, self_key, self_value)):
            pieces.append(w[:, s * group_width : (s + 1) * group_width].astype(low))
            pieces.append(gain_columns if n == 0 else jnp.zeros((share, spare), low))
    own = jnp.concatenate(pieces, axis=1).reshape(share, seq, 3 * padded).transpose(1, 0, 2)
    if aligned:
        everyone, encoded, w_qkv = gather(nz, tokens[0], encoder[0], own.reshape(2, 2, share, 3 * padded))
    else:
        everyone = lax.all_gather(tokens[0], "seq", axis=0)
        encoded = lax.all_gather(encoder[0], "seq", axis=0)
        w_qkv = lax.all_to_all(own, "seq", split_axis=0, concat_axis=0, tiled=True)
        w_qkv = lax.all_gather(w_qkv, "fsdp", axis=1)
    everyone = everyone.reshape(seq * rows, width)
    encoded = encoded.reshape(-1, width)
    w_qkv = w_qkv.reshape(width, 3 * padded)
    length = lengths[0]
    values_in = tokens[0].astype(jnp.float32)
    qkv, normed_all, gain_rows = project(everyone, w_qkv, group_width)
    bias = bias_rows(rel_bias)
    plan = GatherPlan(nz, 4, share, width) if aligned else None
    own_mixed, own_logsum, *gathered = attend_forward(
        qkv, qkv, qkv, group, padded, bias, lengths, plan, (squares,) if aligned else ()
    )
    squares = gathered[0] if aligned else jnp.moveaxis(lax.all_gather(squares, both, axis=0), 1, 0)
    squares = squares.reshape(4, width, width)
    mixed = lax.all_to_all(own_mixed.reshape(seq, rows, padded), "seq", split_axis=0, concat_axis=0, tiled=True)
    cross_keys, cross_values = encode(encoded, squares)
    attended, normed_two, cross_queries = enter(tokens[0], mixed, squares, gain_rows, group_width)
    cross_mixed, cross_logsum = attend_forward(cross_queries, cross_keys, cross_values, heads)
    if aligned:
        scalars = jnp.stack([length, place * rows])
        result, grad_crossed, grad_cmixed, grad_coutput, gain_two, packed = middle(
            scalars, attended, cross_mixed, gain_rows, cotangent[0], wide_weights, inner, world
        )
        grad_gain_two = gain_two[0]
        packed = packed.reshape(width, -1)
    else:
        crossed = attended + nn(cross_mixed, c_output)
        normed_three = rms_norm(crossed, gain_rows[2]).astype(low)
        both_parts = nn(normed_three, gate_up)
        gate, upper = both_parts[:, :inner], both_parts[:, inner:]
        hidden = activate(gate, upper).astype(low)
        result = (crossed + nn(hidden, w_down)).astype(low)

        positions = place * rows + jnp.arange(rows, dtype=jnp.int32)
        grad_out = cotangent[0].astype(jnp.float32) * (positions < length).astype(jnp.float32)[:, None]
        grad_ffn = grad_out.astype(low)
        grad_hidden = nt(grad_ffn, w_down)
        _, pullback = jax.vjp(activate, gate, upper)
        grad_gate, grad_upper = pullback(grad_hidden)
        grad_both = jnp.concatenate([grad_gate.astype(low), grad_upper.astype(low)], axis=1)
        grad_down = tn(hidden, grad_ffn).astype(low).reshape(world, hidden_share, width)
        grad_down = jnp.pad(grad_down, ((0, 0), (0, slabs * share - hidden_share), (0, 0)))
        grad_down = grad_down.reshape(world, slabs, share, width).transpose(0, 2, 1, 3).reshape(world * share, slabs * width)
        packed = jnp.concatenate([tn(normed_three, grad_both).astype(low), grad_down], axis=1)

        grad_normed_three = nt(grad_both, gate_up)
        norm_part, grad_gain_two = rms_back(crossed, gain_rows[2], grad_normed_three)
        grad_crossed = grad_out + norm_part
        grad_branch = grad_crossed.astype(low)
        grad_coutput = tn(cross_mixed, grad_branch).astype(low)
        grad_cmixed = nt(grad_branch, c_output).astype(low)
    share_ffn = lax.psum_scatter(packed, both, scatter_dimension=0, tiled=True)
    slab = 64
    chunked = lambda g: g.reshape(2, 2, nz, 2, share, g.shape[-1])
    by_place = lambda g: g.reshape(2, 2, -1, slab, width)
    plan = ReducePlan(nz, 1, share, width, 4, heads) if aligned else None
    grad_cq, grad_ck, grad_cv, *first_sums = attend_backward(
        cross_queries, cross_keys, cross_values, grad_cmixed, cross_mixed, cross_logsum, heads,
        plan=plan, extra=(chunked(grad_coutput),) if aligned else (),
    )
    grad_attended, branch, grad_mixed, gain_one = leave(
        grad_cq, squares, attended, gain_rows, grad_crossed, seq, group_width, padded
    )
    grad_gain_one = gain_one[0]
    own_grad_mixed = lax.all_to_all(grad_mixed, "seq", split_axis=0, concat_axis=0, tiled=True).reshape(seq * rows, padded)
    grad_cquery, grad_ckey, grad_cvalue, grad_output, grad_encoded = square_terms(
        normed_two, grad_cq, encoded, grad_ck, grad_cv, squares, mixed, branch, group_width
    )
    early = [grad_cquery, grad_ckey, grad_cvalue]
    plan, extra = None, ()
    if aligned:
        extra = (*[chunked(g) for g in early], by_place(grad_encoded))
        plan = ReducePlan(nz, len(early), share, width, 3, 3 * BACKWARD_POINTS, extra[-1].shape[2:])
    own_dq, own_dk, own_dv, by_distance, *sums = attend_backward(
        qkv, qkv, qkv, own_grad_mixed, own_mixed, own_logsum, group, padded, bias, lengths, plan, extra
    )
    grad_normed_part, grad_own, gain_zero = unproject(everyone, normed_all, w_qkv, own_dq, own_dk, own_dv)
    grad_gain_zero = gain_zero[0]
    grad_gains = jnp.stack([grad_gain_zero, grad_gain_one, grad_gain_two])
    grad_gains = grad_gains.reshape(3, world, share).transpose(1, 0, 2).reshape(world, 1, 3 * share)
    grad_gains = jnp.pad(grad_gains, ((0, 0), (0, 7), (0, LANES - 3 * share)))
    wide = jnp.float32
    if aligned:
        share_output, *share_own, grad_normed, share_gains, by_distance = reduce(
            nz, group_width, chunked(grad_output), chunked(grad_own), by_place(grad_normed_part), grad_gains, by_distance
        )
        share_early, grad_encoded = sums
        share_squares = [share_output, *(share_early[n] for n in range(3)), first_sums[0][0]]
        grad_normed, grad_encoded = grad_normed.reshape(rows, width), grad_encoded.reshape(-1, width)
    else:
        scatter = lambda g, axes: lax.psum_scatter(g, axes, scatter_dimension=0, tiled=True)
        share_squares = scatter(jnp.concatenate([grad_output, *early, grad_coutput], axis=1), both).astype(wide)
        share_squares = [share_squares[:, n * width : (n + 1) * width] for n in range(5)]
        grad_own = scatter(grad_own.reshape(seq, fsdp, share, 3 * padded).transpose(1, 0, 2, 3), "fsdp")[0]
        grad_own = lax.all_to_all(grad_own, "seq", split_axis=0, concat_axis=0, tiled=True).astype(wide)
        grad_own = grad_own.reshape(seq, share, 3, padded)[:, :, :, :group_width].transpose(2, 1, 0, 3).reshape(3, share, width)
        share_own = [grad_own[n] for n in range(3)]
        grad_normed = scatter(grad_normed_part, "seq").astype(wide)
        grad_encoded = scatter(grad_encoded, "seq").astype(wide)
        share_gains = scatter(grad_gains, both)[0]
        by_distance = lax.psum(by_distance, "fsdp")
    share_gains = share_gains[0, : 3 * share].reshape(3, share)
    norm_part, _ = rms_back(values_in, gain_rows[0], grad_normed)
    grad_input = grad_attended + norm_part
    bins = rel_bias.shape[0]
    near_map = (buckets(jnp.arange(LANES, dtype=jnp.int32))[:, None] == jnp.arange(bins - 1, dtype=jnp.int32)[None]).astype(wide)
    near_sums = jnp.dot(near_map.T, by_distance[:group].T, precision=highest)
    table_grad = jnp.concatenate([near_sums, -jnp.sum(near_sums, axis=0, keepdims=True)], axis=0)
    share_ffn = share_ffn.astype(wide)
    share_down = share_ffn[:, 2 * inner :].reshape(share, slabs, width).transpose(1, 0, 2).reshape(slabs * share, width)
    return (
        result[None], grad_input[None], grad_encoded[None], share_gains, *share_own, *share_squares,
        share_ffn[:, :inner], share_ffn[:, inner : 2 * inner], share_down[:hidden_share], table_grad,
    )


def solution(mesh):
    split = P(("seq", "fsdp"), None)
    rows = P("fsdp", "seq", None)
    gains = P(None, ("seq", "fsdp"))
    return jax.shard_map(
        per_device,
        mesh=mesh,
        in_specs=(rows, rows, rows, P("fsdp"), gains, *([split] * 11), P(None, "seq")),
        out_specs=(rows, rows, rows, gains, *([split] * 11), P(None, "seq")),
        check_vma=False,
    )
```

```python
import functools

import jax
import jax.numpy as jnp
import numpy as np
from jax import lax
from jax.experimental import pallas as pl
from jax.experimental.pallas import tpu as pltpu
from jax.sharding import PartitionSpec as P

LANES = 128
BLOCK = 512
HEAD = 64
negative = -1e30
epsilon = 1e-06
highest = lax.Precision.HIGHEST
bounds = np.ceil(16.0 * 8.0 ** (np.arange(1, 16) / 16.0)).astype(np.int32)
low = jnp.bfloat16
MESH = pl.DeviceIdType.MESH


def nt(left, right):
    return lax.dot_general(left, right, (((1,), (1,)), ((), ())), preferred_element_type=jnp.float32)


def nn(left, right):
    return jnp.dot(left, right, preferred_element_type=jnp.float32)


def tn(left, right):
    return lax.dot_general(left, right, (((0,), (0,)), ((), ())), preferred_element_type=jnp.float32)


def buckets(distance):
    far = 16 + jnp.sum((distance[..., None] >= jnp.asarray(bounds)).astype(jnp.int32), axis=-1)
    return jnp.where(distance < 16, distance, far)


def bias_rows(table):
    count = table.shape[0]
    place = jnp.arange(3 * LANES, dtype=jnp.int32)
    onehot = buckets(jnp.clip(place, 0, 2 * LANES))[None, :] == jnp.arange(count, dtype=jnp.int32)[:, None]
    relative = table - table[count - 1 :]
    values = jnp.sum(jnp.where(onehot[:, None, :], relative[:, :, None], 0.0), axis=0)
    return jnp.where((place >= 2 * LANES)[None], negative, values)[:, None, :]


def head_place(heads):
    head = pl.program_id(0)
    per_tile = LANES // HEAD
    side = lax.rem(head, per_tile)
    lane = lax.broadcasted_iota(jnp.int32, (1, LANES), 1)
    return head, side == 0, (side == per_tile - 1) | (head == heads - 1), (lane // HEAD) == side


def bias_tiles(base_ref, t_scr):
    wide = jnp.broadcast_to(base_ref[0], (LANES, 3 * LANES))
    t_scr[...] = pltpu.roll(wide, 0, 1, stride=1, stride_axis=0)[:, : 2 * LANES]


def add_near(scores, t_scr):
    near = min(2 * LANES, scores.shape[1])
    fixed = scores[:, :near] + t_scr[:, :near]
    return fixed if near == scores.shape[1] else jnp.concatenate([fixed, scores[:, near:]], axis=1)


def add_corner(scores, t_scr):
    top, bottom = scores[:-LANES], scores[-LANES:]
    bottom = jnp.concatenate([bottom[:, :LANES] + t_scr[:, LANES:], bottom[:, LANES:]], axis=1)
    return jnp.concatenate([top, bottom], axis=0)


def at_step(head, stages, point, points):
    for due, stage in stages:
        if due >= 0 and due % points == point:
            pl.when(head == due // points)(stage)


def at_end(head, heads, stages):
    for due, stage in stages:
        if due < 0:
            pl.when(head == heads - 1)(stage)


FORWARD_POINTS = 4
BACKWARD_POINTS = 10


def attend_forward_kernel(*refs, causal, heads, plan):
    refs = list(refs)
    take = lambda n: [refs.pop(0) for _ in range(n)]
    if causal:
        (length_ref,) = take(1)
    q_ref, k_ref, v_ref = take(3)
    if causal:
        (base_ref,) = take(1)
    given = take(plan.inputs) if plan else []
    o_ref, lse_ref = take(2)
    made = take(plan.outputs) if plan else []
    s_scr, vt_scr, acc_scr, ot_scr = take(4)
    if causal:
        t_scr, mask_scr = take(2)
    stages = plan.stages(given, made, refs) if plan else []
    head, first, last, mask = head_place(heads)
    rows, keys = q_ref.shape[0], k_ref.shape[0]
    block = min(BLOCK, rows)
    if causal:
        bias_tiles(base_ref, t_scr)

        @pl.when(head == 0)
        def _():
            place = lax.broadcasted_iota(jnp.int32, (keys, LANES), 0)
            mask_scr[...] = jnp.where(place < length_ref[0], 0.0, negative)

    for at in range(0, keys, BLOCK):
        vt_scr[:, at : at + BLOCK] = jnp.where(mask, v_ref[at : at + BLOCK, :], 0).T

    def limit(scores, start):
        if start < BLOCK:
            return scores
        part = mask_scr[start : start + scores.shape[0], :]
        return scores + jnp.concatenate([part] * (scores.shape[1] // LANES), axis=1)

    for number in range(rows // block):
        at_step(head, stages, number, FORWARD_POINTS)
        start = number * block
        queries = jnp.where(mask, q_ref[start : start + block, :], 0)
        pieces = [(at, BLOCK, 0) for at in range(0, start if causal else keys, BLOCK)]
        if causal:
            pieces += [(start + part, LANES, part) for part in range(0, block, LANES)]
        largest = jnp.full((1, block), negative, jnp.float32)
        for at, size, skip in pieces:
            scores = nt(k_ref[at : at + size, :], queries[skip:])
            if causal:
                if size == LANES:
                    scores = add_near(scores, t_scr)
                elif at + size == start:
                    scores = add_corner(scores, t_scr)
                scores = limit(scores, at)
            s_scr[at : at + size, skip:] = scores
            top = jnp.maximum(largest[:, skip:], jnp.max(scores, axis=0, keepdims=True))
            largest = top if skip == 0 else jnp.concatenate([largest[:, :skip], top], axis=1)
        totals = jnp.zeros((1, block), jnp.float32)
        acc_scr[...] = jnp.zeros_like(acc_scr)
        for at, size, skip in pieces:
            expos = jnp.exp(s_scr[at : at + size, skip:] - largest[:, skip:])
            more = totals[:, skip:] + jnp.sum(expos, axis=0, keepdims=True)
            totals = more if skip == 0 else jnp.concatenate([totals[:, :skip], more], axis=1)
            acc_scr[:, skip:] += nn(vt_scr[:, at : at + size], expos.astype(low))
        lse_ref[0, :, start : start + block] = jnp.broadcast_to(largest + jnp.log(totals), (8, block))
        mixed = acc_scr[...] / totals
        ot_scr[:, start : start + block] = mixed + jnp.where(first, 0.0, ot_scr[:, start : start + block])

    @pl.when(last)
    def _():
        for at in range(0, rows, block):
            o_ref[at : at + block, :] = ot_scr[:, at : at + block].T.astype(low)

    at_end(head, heads, stages)


def attend_specs(queries, keys, padded):
    rows = queries.shape[0]
    width = padded or queries.shape[1]
    count = keys.shape[0]
    per_tile = LANES // HEAD
    skip = padded // LANES
    row_spec = pl.BlockSpec((rows, LANES), lambda h: (0, h // per_tile))
    key_spec = pl.BlockSpec((count, LANES), lambda h: (0, h // per_tile))
    key_specs = [pl.BlockSpec((count, LANES), lambda h, n=n: (0, n * skip + h // per_tile)) for n in (1, 2)]
    return rows, width, count, row_spec, key_spec, key_specs


def attend_forward(queries, keys, values, heads, padded=0, bias=None, length=None, plan=None, extra=()):
    causal = bias is not None
    rows, width, count, row_spec, _, key_specs = attend_specs(queries, keys, padded)
    block = min(BLOCK, rows)
    in_specs = [row_spec, *key_specs]
    args = [queries, keys, values]
    scratch = [
        pltpu.VMEM((count, block), jnp.float32), pltpu.VMEM((LANES, count), low),
        pltpu.VMEM((LANES, block), jnp.float32), pltpu.VMEM((LANES, rows), jnp.float32),
    ]
    if causal:
        in_specs = [pl.BlockSpec(memory_space=pltpu.SMEM), *in_specs, pl.BlockSpec((1, 1, 3 * LANES), lambda h: (h, 0, 0))]
        args = [length, *args, bias]
        scratch += [pltpu.VMEM((LANES, 2 * LANES), jnp.float32), pltpu.VMEM((count, LANES), jnp.float32)]
    return pl.pallas_call(
        functools.partial(attend_forward_kernel, causal=causal, heads=heads, plan=plan),
        grid=(heads,),
        in_specs=in_specs + (plan.in_specs() if plan else []),
        out_specs=[row_spec, pl.BlockSpec((1, 8, rows), lambda h: (h, 0, 0))] + (plan.out_specs() if plan else []),
        out_shape=[
            jax.ShapeDtypeStruct((rows, width), low),
            jax.ShapeDtypeStruct((heads, 8, rows), jnp.float32),
        ] + (plan.out_shape() if plan else []),
        scratch_shapes=scratch + (plan.scratch() if plan else []),
        compiler_params=plan.params() if plan else pltpu.CompilerParams(vmem_limit_bytes=62 * 2**20),
        cost_estimate=pl.CostEstimate(
            flops=4 * heads * LANES * rows * count // (2 if causal else 1),
            bytes_accessed=4 * (rows + count) * width,
            transcendentals=heads * rows * count // (2 if causal else 1),
        ),
        name="self_forward" if causal else "cross_forward",
    )(*args, *extra)


def attend_backward_kernel(*refs, causal, heads, plan):
    refs = list(refs)
    take = lambda n: [refs.pop(0) for _ in range(n)]
    if causal:
        (length_ref,) = take(1)
    q_ref, k_ref, v_ref, do_ref, o_ref, lse_ref = take(6)
    if causal:
        (base_ref,) = take(1)
    given = take(plan.inputs) if plan else []
    dq_ref, dk_ref, dv_ref = take(3)
    if causal:
        (distance_ref,) = take(1)
    made = take(plan.outputs) if plan else []
    kt_scr, dqt_scr, dk_scr, dv_scr, row_scr = take(5)
    if causal:
        t_scr, near_scr = take(2)
    stages = plan.stages(given, made, refs) if plan else []
    head, first, last, mask = head_place(heads)
    rows, keys = q_ref.shape[0], k_ref.shape[0]
    block = min(BLOCK, rows)
    key_block = min(BLOCK, keys)

    @pl.when(first)
    def _():
        dqt_scr[...] = jnp.zeros_like(dqt_scr)
        dk_scr[...] = jnp.zeros_like(dk_scr)
        dv_scr[...] = jnp.zeros_like(dv_scr)

    if causal:
        bias_tiles(base_ref, t_scr)
        near_scr[...] = jnp.zeros_like(near_scr)
    for at in range(0, keys, key_block):
        kt_scr[:, at : at + key_block] = jnp.where(mask, k_ref[at : at + key_block, :], 0).T
    for start in range(0, rows, block):
        at = slice(start, start + block)
        product = do_ref[at, :].astype(jnp.float32) * o_ref[at, :].astype(jnp.float32)
        delta = jnp.sum(jnp.where(mask, product, 0.0).T, axis=0, keepdims=True)
        logsum = lse_ref[0, 0:1, at]
        if causal:
            place = start + lax.broadcasted_iota(jnp.int32, (1, block), 1)
            logsum = jnp.where(place < length_ref[0], logsum, -negative)
        row_scr[0:1, at] = logsum
        row_scr[1:2, at] = delta

    def piece(key_at, row_at, fix=None):
        queries = jnp.where(mask, q_ref[row_at, :], 0)
        grads = jnp.where(mask, do_ref[row_at, :], 0)
        scores = nt(k_ref[key_at, :], queries)
        if fix is not None:
            scores = fix(scores, t_scr)
        weights = jnp.exp(scores - row_scr[0:1, row_at])
        grad_weights = nt(v_ref[key_at, :], grads)
        grad_scores = weights * (grad_weights - row_scr[1:2, row_at])
        low_scores = grad_scores.astype(low)
        dv_scr[key_at, :] += nn(weights.astype(low), grads)
        dk_scr[key_at, :] += nn(low_scores, queries)
        dqt_scr[:, row_at] += nn(kt_scr[:, key_at], low_scores)
        return grad_scores

    point = 0
    if not causal:
        at_step(head, stages, 0, 1)
        for start in range(0, keys, key_block):
            for at in range(0, rows, block):
                piece(slice(start, start + key_block), slice(at, at + block))
    else:
        for start in range(0, keys, block):
            at_step(head, stages, point, BACKWARD_POINTS)
            point += 1
            for here in range(start, start + block, LANES):
                grad = piece(slice(here, here + LANES), slice(here, start + block), add_near)
                near = min(2 * LANES, grad.shape[1])
                near_scr[:, :near] += grad[:, :near]
            for at in range(start + block, rows, block):
                at_step(head, stages, point, BACKWARD_POINTS)
                point += 1
                beside = at == start + block
                grad = piece(slice(start, start + block), slice(at, at + block), add_corner if beside else None)
                if beside:
                    near_scr[:, LANES:] += grad[-LANES:, :LANES]
        flip = lax.broadcasted_iota(jnp.int32, (LANES, LANES), 0) + lax.broadcasted_iota(jnp.int32, (LANES, LANES), 1)
        flip = (flip == LANES - 1).astype(jnp.float32)
        turned = lax.dot_general(
            flip, near_scr[...], (((1,), (0,)), ((), ())), precision=highest, preferred_element_type=jnp.float32
        )
        turned = pltpu.roll(turned, 1, 1, stride=1, stride_axis=0)
        sums = jnp.sum(turned[:, LANES:], axis=0, keepdims=True)
        at_row = lax.broadcasted_iota(jnp.int32, (8, LANES), 0) == head
        before = jnp.where(head == 0, 0.0, distance_ref[...])
        distance_ref[...] = jnp.where(at_row, jnp.broadcast_to(sums, (8, LANES)), before)

    @pl.when(last)
    def _():
        for at in range(0, rows, block):
            dq_ref[at : at + block, :] = dqt_scr[:, at : at + block].T.astype(low)
        dk_ref[...] = dk_scr[...].astype(low)
        dv_ref[...] = dv_scr[...].astype(low)

    at_end(head, heads, stages)


def attend_backward(queries, keys, values, grad_mixed, mixed, logsum, heads, padded=0, bias=None, length=None, plan=None, extra=()):
    causal = bias is not None
    rows, width, count, row_spec, key_spec, key_specs = attend_specs(queries, keys, padded)
    in_specs = [row_spec, *key_specs, row_spec, row_spec, pl.BlockSpec((1, 8, rows), lambda h: (h, 0, 0))]
    args = [queries, keys, values, grad_mixed, mixed, logsum]
    out_specs = [row_spec, key_spec, key_spec]
    out_shape = [jax.ShapeDtypeStruct((n, width), low) for n in (rows, count, count)]
    scratch = [
        pltpu.VMEM((LANES, count), low), pltpu.VMEM((LANES, rows), jnp.float32),
        pltpu.VMEM((count, LANES), jnp.float32), pltpu.VMEM((count, LANES), jnp.float32), pltpu.VMEM((8, rows), jnp.float32),
    ]
    if causal:
        in_specs = [pl.BlockSpec(memory_space=pltpu.SMEM), *in_specs, pl.BlockSpec((1, 1, 3 * LANES), lambda h: (h, 0, 0))]
        args = [length, *args, bias]
        out_specs += [pl.BlockSpec((8, LANES), lambda h: (0, 0))]
        out_shape += [jax.ShapeDtypeStruct((8, LANES), jnp.float32)]
        scratch += [pltpu.VMEM((LANES, 2 * LANES), jnp.float32), pltpu.VMEM((LANES, 2 * LANES), jnp.float32)]
    return pl.pallas_call(
        functools.partial(attend_backward_kernel, causal=causal, heads=heads, plan=plan),
        grid=(heads,),
        in_specs=in_specs + (plan.in_specs() if plan else []),
        out_specs=out_specs + (plan.out_specs() if plan else []),
        out_shape=out_shape + (plan.out_shape() if plan else []),
        scratch_shapes=scratch + (plan.scratch() if plan else []),
        compiler_params=plan.params() if plan else pltpu.CompilerParams(vmem_limit_bytes=62 * 2**20),
        cost_estimate=pl.CostEstimate(
            flops=10 * heads * LANES * rows * count // (2 if causal else 1),
            bytes_accessed=8 * (rows + count) * width,
            transcendentals=heads * rows * count // (2 if causal else 1),
        ),
        name="self_backward" if causal else "cross_backward",
    )(*args, *extra)


def scale_of(values):
    return lax.rsqrt(jnp.mean(values * values, axis=-1, keepdims=True) + epsilon)


def project_kernel(gain_lane, x_ref, w_ref, qkv_ref, normed_ref, gains_ref):
    @pl.when(pl.program_id(0) == 0)
    def _():
        tile = gain_lane // LANES * LANES
        turned = w_ref[:, tile : tile + LANES].astype(jnp.float32).T
        first = gain_lane - tile
        gains_ref[...] = turned[first : first + 8]

    values = x_ref[...].astype(jnp.float32)
    normed = (values * scale_of(values) * gains_ref[0:1, :]).astype(low)
    normed_ref[...] = normed
    qkv_ref[...] = nn(normed, w_ref[...]).astype(low)


def project(everyone, w_qkv, gain_lane):
    count, width = everyone.shape
    wide = w_qkv.shape[1]
    block = min(BLOCK, count)
    rows = lambda n: pl.BlockSpec((block, n), lambda i: (i, 0))
    return pl.pallas_call(
        functools.partial(project_kernel, gain_lane),
        grid=(count // block,),
        in_specs=[rows(width), pl.BlockSpec((width, wide), lambda i: (0, 0))],
        out_specs=[rows(wide), rows(width), pl.BlockSpec((8, width), lambda i: (0, 0))],
        out_shape=[
            jax.ShapeDtypeStruct((count, wide), low), jax.ShapeDtypeStruct((count, width), low),
            jax.ShapeDtypeStruct((8, width), jnp.float32),
        ],
        compiler_params=pltpu.CompilerParams(vmem_limit_bytes=62 * 2**20),
        name="project",
    )(everyone, w_qkv)


def unproject_kernel(x_ref, normed_ref, w_ref, dq_ref, dk_ref, dv_ref, part_ref, own_ref, gain_ref, own_scr):
    step = pl.program_id(0)
    padded = dq_ref.shape[1]
    grads = [r[...] for r in (dq_ref, dk_ref, dv_ref)]
    part = sum(nt(g, w_ref[:, n * padded : (n + 1) * padded]) for n, g in enumerate(grads))
    values = x_ref[...].astype(jnp.float32)
    share = jnp.sum(part * (values * scale_of(values)), axis=0, keepdims=True)
    part_ref[...] = part.astype(low)
    turned = normed_ref[...].T

    @pl.when(step == 0)
    def _():
        gain_ref[...] = jnp.zeros_like(gain_ref)
        own_scr[...] = jnp.zeros_like(own_scr)

    gain_ref[...] += jnp.broadcast_to(share, gain_ref.shape)
    for n, g in enumerate(grads):
        own_scr[:, n * padded : (n + 1) * padded] += nn(turned, g)

    @pl.when(step == pl.num_programs(0) - 1)
    def _():
        own_ref[...] = own_scr[...].astype(low)


def unproject(everyone, normed, w_qkv, dq, dk, dv):
    count, width = everyone.shape
    wide, padded = w_qkv.shape[1], dq.shape[1]
    block = min(BLOCK, count)
    rows = lambda n: pl.BlockSpec((block, n), lambda i: (i, 0))
    fixed = lambda a, b: pl.BlockSpec((a, b), lambda i: (0, 0))
    return pl.pallas_call(
        unproject_kernel,
        grid=(count // block,),
        in_specs=[rows(width), rows(width), fixed(width, wide), rows(padded), rows(padded), rows(padded)],
        out_specs=[rows(width), fixed(width, wide), fixed(8, width)],
        out_shape=[
            jax.ShapeDtypeStruct((count, width), low), jax.ShapeDtypeStruct((width, wide), low),
            jax.ShapeDtypeStruct((8, width), jnp.float32),
        ],
        scratch_shapes=[pltpu.VMEM((width, wide), jnp.float32)],
        compiler_params=pltpu.CompilerParams(vmem_limit_bytes=62 * 2**20),
        name="unproject",
    )(everyone, normed, w_qkv, dq, dk, dv)


slope = float(np.sqrt(2.0 / np.pi))
cubic = 0.044715


def middle_kernel(
    slabs, scalars, x1_ref, mixed_ref, co_ref, gains_ref, cot_ref, gate_ref, up_ref, *refs
):
    slab_refs, refs = refs[:slabs], refs[slabs:]
    out_ref, dx_ref, dm_ref, co_grad_ref, gain_ref, packed = refs[:6]
    x2_scr, n3_scr, n3t_scr, df_scr, result_scr, dn_scr, down_ref, gate_buf, up_buf, down_buf, sem = refs[6:]
    step, steps = pl.program_id(0), pl.num_programs(0)
    rows, width = x1_ref.shape
    block = gate_ref.shape[1]
    world, share = packed.shape[:2]
    inner = block * steps
    owners = down_buf.shape[1]
    hidden_share = block // owners

    @pl.when(step == 0)
    def _():
        x2 = x1_ref[...] + nn(mixed_ref[...], co_ref[...])
        x2_scr[...] = x2
        normed = (x2 * scale_of(x2) * gains_ref[2:3, :]).astype(low)
        n3_scr[...] = normed
        n3t_scr[...] = normed.T
        place = scalars[1] + lax.broadcasted_iota(jnp.int32, (rows, 1), 0)
        df_scr[...] = jnp.where(place < scalars[0], cot_ref[...], 0)
        result_scr[...] = x2
        dn_scr[...] = jnp.zeros_like(dn_scr)
        down_buf[...] = jnp.zeros_like(down_buf)

    for o in range(owners):
        for k in range(slabs):
            size = min(share, hidden_share - k * share)
            start = o * hidden_share + k * share
            down_ref[start : start + size] = slab_refs[k][o, :size]

    normed, df = n3_scr[...], df_scr[...]
    gate, upper = nn(normed, gate_ref[...]), nn(normed, up_ref[...])
    bent = jnp.tanh(slope * (gate + cubic * (gate * gate * gate)))
    half = 0.5 * (1.0 + bent)
    active = gate * half
    hidden = (active * upper).astype(low)
    result_scr[...] += nn(hidden, down_ref[...])
    grad_hidden = nt(df, down_ref[...])
    rise = half + (0.5 * gate) * ((1.0 - bent * bent) * (slope + (3.0 * cubic * slope) * (gate * gate)))
    grad_gate = (grad_hidden * upper * rise).astype(low)
    grad_upper = (grad_hidden * active).astype(low)
    dn_scr[...] += nt(grad_gate, gate_ref[...]) + nt(grad_upper, up_ref[...])
    slot = lax.rem(step, 2)

    def sends(at, which):
        first = pl.multiple_of(at * block, LANES)
        yield pltpu.make_async_copy(gate_buf.at[which], packed.at[:, :, pl.ds(first, block)], sem.at[which, 0])
        yield pltpu.make_async_copy(up_buf.at[which], packed.at[:, :, pl.ds(pl.multiple_of(inner + at * block, LANES), block)], sem.at[which, 1])
        for k in range(slabs):
            column = 2 * inner + k * width
            yield pltpu.make_async_copy(
                down_buf.at[which, :, k], packed.at[pl.ds(at * owners, owners), :, column : column + width], sem.at[which, 2 + k]
            )

    @pl.when(step >= 2)
    def _():
        for copy in sends(step - 2, slot):
            copy.wait()

    turned = n3t_scr[...]
    gate_buf[slot] = nn(turned, grad_gate).reshape(world, share, block).astype(low)
    up_buf[slot] = nn(turned, grad_upper).reshape(world, share, block).astype(low)
    grad_down = tn(hidden, df)
    for o in range(owners):
        for k in range(slabs):
            size = min(share, hidden_share - k * share)
            start = o * hidden_share + k * share
            down_buf[slot, o, k, :size] = grad_down[start : start + size].astype(low)
    for copy in sends(step, slot):
        copy.start()

    @pl.when(step == steps - 1)
    def _():
        out_ref[...] = result_scr[...].astype(low)
        x2, grad_normed = x2_scr[...], dn_scr[...]
        scale = scale_of(x2)
        unit = x2 * scale
        grad_unit = grad_normed * gains_ref[2:3, :]
        gain_ref[...] = jnp.broadcast_to(jnp.sum(grad_normed * unit, axis=0, keepdims=True), gain_ref.shape)
        back = scale * (grad_unit - unit * jnp.mean(grad_unit * unit, axis=-1, keepdims=True))
        dx = df.astype(jnp.float32) + back
        dx_ref[...] = dx
        branch = dx.astype(low)
        dm_ref[...] = nt(branch, co_ref[...]).astype(low)
        co_grad_ref[...] = tn(mixed_ref[...], branch).astype(low)
        if steps > 1:
            for copy in sends(step - 1, 1 - slot):
                copy.wait()
        for copy in sends(step, slot):
            copy.wait()


def middle(scalars, x1, mixed, gains, cotangent, weights, inner, world):
    rows, width = x1.shape
    block = min(BLOCK, inner)
    steps = inner // block
    share, hidden_share = width // world, inner // world
    slabs = -(-hidden_share // share)
    owners = block // hidden_share
    ahead = (1 + slabs) * width // block
    fixed = lambda *shape: pl.BlockSpec(shape, lambda j: (0,) * len(shape))
    f32 = jnp.float32
    return pl.pallas_call(
        functools.partial(middle_kernel, slabs),
        grid=(steps,),
        in_specs=[
            pl.BlockSpec(memory_space=pltpu.SMEM), fixed(rows, width), fixed(rows, width), fixed(width, width),
            fixed(8, width), fixed(rows, width),
            pl.BlockSpec((width, block), lambda j: (0, ahead + j)), pl.BlockSpec((width, block), lambda j: (0, ahead + steps + j)),
            *[pl.BlockSpec((owners, share, width), lambda j, k=k: (j, 0, 1 + k)) for k in range(slabs)],
        ],
        out_specs=[
            fixed(rows, width), fixed(rows, width), fixed(rows, width), fixed(width, width), fixed(8, width),
            pl.BlockSpec(memory_space=pl.ANY),
        ],
        out_shape=[
            jax.ShapeDtypeStruct((rows, width), low), jax.ShapeDtypeStruct((rows, width), f32),
            jax.ShapeDtypeStruct((rows, width), low), jax.ShapeDtypeStruct((width, width), low),
            jax.ShapeDtypeStruct((8, width), f32),
            jax.ShapeDtypeStruct((world, share, 2 * inner + slabs * width), low),
        ],
        scratch_shapes=[
            pltpu.VMEM((rows, width), f32), pltpu.VMEM((rows, width), low), pltpu.VMEM((width, rows), low),
            pltpu.VMEM((rows, width), low), pltpu.VMEM((rows, width), f32), pltpu.VMEM((rows, width), f32),
            pltpu.VMEM((block, width), low),
            pltpu.VMEM((2, world, share, block), low), pltpu.VMEM((2, world, share, block), low),
            pltpu.VMEM((2, owners, slabs, share, width), low), pltpu.SemaphoreType.DMA((2, 2 + slabs)),
        ],
        compiler_params=pltpu.CompilerParams(vmem_limit_bytes=62 * 2**20),
        cost_estimate=pl.CostEstimate(
            flops=2 * rows * width * (9 * inner + 3 * width), transcendentals=rows * inner, bytes_accessed=26 * width * inner // 4
        ),
        name="middle",
    )(scalars, x1, mixed, weights, gains, cotangent, weights, weights, *[weights.reshape(world, share, -1)] * slabs)


def encode_kernel(enc_ref, w_ref, key_ref, value_ref):
    for n, out in enumerate((key_ref, value_ref)):
        out[...] = nn(enc_ref[...], w_ref[n]).astype(low)


def encode(encoded, squares):
    count, width = encoded.shape
    part = width // 3
    columns = pl.BlockSpec((count, part), lambda j: (0, j))
    return pl.pallas_call(
        encode_kernel,
        grid=(3,),
        in_specs=[pl.BlockSpec((count, width), lambda j: (0, 0)), pl.BlockSpec((2, width, part), lambda j: (1, 0, j))],
        out_specs=[columns] * 2,
        out_shape=[jax.ShapeDtypeStruct((count, width), low)] * 2,
        compiler_params=pltpu.CompilerParams(vmem_limit_bytes=62 * 2**20),
        cost_estimate=pl.CostEstimate(flops=4 * count * width * width, transcendentals=0, bytes_accessed=8 * width * width),
        name="encode",
    )(encoded, squares)


def enter_kernel(group_width, x_ref, mixed_ref, w_ref, gains_ref, attended_ref, normed_ref, query_ref):
    total = x_ref[...].astype(jnp.float32)
    for s in range(mixed_ref.shape[0]):
        total += nn(mixed_ref[s, :, :group_width], w_ref[0, s * group_width : (s + 1) * group_width])
    attended_ref[...] = total
    normed = (total * scale_of(total) * gains_ref[1:2, :]).astype(low)
    normed_ref[...] = normed
    query_ref[...] = nn(normed, w_ref[1]).astype(low)


def enter(tokens, mixed, squares, gains, group_width):
    rows, width = tokens.shape
    seq, _, padded = mixed.shape
    block = min(256, rows)
    by_rows = pl.BlockSpec((block, width), lambda i: (i, 0))
    return pl.pallas_call(
        functools.partial(enter_kernel, group_width),
        grid=(rows // block,),
        in_specs=[
            by_rows, pl.BlockSpec((seq, block, padded), lambda i: (0, i, 0)), pl.BlockSpec((2, width, width), lambda i: (0, 0, 0)),
            pl.BlockSpec((8, width), lambda i: (0, 0)),
        ],
        out_specs=[by_rows] * 3,
        out_shape=[jax.ShapeDtypeStruct((rows, width), t) for t in (jnp.float32, low, low)],
        compiler_params=pltpu.CompilerParams(vmem_limit_bytes=62 * 2**20),
        cost_estimate=pl.CostEstimate(flops=4 * rows * width * width, transcendentals=0, bytes_accessed=12 * width * width),
        name="enter",
    )(tokens, mixed, squares, gains)


def leave_kernel(group_width, grad_ref, w_ref, attended_ref, gains_ref, dx_ref, total_ref, branch_ref, dm_ref, gain_ref):
    @pl.when(pl.program_id(0) == 0)
    def _():
        gain_ref[...] = jnp.zeros_like(gain_ref)

    grad_normed = nt(grad_ref[...], w_ref[1])
    values = attended_ref[...]
    scale = scale_of(values)
    unit = values * scale
    grad_unit = grad_normed * gains_ref[1:2, :]
    gain_ref[...] += jnp.broadcast_to(jnp.sum(grad_normed * unit, axis=0, keepdims=True), gain_ref.shape)
    total = dx_ref[...] + scale * (grad_unit - unit * jnp.mean(grad_unit * unit, axis=-1, keepdims=True))
    total_ref[...] = total
    branch = total.astype(low)
    branch_ref[...] = branch
    for s in range(dm_ref.shape[0]):
        dm_ref[s, :, :group_width] = nt(branch, w_ref[0, s * group_width : (s + 1) * group_width]).astype(low)
        if dm_ref.shape[2] > group_width:
            dm_ref[s, :, group_width:] = jnp.zeros((branch.shape[0], dm_ref.shape[2] - group_width), low)


def leave(grad_queries, squares, attended, gains, grad_crossed, seq, group_width, padded):
    rows, width = grad_queries.shape
    block = min(256, rows)
    by_rows = pl.BlockSpec((block, width), lambda i: (i, 0))
    fixed = pl.BlockSpec((8, width), lambda i: (0, 0))
    return pl.pallas_call(
        functools.partial(leave_kernel, group_width),
        grid=(rows // block,),
        in_specs=[by_rows, pl.BlockSpec((2, width, width), lambda i: (0, 0, 0)), by_rows, fixed, by_rows],
        out_specs=[by_rows, by_rows, pl.BlockSpec((seq, block, padded), lambda i: (0, i, 0)), fixed],
        out_shape=[
            jax.ShapeDtypeStruct((rows, width), jnp.float32), jax.ShapeDtypeStruct((rows, width), low),
            jax.ShapeDtypeStruct((seq, rows, padded), low), jax.ShapeDtypeStruct((8, width), jnp.float32),
        ],
        compiler_params=pltpu.CompilerParams(vmem_limit_bytes=62 * 2**20),
        cost_estimate=pl.CostEstimate(flops=4 * rows * width * width, transcendentals=0, bytes_accessed=16 * width * width),
        name="leave",
    )(grad_queries, squares, attended, gains, grad_crossed)


def square_terms_kernel(group_width, normed, grad_q, encoded, grad_k, grad_v, w_ref, mixed, branch, q_out, k_out, v_out, o_out, e_out, *scratch):
    normed_t, encoded_t, mixed_t, total = scratch
    step = pl.program_id(0)

    @pl.when(step == 0)
    def _():
        normed_t[...] = normed[...].T
        encoded_t[...] = encoded[...].T
        for s in range(mixed.shape[0]):
            mixed_t[s * group_width : (s + 1) * group_width] = mixed[s].T[:group_width]
        total[...] = jnp.zeros_like(total)

    q_out[...] = nn(normed_t[...], grad_q[...]).astype(low)
    k_out[...] = nn(encoded_t[...], grad_k[...]).astype(low)
    v_out[...] = nn(encoded_t[...], grad_v[...]).astype(low)
    o_out[...] = nn(mixed_t[...], branch[...]).astype(low)
    total[...] += nt(grad_k[...], w_ref[0]) + nt(grad_v[...], w_ref[1])

    @pl.when(step == pl.num_programs(0) - 1)
    def _():
        e_out[...] = total[...].astype(low)


def square_terms(normed, grad_q, encoded, grad_k, grad_v, squares, mixed, branch, group_width):
    rows, width = normed.shape
    count = encoded.shape[0]
    part = width // 3
    fixed = lambda v: pl.BlockSpec(v.shape, lambda j: (0,) * v.ndim)
    columns = lambda n: pl.BlockSpec((n, part), lambda j: (0, j))
    return pl.pallas_call(
        functools.partial(square_terms_kernel, group_width),
        grid=(3,),
        in_specs=[
            fixed(normed), columns(rows), fixed(encoded), columns(count), columns(count),
            pl.BlockSpec((2, width, part), lambda j: (1, 0, j)), fixed(mixed), columns(rows),
        ],
        out_specs=[columns(width)] * 4 + [fixed(encoded)],
        out_shape=[jax.ShapeDtypeStruct((width, width), low)] * 4 + [jax.ShapeDtypeStruct((count, width), low)],
        scratch_shapes=[
            pltpu.VMEM((width, rows), low), pltpu.VMEM((width, count), low), pltpu.VMEM((width, rows), low),
            pltpu.VMEM((count, width), jnp.float32),
        ],
        compiler_params=pltpu.CompilerParams(vmem_limit_bytes=62 * 2**20),
        cost_estimate=pl.CostEstimate(flops=12 * rows * width * width, transcendentals=0, bytes_accessed=24 * width * width),
        name="square_terms",
    )(normed, grad_q, encoded, grad_k, grad_v, squares, mixed, branch)


def coordinates():
    place, slot = lax.axis_index("seq"), lax.axis_index("fsdp")
    return place // 2, lax.rem(place, 2), slot // 2, lax.rem(slot, 2)


def device(x, c, z, y):
    return (x * 2 + c, z * 2 + y)


class Near:
    def __init__(self, nz):
        self.nz = nz
        x, c, z, y = self.x, self.c, self.z, self.y = coordinates()
        self.by_x, self.by_core, self.by_y = device(1 - x, c, z, y), device(x, 1 - c, z, y), device(x, c, z, 1 - y)
        self.diagonal = device(1 - x, 1 - c, z, y)
        self.steps = [lax.rem(z + t, nz) for t in range(nz)]
        self.backs = [lax.rem(z - t + nz, nz) for t in range(nz)]
        self.by_z = [device(x, c, self.steps[t], y) for t in range(nz)]


def greet(others):
    barrier = pltpu.get_barrier_semaphore()
    for other in others:
        pl.semaphore_signal(barrier, inc=1, device_id=other, device_id_type=MESH)
    pl.semaphore_wait(barrier, len(others))


class Copies:
    def __init__(self, send_sem, recv_sem):
        self.send_sem, self.recv_sem, self.made = send_sem, recv_sem, []

    def add(self, source, target, other):
        self.made.append((source, target, other))
        return len(self.made) - 1

    def copy(self, number):
        source, target, other = self.made[number]
        return pltpu.make_async_remote_copy(
            src_ref=source(), dst_ref=target(), send_sem=self.send_sem.at[number], recv_sem=self.recv_sem.at[number],
            device_id=other, device_id_type=MESH,
        )

    def start(self, *numbers):
        for number in numbers:
            self.copy(number).start()

    def arrive(self, *numbers):
        for number in numbers:
            self.copy(number).wait_recv()

    def finish(self):
        for number in range(len(self.made)):
            self.copy(number).wait_send()


def add_low(target, left, right):
    count = left.shape[0]
    unroll = 4 if count % 4 == 0 else 1

    @pl.loop(0, count // unroll)
    def _(n):
        for k in range(unroll):
            at = n * unroll + k
            if target.dtype == low:
                target[at] = left[at] + right[at]
            else:
                target[at] = left[at].astype(target.dtype) + right[at].astype(target.dtype)


def whole(space=pltpu.VMEM):
    return pl.BlockSpec(memory_space=space)


class GatherPlan:
    inputs, outputs = 1, 1

    def __init__(self, nz, count, share, width):
        self.nz, self.count, self.share, self.width = nz, count, share, width
        self.total = 8 * nz - 1

    def in_specs(self):
        return [whole()]

    def out_specs(self):
        return [whole(pl.ANY)]

    def out_shape(self):
        return [jax.ShapeDtypeStruct((self.count, 2, 2, self.nz, 2, self.share, self.width), low)]

    def scratch(self):
        return [pltpu.SemaphoreType.DMA((self.total,)), pltpu.SemaphoreType.DMA((self.total,)), pltpu.SemaphoreType.DMA((1,))]

    def params(self):
        return pltpu.CompilerParams(collective_id=2, has_side_effects=True, vmem_limit_bytes=62 * 2**20)

    def stages(self, given, made, scratch):
        (src,), (out,), (send_sem, recv_sem, local_sem) = given, made, scratch
        nz, my = self.nz, Near(self.nz)
        x, c, z, y, backs = my.x, my.c, my.z, my.y, my.backs
        copies = Copies(send_sem, recv_sem)
        own = lambda: src
        at = lambda xx, cc, zz, yy: lambda: out.at[:, xx, cc, zz, yy]
        mine = at(x, c, z, y)
        by_z = [None] + [copies.add(own, mine, my.by_z[t]) for t in range(1, nz)]
        held = [mine if t == 0 else at(x, c, backs[t], y) for t in range(nz)]
        source = [own if t == 0 else held[t] for t in range(nz)]
        by_y = [copies.add(source[t], held[t], my.by_y) for t in range(nz)]
        by_x = [copies.add(source[t], held[t], my.by_x) for t in range(nz)]
        by_core = [copies.add(source[t], held[t], my.by_core) for t in range(nz)]
        from_x = [at(1 - x, c, backs[t], y) for t in range(nz)]
        from_y = [at(x, c, backs[t], 1 - y) for t in range(nz)]
        far = [at(1 - x, c, backs[t], 1 - y) for t in range(nz)]
        corner = [
            copies.add(from_x[t], from_x[t], my.by_y) if t % 2 == 0 else copies.add(from_y[t], from_y[t], my.by_x)
            for t in range(nz)
        ]
        core_x = [copies.add(from_x[t], from_x[t], my.by_core) for t in range(nz)]
        core_y = [copies.add(from_y[t], from_y[t], my.by_core) for t in range(nz)]
        core_far = [copies.add(far[t], far[t], my.by_core) for t in range(nz)]
        local = lambda: pltpu.make_async_copy(src, mine(), local_sem.at[0])

        def begin():
            greet([my.by_x, my.by_core, my.by_y, *my.by_z[1:]])
            copies.start(*by_z[1:], by_y[0], by_x[0], by_core[0])
            local().start()

        def line(t):
            copies.arrive(by_z[t])
            copies.start(by_y[t], by_x[t], by_core[t])

        def plane(t):
            copies.arrive(by_x[t])
            copies.start(*([corner[t]] if t % 2 == 0 else []), core_x[t])
            copies.arrive(by_y[t])
            copies.start(*([corner[t]] if t % 2 == 1 else []), core_y[t])

        def turn(t):
            copies.arrive(corner[t])
            copies.start(core_far[t])

        def end():
            local().wait()
            copies.arrive(*by_core, *core_x, *core_y, *core_far)
            copies.finish()

        work = [functools.partial(line, t) for t in range(1, nz)]
        work += [functools.partial(plane, t) for t in range(nz)] + [functools.partial(turn, t) for t in range(nz)]
        points = 3 * FORWARD_POINTS - 1
        stages = [(0, begin)]
        for number, stage in enumerate(work):
            stages.append((1 + number * points // (len(work) + 1), stage))
        return stages + [(-1, end)]


class ReducePlan:
    def __init__(self, nz, count, share, width, number, points, slabs=None):
        self.nz, self.count, self.share, self.width, self.slabs = nz, count, share, width, slabs
        self.number, self.points = number, points
        self.inputs = count + (slabs is not None)
        self.outputs = 1 + (slabs is not None)
        self.total = count * (nz + 1) + count + 2 * (slabs is not None)

    def in_specs(self):
        return [whole()] * self.inputs

    def out_specs(self):
        return [whole()] * self.outputs

    def out_shape(self):
        shapes = [jax.ShapeDtypeStruct((self.count, self.share, self.width), jnp.float32)]
        return shapes + ([jax.ShapeDtypeStruct(self.slabs, jnp.float32)] if self.slabs else [])

    def scratch(self):
        nz, tail = self.nz, (self.share, self.width)
        vmem = lambda *shape: pltpu.VMEM((self.count, *shape, *tail), low)
        slabs = [pltpu.VMEM((*lead, *self.slabs), low) for lead in ((2,), (2,), ())] if self.slabs else []
        sems = [pltpu.SemaphoreType.DMA((self.total,)), pltpu.SemaphoreType.DMA((self.total,))]
        return [vmem(2, 2, nz), vmem(2, nz, 2), vmem(2, nz), vmem(2, nz), vmem(nz), vmem(nz), vmem(nz - 1), *slabs, *sems]

    def params(self):
        return pltpu.CompilerParams(collective_id=self.number, has_side_effects=True, vmem_limit_bytes=62 * 2**20)

    def stages(self, given, made, scratch):
        squares, out, beside = given[: self.count], made[0], self.slabs is not None
        a, ra, b, rb, d, rd, re = scratch[:7]
        send_sem, recv_sem = scratch[-2:]
        if beside:
            enc, out_enc, (enc_r, enc_a, enc_rx) = given[-1], made[1], scratch[7:10]
        nz, my, count = self.nz, Near(self.nz), self.count
        x, c, z, y = my.x, my.c, my.z, my.y
        copies = Copies(send_sem, recv_sem)
        if beside:
            enc_core = copies.add(lambda: enc.at[:, 1 - c], lambda: enc_r, my.by_core)
            enc_x = copies.add(lambda: enc_a.at[1 - x], lambda: enc_rx, my.by_x)
        core = [copies.add(lambda n=n: squares[n].at[:, 1 - c], lambda n=n: ra.at[n], my.by_core) for n in range(count)]
        one, two, three = [], [], []
        for n in range(count):
            y_first = n % 2 == 0
            if y_first:
                one.append(copies.add(lambda n=n: a.at[n, :, 1 - y], lambda n=n: rb.at[n], my.by_y))
                two.append(copies.add(lambda n=n: b.at[n, 1 - x], lambda n=n: rd.at[n], my.by_x))
            else:
                one.append(copies.add(lambda n=n: a.at[n, 1 - x], lambda n=n: rb.at[n], my.by_x))
                two.append(copies.add(lambda n=n: b.at[n, 1 - y], lambda n=n: rd.at[n], my.by_y))
            three.append([
                copies.add(lambda n=n, t=t: d.at[n, my.steps[t]], lambda n=n, t=t: re.at[n, t - 1], my.by_z[t])
                for t in range(1, nz)
            ])

        def begin():
            greet([my.by_x, my.by_core, my.by_y, *my.by_z[1:]])
            copies.start(*core, *([enc_core] if beside else []))

        def after_core(n):
            copies.arrive(core[n])
            for half in range(2):
                for side in range(2):
                    add_low(a.at[n, half, side], squares[n].at[half, c, :, side], ra.at[n, half, :, side])
            copies.start(one[n])

        def after_one(n):
            copies.arrive(one[n])
            for side in range(2):
                if n % 2 == 0:
                    add_low(b.at[n, side], a.at[n, side, y], rb.at[n, side])
                else:
                    add_low(b.at[n, side], a.at[n, x, side], rb.at[n, side])
            copies.start(two[n])

        def after_two(n):
            copies.arrive(two[n])
            add_low(d.at[n], b.at[n, x if n % 2 == 0 else y], rd.at[n])
            copies.start(*three[n])

        def after_three(n):
            copies.arrive(*three[n])
            total = d[n, z].astype(jnp.float32)
            for t in range(nz - 1):
                total += re[n, t].astype(jnp.float32)
            out[n] = total

        def encoder():
            copies.arrive(enc_core)
            for half in range(2):
                add_low(enc_a.at[half], enc.at[half, c], enc_r.at[half])
            copies.start(enc_x)

        def end():
            if beside:
                copies.arrive(enc_x)
                add_low(out_enc, enc_a.at[x], enc_rx)
            for n in range(count):
                after_three(n)
            copies.finish()

        part = functools.partial
        work = [part(after_core, n) for n in range(count)] + ([encoder] if beside else [])
        work += [part(after_one, n) for n in range(count)] + [part(after_two, n) for n in range(count)]
        first, last = self.points // 12, self.points - 1 - self.points // 12
        stages = [(0, begin)]
        for number, stage in enumerate(work):
            stages.append((first + number * (last - first) // max(len(work) - 1, 1), stage))
        return stages + [(-1, end)]


def gather_kernel(nz, tok, enc, own, everyone, encoded, qkv_out, send_sem, recv_sem, local_sem):
    my = Near(nz)
    x, c, z, y, backs = my.x, my.c, my.z, my.y, my.backs
    greet([my.by_x, my.by_core, my.diagonal, my.by_y, *my.by_z[1:]])
    copies = Copies(send_sem, recv_sem)
    local = [
        pltpu.make_async_copy(source, target, local_sem.at[n])
        for n, (source, target) in enumerate(
            [(own.at[x, c], qkv_out.at[x, c, z, y]), (tok, everyone.at[x, c]), (enc, encoded.at[x, c])]
        )
    ]
    for copy in local:
        copy.start()
    mine = lambda: qkv_out.at[x, c, z, y]
    first = [
        copies.add(lambda: own.at[1 - x, c], mine, my.by_x),
        copies.add(lambda: own.at[x, 1 - c], mine, my.by_core),
        copies.add(lambda: own.at[1 - x, 1 - c], mine, my.diagonal),
    ]
    rows = [(tok, everyone), (enc, encoded)]
    rows_x = [copies.add(lambda s=s: s, lambda t=t: t.at[x, c], my.by_x) for s, t in rows]
    rows_core = [copies.add(lambda s=s: s, lambda t=t: t.at[x, c], my.by_core) for s, t in rows]
    rows_far = [copies.add(lambda t=t: t.at[1 - x, c], lambda t=t: t.at[1 - x, c], my.by_core) for s, t in rows]
    line = [lambda t=t: qkv_out.at[:, :, backs[t], y] for t in range(nz)]
    by_z = [None] + [copies.add(line[0], line[0], my.by_z[t]) for t in range(1, nz)]
    by_y = [copies.add(line[t], line[t], my.by_y) for t in range(nz)]
    copies.start(*first, *rows_x, *rows_core)
    for copy in local:
        copy.wait()
    copies.arrive(*first)
    copies.start(*by_z[1:], by_y[0])
    for t in range(1, nz):
        copies.arrive(by_z[t])
        copies.start(by_y[t])
    for n in range(2):
        copies.arrive(rows_x[n])
        copies.start(rows_far[n])
    copies.arrive(*by_y, *rows_core, *rows_far)
    copies.finish()


def gather(nz, tok, enc, own):
    share, wide = own.shape[-2:]
    shapes = [
        jax.ShapeDtypeStruct((2, 2, *tok.shape), tok.dtype),
        jax.ShapeDtypeStruct((2, 2, *enc.shape), enc.dtype),
        jax.ShapeDtypeStruct((2, 2, nz, 2, share, wide), own.dtype),
    ]
    total = 9 + 2 * nz - 1
    return pl.pallas_call(
        functools.partial(gather_kernel, nz),
        in_specs=[whole()] * 3,
        out_specs=[whole(pl.ANY)] * 3,
        out_shape=shapes,
        scratch_shapes=[
            pltpu.SemaphoreType.DMA((total,)), pltpu.SemaphoreType.DMA((total,)), pltpu.SemaphoreType.DMA((3,)),
        ],
        compiler_params=pltpu.CompilerParams(collective_id=0, has_side_effects=True, vmem_limit_bytes=62 * 2**20),
        name="gather",
    )(tok, enc, own)


def reduce_kernel(nz, group_width, square, own, tok, gain, near, out_square, out_q, out_k, out_v, out_tok, out_gain, out_near, *refs):
    (a, ra, b, rb, d, rd, re, own_r, own_a, own_rz, own_f, own_in, tok_r, tok_a, tok_rx, gain_r, near_r,
     send_sem, recv_sem, gain_send, gain_recv) = refs
    my = Near(nz)
    x, c, z, y = my.x, my.c, my.z, my.y
    world, slots = 8 * nz, 2 * nz
    place, slot = lax.axis_index("seq"), lax.axis_index("fsdp")
    me = place * slots + slot
    barrier = pltpu.get_barrier_semaphore()

    @pl.loop(1, world)
    def _(t):
        other = lax.rem(me + t, world)
        pl.semaphore_signal(barrier, inc=1, device_id=(other // slots, lax.rem(other, slots)), device_id_type=MESH)

    pl.semaphore_wait(barrier, world - 1)
    copies = Copies(send_sem, recv_sem)
    add = copies.add
    half = tok.shape[2] // 2
    padded = own.shape[-1] // 3
    cut = lambda p: slice(p * half, (p + 1) * half)
    own_cut = lambda n: slice(n * padded, (n + 1) * padded)
    tok_core = [
        add(lambda h=h, p=p: tok.at[h, 1 - c, cut(p)], lambda h=h, p=p: tok_r.at[h, cut(p)], my.by_core)
        for h in (1 - x, x) for p in range(2)
    ]
    own_y = [
        add(lambda n=n: own.at[:, :, :, 1 - y, :, own_cut(n)], lambda n=n: own_r.at[n], my.by_y) for n in range(3)
    ]
    core = add(lambda: square.at[:, 1 - c], lambda: ra, my.by_core)
    near_all = [add(lambda: near, lambda t=t: near_r.at[t - 1], (place, lax.rem(slot + t, slots))) for t in range(1, slots)]
    tok_x = [add(lambda p=p: tok_a.at[1 - x, cut(p)], lambda p=p: tok_rx.at[cut(p)], my.by_x) for p in range(2)]
    one = add(lambda: a.at[:, 1 - y], lambda: rb, my.by_y)
    two = add(lambda: b.at[1 - x], lambda: rd, my.by_x)
    three = [add(lambda t=t: d.at[my.steps[t]], lambda t=t: re.at[t - 1], my.by_z[t]) for t in range(1, nz)]
    own_z = [
        [add(lambda n=n, t=t: own_a.at[n, :, :, my.steps[t]], lambda n=n, t=t: own_rz.at[n, t - 1], my.by_z[t]) for t in range(1, nz)]
        for n in range(3)
    ]
    landing = lambda: own_in.at[:, x, c]
    own_seq = [
        add(lambda: own_f.at[:, 1 - x, c], landing, my.by_x),
        add(lambda: own_f.at[:, x, 1 - c], landing, my.by_core),
        add(lambda: own_f.at[:, 1 - x, 1 - c], landing, my.diagonal),
    ]

    def gain_copy(t):
        other = lax.rem(me + t, world)
        return pltpu.make_async_remote_copy(
            src_ref=gain.at[other], dst_ref=gain_r.at[t - 1], send_sem=gain_send.at[t - 1], recv_sem=gain_recv.at[t - 1],
            device_id=(other // slots, lax.rem(other, slots)), device_id_type=MESH,
        )

    copies.start(own_y[0], *tok_core[:2], own_y[1], core, *tok_core[2:], own_y[2], *near_all)

    @pl.loop(1, world)
    def _(t):
        gain_copy(t).start()

    def tok_sum(h, p):
        add_low(tok_a.at[h, cut(p)], tok.at[h, c, cut(p)], tok_r.at[h, cut(p)])

    for p in range(2):
        copies.arrive(tok_core[p])
        tok_sum(1 - x, p)
        copies.start(tok_x[p])
    copies.arrive(core)
    for h in range(2):
        for side in range(2):
            add_low(a.at[h, side], square.at[h, c, :, side], ra.at[h, :, side])
    copies.start(one)

    def own_sum(n):
        copies.arrive(own_y[n])
        for h in range(2):
            for side in range(2):
                for k in range(nz):
                    own_a[n, h, side, k] = own[h, side, k, y, :, own_cut(n)] + own_r[n, h, side, k]
        copies.start(*own_z[n])

    own_sum(0)
    for p in range(2):
        copies.arrive(tok_core[2 + p])
        tok_sum(x, p)
    own_sum(1)
    own_sum(2)
    copies.arrive(one)
    for side in range(2):
        add_low(b.at[side], a.at[side, y], rb.at[side])
    copies.start(two)
    for n in range(3):
        copies.arrive(*own_z[n])
        for h in range(2):
            for side in range(2):
                total = own_a[n, h, side, z].astype(jnp.float32)
                for t in range(nz - 1):
                    total += own_rz[n, t, h, side].astype(jnp.float32)
                own_f[n, h, side] = total.astype(low)
    copies.start(*own_seq)
    own_in[:, x, c] = own_f[:, x, c]
    copies.arrive(two)
    add_low(d, b.at[x], rd)
    copies.start(*three)
    copies.arrive(*near_all)
    total = near[...]
    for t in range(slots - 1):
        total += near_r[t]
    out_near[...] = total
    out_gain[...] = gain[me]

    @pl.loop(1, world)
    def _(t):
        gain_copy(t).wait_recv()
        out_gain[...] += gain_r[t - 1]

    for p in range(2):
        copies.arrive(tok_x[p])
        add_low(out_tok.at[cut(p)], tok_a.at[x, cut(p)], tok_rx.at[cut(p)])
    copies.arrive(*own_seq)
    for n, out in enumerate((out_q, out_k, out_v)):
        parts = [own_in[n, s // 2, s % 2, :, :group_width].astype(jnp.float32) for s in range(4)]
        out[...] = jnp.concatenate(parts, axis=1)
    copies.arrive(*three)
    total = d[z].astype(jnp.float32)
    for t in range(nz - 1):
        total += re[t].astype(jnp.float32)
    out_square[...] = total
    copies.finish()

    @pl.loop(1, world)
    def _(t):
        gain_copy(t).wait_send()


def reduce(nz, group_width, square, own, tok, gain, near):
    share, width = square.shape[-2:]
    wide = own.shape[-1]
    vmem = lambda *shape: pltpu.VMEM(shape, low)
    slabs = tok.shape[2:]
    world = 8 * nz
    padded = wide // 3
    total = 4 + 3 + 1 + 2 * nz - 1 + 2 + 2 + nz - 1 + 3 * (nz - 1) + 3
    f32 = lambda *shape: jax.ShapeDtypeStruct(shape, jnp.float32)
    return pl.pallas_call(
        functools.partial(reduce_kernel, nz, group_width),
        in_specs=[whole()] * 5,
        out_specs=[whole()] * 7,
        out_shape=[f32(share, width)] * 4 + [f32(*slabs), f32(*gain.shape[1:]), f32(*near.shape)],
        scratch_shapes=[
            vmem(2, 2, nz, share, width), vmem(2, nz, 2, share, width), vmem(2, nz, share, width), vmem(2, nz, share, width),
            vmem(nz, share, width), vmem(nz, share, width), vmem(nz - 1, share, width),
            vmem(3, 2, 2, nz, share, padded), vmem(3, 2, 2, nz, share, padded), vmem(3, nz - 1, 2, 2, share, padded),
            vmem(3, 2, 2, share, padded), vmem(3, 2, 2, share, padded),
            vmem(2, *slabs), vmem(2, *slabs), vmem(*slabs),
            pltpu.VMEM((world - 1, *gain.shape[1:]), jnp.float32), pltpu.VMEM((2 * nz - 1, *near.shape), jnp.float32),
            pltpu.SemaphoreType.DMA((total,)), pltpu.SemaphoreType.DMA((total,)),
            pltpu.SemaphoreType.DMA((world - 1,)), pltpu.SemaphoreType.DMA((world - 1,)),
        ],
        compiler_params=pltpu.CompilerParams(collective_id=1, has_side_effects=True, vmem_limit_bytes=62 * 2**20),
        name="reduce",
    )(square, own, tok, gain, near)


def finish_kernel(
    slabs, x_ref, attended_ref, normed_ref, rows_ref, share_gain_ref, near_ref, map_ref, ffn_ref, enc_ref, early_ref, last_ref, *refs
):
    squares, refs = refs[:4], refs[4:]
    dx_ref, gain_ref, table_ref, gate_ref, up_ref, down_ref, enc_out = refs[:7]
    outs = refs[7:]
    values = x_ref[...].astype(jnp.float32)
    scale = scale_of(values)
    unit = values * scale
    grad_unit = normed_ref[...] * rows_ref[0:1, :]
    dx_ref[0] = attended_ref[...] + scale * (grad_unit - unit * jnp.mean(grad_unit * unit, axis=-1, keepdims=True))

    @pl.when(pl.program_id(0) == 0)
    def _():
        share, inner = gate_ref.shape
        width = down_ref.shape[1]
        for n in range(3):
            gain_ref[n : n + 1, :] = share_gain_ref[0:1, n * share : (n + 1) * share]
        table = lax.dot_general(
            map_ref[...], near_ref[...], (((1,), (1,)), ((), ())), precision=highest, preferred_element_type=jnp.float32
        )
        table_ref[...] = table[:, : table_ref.shape[1]]
        gate_ref[...] = ffn_ref[:, :inner].astype(jnp.float32)
        up_ref[...] = ffn_ref[:, inner : 2 * inner].astype(jnp.float32)
        for k in range(slabs):
            size = min(share, down_ref.shape[0] - k * share)
            column = 2 * inner + k * width
            down_ref[k * share : k * share + size] = ffn_ref[:size, column : column + width].astype(jnp.float32)
        enc_out[0] = enc_ref[...]
        for n, square in enumerate(squares):
            outs[n][...] = square[...]
        for n in range(3):
            outs[4 + n][...] = early_ref[n]
        outs[7][...] = last_ref[0]


def finish(tokens, grad_attended, grad_normed, gains, share_gains, by_distance, share_ffn, grad_encoded, early, last, squares, group, bins, sizes):
    rows, width = tokens.shape
    share, inner, hidden_share = sizes
    block = min(128, rows)
    place = np.arange(LANES)
    far = 16 + np.sum(place[:, None] >= bounds[None], axis=1)
    bucket = np.where(place < 16, place, far)
    table_map = (bucket[None] == np.arange(bins)[:, None]).astype(np.float32)
    table_map[bins - 1] = -(bucket < bins - 1).astype(np.float32)
    by_rows = pl.BlockSpec((block, width), lambda i: (i, 0))
    fixed = lambda shape: pl.BlockSpec(shape, lambda i: (0,) * len(shape))
    f32 = lambda *shape: jax.ShapeDtypeStruct(shape, jnp.float32)
    given = [gains, share_gains, by_distance, jnp.asarray(table_map), share_ffn, grad_encoded, early, last, *squares]
    made = [
        f32(3, share), f32(bins, group), f32(share, inner), f32(share, inner), f32(hidden_share, width),
        f32(1, *grad_encoded.shape), *[f32(share, width)] * 8,
    ]
    return pl.pallas_call(
        functools.partial(finish_kernel, -(-hidden_share // share)),
        grid=(rows // block,),
        in_specs=[by_rows] * 3 + [fixed(v.shape) for v in given],
        out_specs=[pl.BlockSpec((1, block, width), lambda i: (0, i, 0))] + [fixed(v.shape) for v in made],
        out_shape=[f32(1, rows, width), *made],
        compiler_params=pltpu.CompilerParams(vmem_limit_bytes=62 * 2**20),
        name="finish",
    )(tokens, grad_attended, grad_normed, *given)


def rms_norm(values, gain):
    scale = lax.rsqrt(jnp.mean(values * values, axis=-1, keepdims=True) + epsilon)
    return values * scale * gain


def rms_back(values, gain, grad_normed):
    scale = lax.rsqrt(jnp.mean(values * values, axis=-1, keepdims=True) + epsilon)
    unit = values * scale
    grad_unit = grad_normed * gain
    grad_gain = jnp.sum(grad_normed * unit, axis=0)
    grad_values = scale * (grad_unit - unit * jnp.mean(grad_unit * unit, axis=-1, keepdims=True))
    return (grad_values, grad_gain)


def activate(gate, upper):
    return jax.nn.gelu(gate, approximate=True) * upper


def per_device(
    tokens, encoder, cotangent, lengths, gains, self_query, self_key, self_value, self_output,
    cross_query, cross_key, cross_value, cross_output, ffn_gate, ffn_up, ffn_down, rel_bias,
):
    both = ("seq", "fsdp")
    seq, fsdp = lax.axis_size("seq"), lax.axis_size("fsdp")
    world = seq * fsdp
    nz = fsdp // 2
    share, width = self_query.shape
    hidden_share = ffn_down.shape[0]
    inner = ffn_gate.shape[1]
    rows = tokens.shape[1]
    group = rel_bias.shape[1]
    group_width = group * HEAD
    padded = -(-group_width // LANES) * LANES
    spare = padded - group_width
    heads = width // HEAD
    place = lax.axis_index("seq")
    aligned = share % 8 == 0

    slabs = -(-hidden_share // share)
    squares = jnp.stack([w.astype(low) for w in (self_output, cross_query, cross_key, cross_value)])
    if aligned:
        down = jnp.pad(ffn_down.astype(low), ((0, slabs * share - hidden_share), (0, 0))).reshape(slabs, share, width)
        wide_share = [cross_output.astype(low), *[down[k] for k in range(slabs)], ffn_gate.astype(low), ffn_up.astype(low)]
        wide_weights = lax.all_gather(jnp.concatenate(wide_share, axis=1), both, axis=0, tiled=True)
    else:
        gate_up = lax.all_gather(jnp.concatenate([ffn_gate.astype(low), ffn_up.astype(low)], axis=1), both, axis=0, tiled=True)
        w_down = lax.all_gather(ffn_down.astype(low), both, axis=0, tiled=True)
        c_output = lax.all_gather(cross_output.astype(low), both, axis=0, tiled=True)
    gain_columns = jnp.pad(gains.astype(low).T, ((0, 0), (0, spare - 3)))
    pieces = []
    for s in range(seq):
        for n, w in enumerate((self_query, self_key, self_value)):
            pieces.append(w[:, s * group_width : (s + 1) * group_width].astype(low))
            pieces.append(gain_columns if n == 0 else jnp.zeros((share, spare), low))
    own = jnp.concatenate(pieces, axis=1).reshape(share, seq, 3 * padded).transpose(1, 0, 2)
    if aligned:
        everyone, encoded, w_qkv = gather(nz, tokens[0], encoder[0], own.reshape(2, 2, share, 3 * padded))
    else:
        everyone = lax.all_gather(tokens[0], "seq", axis=0)
        encoded = lax.all_gather(encoder[0], "seq", axis=0)
        w_qkv = lax.all_to_all(own, "seq", split_axis=0, concat_axis=0, tiled=True)
        w_qkv = lax.all_gather(w_qkv, "fsdp", axis=1)
    everyone = everyone.reshape(seq * rows, width)
    encoded = encoded.reshape(-1, width)
    w_qkv = w_qkv.reshape(width, 3 * padded)
    length = lengths[0]
    values_in = tokens[0].astype(jnp.float32)
    qkv, normed_all, gain_rows = project(everyone, w_qkv, group_width)
    bias = bias_rows(rel_bias)
    plan = GatherPlan(nz, 4, share, width) if aligned else None
    own_mixed, own_logsum, *gathered = attend_forward(
        qkv, qkv, qkv, group, padded, bias, lengths, plan, (squares,) if aligned else ()
    )
    squares = gathered[0] if aligned else jnp.moveaxis(lax.all_gather(squares, both, axis=0), 1, 0)
    squares = squares.reshape(4, width, width)
    mixed = lax.all_to_all(own_mixed.reshape(seq, rows, padded), "seq", split_axis=0, concat_axis=0, tiled=True)
    cross_keys, cross_values = encode(encoded, squares)
    attended, normed_two, cross_queries = enter(tokens[0], mixed, squares, gain_rows, group_width)
    cross_mixed, cross_logsum = attend_forward(cross_queries, cross_keys, cross_values, heads)
    if aligned:
        scalars = jnp.stack([length, place * rows])
        result, grad_crossed, grad_cmixed, grad_coutput, gain_two, packed = middle(
            scalars, attended, cross_mixed, gain_rows, cotangent[0], wide_weights, inner, world
        )
        grad_gain_two = gain_two[0]
        packed = packed.reshape(width, -1)
    else:
        crossed = attended + nn(cross_mixed, c_output)
        normed_three = rms_norm(crossed, gain_rows[2]).astype(low)
        both_parts = nn(normed_three, gate_up)
        gate, upper = both_parts[:, :inner], both_parts[:, inner:]
        hidden = activate(gate, upper).astype(low)
        result = (crossed + nn(hidden, w_down)).astype(low)

        positions = place * rows + jnp.arange(rows, dtype=jnp.int32)
        grad_out = cotangent[0].astype(jnp.float32) * (positions < length).astype(jnp.float32)[:, None]
        grad_ffn = grad_out.astype(low)
        grad_hidden = nt(grad_ffn, w_down)
        _, pullback = jax.vjp(activate, gate, upper)
        grad_gate, grad_upper = pullback(grad_hidden)
        grad_both = jnp.concatenate([grad_gate.astype(low), grad_upper.astype(low)], axis=1)
        grad_down = tn(hidden, grad_ffn).astype(low).reshape(world, hidden_share, width)
        grad_down = jnp.pad(grad_down, ((0, 0), (0, slabs * share - hidden_share), (0, 0)))
        grad_down = grad_down.reshape(world, slabs, share, width).transpose(0, 2, 1, 3).reshape(world * share, slabs * width)
        packed = jnp.concatenate([tn(normed_three, grad_both).astype(low), grad_down], axis=1)

        grad_normed_three = nt(grad_both, gate_up)
        norm_part, grad_gain_two = rms_back(crossed, gain_rows[2], grad_normed_three)
        grad_crossed = grad_out + norm_part
        grad_branch = grad_crossed.astype(low)
        grad_coutput = tn(cross_mixed, grad_branch).astype(low)
        grad_cmixed = nt(grad_branch, c_output).astype(low)
    share_ffn = lax.psum_scatter(packed, both, scatter_dimension=0, tiled=True)
    slab = 64
    chunked = lambda g: g.reshape(2, 2, nz, 2, share, g.shape[-1])
    by_place = lambda g: g.reshape(2, 2, -1, slab, width)
    plan = ReducePlan(nz, 1, share, width, 4, heads) if aligned else None
    grad_cq, grad_ck, grad_cv, *first_sums = attend_backward(
        cross_queries, cross_keys, cross_values, grad_cmixed, cross_mixed, cross_logsum, heads,
        plan=plan, extra=(chunked(grad_coutput),) if aligned else (),
    )
    grad_attended, branch, grad_mixed, gain_one = leave(
        grad_cq, squares, attended, gain_rows, grad_crossed, seq, group_width, padded
    )
    grad_gain_one = gain_one[0]
    own_grad_mixed = lax.all_to_all(grad_mixed, "seq", split_axis=0, concat_axis=0, tiled=True).reshape(seq * rows, padded)
    grad_cquery, grad_ckey, grad_cvalue, grad_output, grad_encoded = square_terms(
        normed_two, grad_cq, encoded, grad_ck, grad_cv, squares, mixed, branch, group_width
    )
    early = [grad_cquery, grad_ckey, grad_cvalue]
    plan, extra = None, ()
    if aligned:
        extra = (*[chunked(g) for g in early], by_place(grad_encoded))
        plan = ReducePlan(nz, len(early), share, width, 3, 3 * BACKWARD_POINTS, extra[-1].shape[2:])
    own_dq, own_dk, own_dv, by_distance, *sums = attend_backward(
        qkv, qkv, qkv, own_grad_mixed, own_mixed, own_logsum, group, padded, bias, lengths, plan, extra
    )
    grad_normed_part, grad_own, gain_zero = unproject(everyone, normed_all, w_qkv, own_dq, own_dk, own_dv)
    grad_gain_zero = gain_zero[0]
    grad_gains = jnp.stack([grad_gain_zero, grad_gain_one, grad_gain_two])
    grad_gains = grad_gains.reshape(3, world, share).transpose(1, 0, 2).reshape(world, 1, 3 * share)
    grad_gains = jnp.pad(grad_gains, ((0, 0), (0, 7), (0, LANES - 3 * share)))
    wide = jnp.float32
    if aligned:
        share_output, *share_own, grad_normed, share_gains, by_distance = reduce(
            nz, group_width, chunked(grad_output), chunked(grad_own), by_place(grad_normed_part), grad_gains, by_distance
        )
        share_early, grad_encoded = sums
        grad_input, share_gains, table_grad, share_gate, share_up, share_down, grad_encoded, *shares = finish(
            tokens[0], grad_attended, grad_normed.reshape(rows, width), gain_rows, share_gains, by_distance, share_ffn,
            grad_encoded.reshape(-1, width), share_early, first_sums[0], (*share_own, share_output),
            group, rel_bias.shape[0], (share, inner, hidden_share),
        )
        return (
            result[None], grad_input, grad_encoded, share_gains, *shares, share_gate, share_up, share_down, table_grad,
        )
    else:
        scatter = lambda g, axes: lax.psum_scatter(g, axes, scatter_dimension=0, tiled=True)
        share_squares = scatter(jnp.concatenate([grad_output, *early, grad_coutput], axis=1), both).astype(wide)
        share_squares = [share_squares[:, n * width : (n + 1) * width] for n in range(5)]
        grad_own = scatter(grad_own.reshape(seq, fsdp, share, 3 * padded).transpose(1, 0, 2, 3), "fsdp")[0]
        grad_own = lax.all_to_all(grad_own, "seq", split_axis=0, concat_axis=0, tiled=True).astype(wide)
        grad_own = grad_own.reshape(seq, share, 3, padded)[:, :, :, :group_width].transpose(2, 1, 0, 3).reshape(3, share, width)
        share_own = [grad_own[n] for n in range(3)]
        grad_normed = scatter(grad_normed_part, "seq").astype(wide)
        grad_encoded = scatter(grad_encoded, "seq").astype(wide)
        share_gains = scatter(grad_gains, both)[0]
        by_distance = lax.psum(by_distance, "fsdp")
    share_gains = share_gains[0, : 3 * share].reshape(3, share)
    norm_part, _ = rms_back(values_in, gain_rows[0], grad_normed)
    grad_input = grad_attended + norm_part
    bins = rel_bias.shape[0]
    near_map = (buckets(jnp.arange(LANES, dtype=jnp.int32))[:, None] == jnp.arange(bins - 1, dtype=jnp.int32)[None]).astype(wide)
    near_sums = jnp.dot(near_map.T, by_distance[:group].T, precision=highest)
    table_grad = jnp.concatenate([near_sums, -jnp.sum(near_sums, axis=0, keepdims=True)], axis=0)
    share_ffn = share_ffn.astype(wide)
    share_down = share_ffn[:, 2 * inner :].reshape(share, slabs, width).transpose(1, 0, 2).reshape(slabs * share, width)
    return (
        result[None], grad_input[None], grad_encoded[None], share_gains, *share_own, *share_squares,
        share_ffn[:, :inner], share_ffn[:, inner : 2 * inner], share_down[:hidden_share], table_grad,
    )


def solution(mesh):
    split = P(("seq", "fsdp"), None)
    rows = P("fsdp", "seq", None)
    gains = P(None, ("seq", "fsdp"))
    return jax.shard_map(
        per_device,
        mesh=mesh,
        in_specs=(rows, rows, rows, P("fsdp"), gains, *([split] * 11), P(None, "seq")),
        out_specs=(rows, rows, rows, gains, *([split] * 11), P(None, "seq")),
        check_vma=False,
    )
```

```python
import functools

import jax
import jax.numpy as jnp
import numpy as np
from jax import lax
from jax.experimental import pallas as pl
from jax.experimental.pallas import tpu as pltpu
from jax.sharding import PartitionSpec as P

LANES = 128
BLOCK = 512
HEAD = 64
negative = -1e30
epsilon = 1e-06
highest = lax.Precision.HIGHEST
bounds = np.ceil(16.0 * 8.0 ** (np.arange(1, 16) / 16.0)).astype(np.int32)
low = jnp.bfloat16
MESH = pl.DeviceIdType.MESH


def nt(left, right):
    return lax.dot_general(left, right, (((1,), (1,)), ((), ())), preferred_element_type=jnp.float32)


def nn(left, right):
    return jnp.dot(left, right, preferred_element_type=jnp.float32)


def tn(left, right):
    return lax.dot_general(left, right, (((0,), (0,)), ((), ())), preferred_element_type=jnp.float32)


def buckets(distance):
    far = 16 + jnp.sum((distance[..., None] >= jnp.asarray(bounds)).astype(jnp.int32), axis=-1)
    return jnp.where(distance < 16, distance, far)


def bias_rows(table):
    count = table.shape[0]
    place = jnp.arange(3 * LANES, dtype=jnp.int32)
    onehot = buckets(jnp.clip(place, 0, 2 * LANES))[None, :] == jnp.arange(count, dtype=jnp.int32)[:, None]
    relative = table - table[count - 1 :]
    values = jnp.sum(jnp.where(onehot[:, None, :], relative[:, :, None], 0.0), axis=0)
    return jnp.where((place >= 2 * LANES)[None], negative, values)[:, None, :]


def head_place(heads):
    head = pl.program_id(0)
    per_tile = LANES // HEAD
    side = lax.rem(head, per_tile)
    lane = lax.broadcasted_iota(jnp.int32, (1, LANES), 1)
    return head, side == 0, (side == per_tile - 1) | (head == heads - 1), (lane // HEAD) == side


def bias_tiles(base_ref, t_scr):
    wide = jnp.broadcast_to(base_ref[0], (LANES, 3 * LANES))
    t_scr[...] = pltpu.roll(wide, 0, 1, stride=1, stride_axis=0)[:, : 2 * LANES]


def add_near(scores, t_scr):
    near = min(2 * LANES, scores.shape[1])
    fixed = scores[:, :near] + t_scr[:, :near]
    return fixed if near == scores.shape[1] else jnp.concatenate([fixed, scores[:, near:]], axis=1)


def add_corner(scores, t_scr):
    top, bottom = scores[:-LANES], scores[-LANES:]
    bottom = jnp.concatenate([bottom[:, :LANES] + t_scr[:, LANES:], bottom[:, LANES:]], axis=1)
    return jnp.concatenate([top, bottom], axis=0)


def at_step(head, stages, point, points):
    for due, stage in stages:
        if due >= 0 and due % points == point:
            pl.when(head == due // points)(stage)


def at_end(head, heads, stages):
    for due, stage in stages:
        if due < 0:
            pl.when(head == heads - 1)(stage)


FORWARD_POINTS = 4
BACKWARD_POINTS = 10


def attend_forward_kernel(*refs, causal, heads, plan):
    refs = list(refs)
    take = lambda n: [refs.pop(0) for _ in range(n)]
    if causal:
        (length_ref,) = take(1)
    q_ref, k_ref, v_ref = take(3)
    if causal:
        (base_ref,) = take(1)
    given = take(plan.inputs) if plan else []
    o_ref, lse_ref = take(2)
    made = take(plan.outputs) if plan else []
    s_scr, vt_scr, acc_scr, ot_scr = take(4)
    if causal:
        t_scr, mask_scr = take(2)
    stages = plan.stages(given, made, refs) if plan else []
    head, first, last, mask = head_place(heads)
    rows, keys = q_ref.shape[0], k_ref.shape[0]
    block = min(BLOCK, rows)
    if causal:
        bias_tiles(base_ref, t_scr)

        @pl.when(head == 0)
        def _():
            place = lax.broadcasted_iota(jnp.int32, (keys, LANES), 0)
            mask_scr[...] = jnp.where(place < length_ref[0], 0.0, negative)

    for at in range(0, keys, BLOCK):
        vt_scr[:, at : at + BLOCK] = jnp.where(mask, v_ref[at : at + BLOCK, :], 0).T

    def limit(scores, start):
        if start < BLOCK:
            return scores
        part = mask_scr[start : start + scores.shape[0], :]
        return scores + jnp.concatenate([part] * (scores.shape[1] // LANES), axis=1)

    for number in range(rows // block):
        at_step(head, stages, number, FORWARD_POINTS)
        start = number * block
        queries = jnp.where(mask, q_ref[start : start + block, :], 0)
        pieces = [(at, BLOCK, 0) for at in range(0, start if causal else keys, BLOCK)]
        if causal:
            pieces += [(start + part, LANES, part) for part in range(0, block, LANES)]
        largest = jnp.full((1, block), negative, jnp.float32)
        for at, size, skip in pieces:
            scores = nt(k_ref[at : at + size, :], queries[skip:])
            if causal:
                if size == LANES:
                    scores = add_near(scores, t_scr)
                elif at + size == start:
                    scores = add_corner(scores, t_scr)
                scores = limit(scores, at)
            s_scr[at : at + size, skip:] = scores
            top = jnp.maximum(largest[:, skip:], jnp.max(scores, axis=0, keepdims=True))
            largest = top if skip == 0 else jnp.concatenate([largest[:, :skip], top], axis=1)
        totals = jnp.zeros((1, block), jnp.float32)
        acc_scr[...] = jnp.zeros_like(acc_scr)
        for at, size, skip in pieces:
            expos = jnp.exp(s_scr[at : at + size, skip:] - largest[:, skip:])
            more = totals[:, skip:] + jnp.sum(expos, axis=0, keepdims=True)
            totals = more if skip == 0 else jnp.concatenate([totals[:, :skip], more], axis=1)
            acc_scr[:, skip:] += nn(vt_scr[:, at : at + size], expos.astype(low))
        lse_ref[0, :, start : start + block] = jnp.broadcast_to(largest + jnp.log(totals), (8, block))
        mixed = acc_scr[...] / totals
        ot_scr[:, start : start + block] = mixed + jnp.where(first, 0.0, ot_scr[:, start : start + block])

    @pl.when(last)
    def _():
        for at in range(0, rows, block):
            o_ref[at : at + block, :] = ot_scr[:, at : at + block].T.astype(low)

    if plan:
        per_tile = LANES // HEAD
        for tile in range(-(-heads // per_tile)):
            pl.when(head == min((tile + 1) * per_tile, heads) - 1)(functools.partial(plan.send, tile, o_ref))
    at_end(head, heads, stages)


def attend_specs(queries, keys, padded):
    rows = queries.shape[0]
    width = padded or queries.shape[1]
    count = keys.shape[0]
    per_tile = LANES // HEAD
    skip = padded // LANES
    row_spec = pl.BlockSpec((rows, LANES), lambda h: (0, h // per_tile))
    key_spec = pl.BlockSpec((count, LANES), lambda h: (0, h // per_tile))
    key_specs = [pl.BlockSpec((count, LANES), lambda h, n=n: (0, n * skip + h // per_tile)) for n in (1, 2)]
    return rows, width, count, row_spec, key_spec, key_specs


def attend_forward(queries, keys, values, heads, padded=0, bias=None, length=None, plan=None, extra=()):
    causal = bias is not None
    rows, width, count, row_spec, _, key_specs = attend_specs(queries, keys, padded)
    block = min(BLOCK, rows)
    in_specs = [row_spec, *key_specs]
    args = [queries, keys, values]
    scratch = [
        pltpu.VMEM((count, block), jnp.float32), pltpu.VMEM((LANES, count), low),
        pltpu.VMEM((LANES, block), jnp.float32), pltpu.VMEM((LANES, rows), jnp.float32),
    ]
    if causal:
        in_specs = [pl.BlockSpec(memory_space=pltpu.SMEM), *in_specs, pl.BlockSpec((1, 1, 3 * LANES), lambda h: (h, 0, 0))]
        args = [length, *args, bias]
        scratch += [pltpu.VMEM((LANES, 2 * LANES), jnp.float32), pltpu.VMEM((count, LANES), jnp.float32)]
    return pl.pallas_call(
        functools.partial(attend_forward_kernel, causal=causal, heads=heads, plan=plan),
        grid=(heads,),
        in_specs=in_specs + (plan.in_specs() if plan else []),
        out_specs=[row_spec, pl.BlockSpec((1, 8, rows), lambda h: (h, 0, 0))] + (plan.out_specs() if plan else []),
        out_shape=[
            jax.ShapeDtypeStruct((rows, width), low),
            jax.ShapeDtypeStruct((heads, 8, rows), jnp.float32),
        ] + (plan.out_shape() if plan else []),
        scratch_shapes=scratch + (plan.scratch() if plan else []),
        compiler_params=plan.params() if plan else pltpu.CompilerParams(vmem_limit_bytes=62 * 2**20),
        cost_estimate=pl.CostEstimate(
            flops=4 * heads * LANES * rows * count // (2 if causal else 1),
            bytes_accessed=4 * (rows + count) * width,
            transcendentals=heads * rows * count // (2 if causal else 1),
        ),
        name="self_forward" if causal else "cross_forward",
    )(*args, *extra)


def attend_backward_kernel(*refs, causal, heads, plan):
    refs = list(refs)
    take = lambda n: [refs.pop(0) for _ in range(n)]
    if causal:
        (length_ref,) = take(1)
    q_ref, k_ref, v_ref, do_ref, o_ref, lse_ref = take(6)
    if causal:
        (base_ref,) = take(1)
    given = take(plan.inputs) if plan else []
    dq_ref, dk_ref, dv_ref = take(3)
    if causal:
        (distance_ref,) = take(1)
    made = take(plan.outputs) if plan else []
    kt_scr, dqt_scr, dk_scr, dv_scr, row_scr = take(5)
    if causal:
        t_scr, near_scr = take(2)
    stages = plan.stages(given, made, refs) if plan else []
    head, first, last, mask = head_place(heads)
    rows, keys = q_ref.shape[0], k_ref.shape[0]
    block = min(BLOCK, rows)
    key_block = min(BLOCK, keys)

    @pl.when(first)
    def _():
        dqt_scr[...] = jnp.zeros_like(dqt_scr)
        dk_scr[...] = jnp.zeros_like(dk_scr)
        dv_scr[...] = jnp.zeros_like(dv_scr)

    if causal:
        bias_tiles(base_ref, t_scr)
        near_scr[...] = jnp.zeros_like(near_scr)
    for at in range(0, keys, key_block):
        kt_scr[:, at : at + key_block] = jnp.where(mask, k_ref[at : at + key_block, :], 0).T
    for start in range(0, rows, block):
        at = slice(start, start + block)
        product = do_ref[at, :].astype(jnp.float32) * o_ref[at, :].astype(jnp.float32)
        delta = jnp.sum(jnp.where(mask, product, 0.0).T, axis=0, keepdims=True)
        logsum = lse_ref[0, 0:1, at]
        if causal:
            place = start + lax.broadcasted_iota(jnp.int32, (1, block), 1)
            logsum = jnp.where(place < length_ref[0], logsum, -negative)
        row_scr[0:1, at] = logsum
        row_scr[1:2, at] = delta

    def piece(key_at, row_at, fix=None):
        queries = jnp.where(mask, q_ref[row_at, :], 0)
        grads = jnp.where(mask, do_ref[row_at, :], 0)
        scores = nt(k_ref[key_at, :], queries)
        if fix is not None:
            scores = fix(scores, t_scr)
        weights = jnp.exp(scores - row_scr[0:1, row_at])
        grad_weights = nt(v_ref[key_at, :], grads)
        grad_scores = weights * (grad_weights - row_scr[1:2, row_at])
        low_scores = grad_scores.astype(low)
        dv_scr[key_at, :] += nn(weights.astype(low), grads)
        dk_scr[key_at, :] += nn(low_scores, queries)
        dqt_scr[:, row_at] += nn(kt_scr[:, key_at], low_scores)
        return grad_scores

    point = 0
    if not causal:
        at_step(head, stages, 0, 1)
        for start in range(0, keys, key_block):
            for at in range(0, rows, block):
                piece(slice(start, start + key_block), slice(at, at + block))
    else:
        for start in range(0, keys, block):
            at_step(head, stages, point, BACKWARD_POINTS)
            point += 1
            for here in range(start, start + block, LANES):
                grad = piece(slice(here, here + LANES), slice(here, start + block), add_near)
                near = min(2 * LANES, grad.shape[1])
                near_scr[:, :near] += grad[:, :near]
            for at in range(start + block, rows, block):
                at_step(head, stages, point, BACKWARD_POINTS)
                point += 1
                beside = at == start + block
                grad = piece(slice(start, start + block), slice(at, at + block), add_corner if beside else None)
                if beside:
                    near_scr[:, LANES:] += grad[-LANES:, :LANES]
        flip = lax.broadcasted_iota(jnp.int32, (LANES, LANES), 0) + lax.broadcasted_iota(jnp.int32, (LANES, LANES), 1)
        flip = (flip == LANES - 1).astype(jnp.float32)
        turned = lax.dot_general(
            flip, near_scr[...], (((1,), (0,)), ((), ())), precision=highest, preferred_element_type=jnp.float32
        )
        turned = pltpu.roll(turned, 1, 1, stride=1, stride_axis=0)
        sums = jnp.sum(turned[:, LANES:], axis=0, keepdims=True)
        at_row = lax.broadcasted_iota(jnp.int32, (8, LANES), 0) == head
        before = jnp.where(head == 0, 0.0, distance_ref[...])
        distance_ref[...] = jnp.where(at_row, jnp.broadcast_to(sums, (8, LANES)), before)

    @pl.when(last)
    def _():
        for at in range(0, rows, block):
            dq_ref[at : at + block, :] = dqt_scr[:, at : at + block].T.astype(low)
        dk_ref[...] = dk_scr[...].astype(low)
        dv_ref[...] = dv_scr[...].astype(low)

    at_end(head, heads, stages)


def attend_backward(queries, keys, values, grad_mixed, mixed, logsum, heads, padded=0, bias=None, length=None, plan=None, extra=()):
    causal = bias is not None
    rows, width, count, row_spec, key_spec, key_specs = attend_specs(queries, keys, padded)
    in_specs = [row_spec, *key_specs, row_spec, row_spec, pl.BlockSpec((1, 8, rows), lambda h: (h, 0, 0))]
    args = [queries, keys, values, grad_mixed, mixed, logsum]
    out_specs = [row_spec, key_spec, key_spec]
    out_shape = [jax.ShapeDtypeStruct((n, width), low) for n in (rows, count, count)]
    scratch = [
        pltpu.VMEM((LANES, count), low), pltpu.VMEM((LANES, rows), jnp.float32),
        pltpu.VMEM((count, LANES), jnp.float32), pltpu.VMEM((count, LANES), jnp.float32), pltpu.VMEM((8, rows), jnp.float32),
    ]
    if causal:
        in_specs = [pl.BlockSpec(memory_space=pltpu.SMEM), *in_specs, pl.BlockSpec((1, 1, 3 * LANES), lambda h: (h, 0, 0))]
        args = [length, *args, bias]
        out_specs += [pl.BlockSpec((8, LANES), lambda h: (0, 0))]
        out_shape += [jax.ShapeDtypeStruct((8, LANES), jnp.float32)]
        scratch += [pltpu.VMEM((LANES, 2 * LANES), jnp.float32), pltpu.VMEM((LANES, 2 * LANES), jnp.float32)]
    return pl.pallas_call(
        functools.partial(attend_backward_kernel, causal=causal, heads=heads, plan=plan),
        grid=(heads,),
        in_specs=in_specs + (plan.in_specs() if plan else []),
        out_specs=out_specs + (plan.out_specs() if plan else []),
        out_shape=out_shape + (plan.out_shape() if plan else []),
        scratch_shapes=scratch + (plan.scratch() if plan else []),
        compiler_params=plan.params() if plan else pltpu.CompilerParams(vmem_limit_bytes=62 * 2**20),
        cost_estimate=pl.CostEstimate(
            flops=10 * heads * LANES * rows * count // (2 if causal else 1),
            bytes_accessed=8 * (rows + count) * width,
            transcendentals=heads * rows * count // (2 if causal else 1),
        ),
        name="self_backward" if causal else "cross_backward",
    )(*args, *extra)


def scale_of(values):
    return lax.rsqrt(jnp.mean(values * values, axis=-1, keepdims=True) + epsilon)


def project_kernel(gain_lane, x_ref, w_ref, qkv_ref, normed_ref, gains_ref):
    @pl.when(pl.program_id(0) == 0)
    def _():
        tile = gain_lane // LANES * LANES
        turned = w_ref[:, tile : tile + LANES].astype(jnp.float32).T
        first = gain_lane - tile
        gains_ref[...] = turned[first : first + 8]

    values = x_ref[...].astype(jnp.float32)
    normed = (values * scale_of(values) * gains_ref[0:1, :]).astype(low)
    normed_ref[...] = normed
    qkv_ref[...] = nn(normed, w_ref[...]).astype(low)


def project(everyone, w_qkv, gain_lane):
    count, width = everyone.shape
    wide = w_qkv.shape[1]
    block = min(BLOCK, count)
    rows = lambda n: pl.BlockSpec((block, n), lambda i: (i, 0))
    return pl.pallas_call(
        functools.partial(project_kernel, gain_lane),
        grid=(count // block,),
        in_specs=[rows(width), pl.BlockSpec((width, wide), lambda i: (0, 0))],
        out_specs=[rows(wide), rows(width), pl.BlockSpec((8, width), lambda i: (0, 0))],
        out_shape=[
            jax.ShapeDtypeStruct((count, wide), low), jax.ShapeDtypeStruct((count, width), low),
            jax.ShapeDtypeStruct((8, width), jnp.float32),
        ],
        compiler_params=pltpu.CompilerParams(vmem_limit_bytes=62 * 2**20),
        name="project",
    )(everyone, w_qkv)


def unproject_kernel(x_ref, normed_ref, w_ref, dq_ref, dk_ref, dv_ref, part_ref, own_ref, gain_ref, own_scr):
    step = pl.program_id(0)
    padded = dq_ref.shape[1]
    grads = [r[...] for r in (dq_ref, dk_ref, dv_ref)]
    part = sum(nt(g, w_ref[:, n * padded : (n + 1) * padded]) for n, g in enumerate(grads))
    values = x_ref[...].astype(jnp.float32)
    share = jnp.sum(part * (values * scale_of(values)), axis=0, keepdims=True)
    part_ref[...] = part.astype(low)
    turned = normed_ref[...].T

    @pl.when(step == 0)
    def _():
        gain_ref[...] = jnp.zeros_like(gain_ref)
        own_scr[...] = jnp.zeros_like(own_scr)

    gain_ref[...] += jnp.broadcast_to(share, gain_ref.shape)
    for n, g in enumerate(grads):
        own_scr[:, n * padded : (n + 1) * padded] += nn(turned, g)

    @pl.when(step == pl.num_programs(0) - 1)
    def _():
        own_ref[...] = own_scr[...].astype(low)


def unproject(everyone, normed, w_qkv, dq, dk, dv):
    count, width = everyone.shape
    wide, padded = w_qkv.shape[1], dq.shape[1]
    block = min(BLOCK, count)
    rows = lambda n: pl.BlockSpec((block, n), lambda i: (i, 0))
    fixed = lambda a, b: pl.BlockSpec((a, b), lambda i: (0, 0))
    return pl.pallas_call(
        unproject_kernel,
        grid=(count // block,),
        in_specs=[rows(width), rows(width), fixed(width, wide), rows(padded), rows(padded), rows(padded)],
        out_specs=[rows(width), fixed(width, wide), fixed(8, width)],
        out_shape=[
            jax.ShapeDtypeStruct((count, width), low), jax.ShapeDtypeStruct((width, wide), low),
            jax.ShapeDtypeStruct((8, width), jnp.float32),
        ],
        scratch_shapes=[pltpu.VMEM((width, wide), jnp.float32)],
        compiler_params=pltpu.CompilerParams(vmem_limit_bytes=62 * 2**20),
        name="unproject",
    )(everyone, normed, w_qkv, dq, dk, dv)


slope = float(np.sqrt(2.0 / np.pi))
cubic = 0.044715


def middle_kernel(
    slabs, scalars, x1_ref, mixed_ref, co_ref, gains_ref, cot_ref, gate_ref, up_ref, *refs
):
    slab_refs, refs = refs[:slabs], refs[slabs:]
    out_ref, dx_ref, dm_ref, co_grad_ref, gain_ref, packed = refs[:6]
    x2_scr, n3_scr, n3t_scr, df_scr, result_scr, dn_scr, down_ref, gate_buf, up_buf, down_buf, sem = refs[6:]
    step, steps = pl.program_id(0), pl.num_programs(0)
    rows, width = x1_ref.shape
    block = gate_ref.shape[1]
    world, share = packed.shape[:2]
    inner = block * steps
    owners = down_buf.shape[1]
    hidden_share = block // owners

    @pl.when(step == 0)
    def _():
        x2 = x1_ref[...] + nn(mixed_ref[...], co_ref[...])
        x2_scr[...] = x2
        normed = (x2 * scale_of(x2) * gains_ref[2:3, :]).astype(low)
        n3_scr[...] = normed
        n3t_scr[...] = normed.T
        place = scalars[1] + lax.broadcasted_iota(jnp.int32, (rows, 1), 0)
        df_scr[...] = jnp.where(place < scalars[0], cot_ref[...], 0)
        result_scr[...] = x2
        dn_scr[...] = jnp.zeros_like(dn_scr)
        down_buf[...] = jnp.zeros_like(down_buf)

    for o in range(owners):
        for k in range(slabs):
            size = min(share, hidden_share - k * share)
            start = o * hidden_share + k * share
            down_ref[start : start + size] = slab_refs[k][o, :size]

    normed, df = n3_scr[...], df_scr[...]
    gate, upper = nn(normed, gate_ref[...]), nn(normed, up_ref[...])
    bent = jnp.tanh(slope * (gate + cubic * (gate * gate * gate)))
    half = 0.5 * (1.0 + bent)
    active = gate * half
    hidden = (active * upper).astype(low)
    result_scr[...] += nn(hidden, down_ref[...])
    grad_hidden = nt(df, down_ref[...])
    rise = half + (0.5 * gate) * ((1.0 - bent * bent) * (slope + (3.0 * cubic * slope) * (gate * gate)))
    grad_gate = (grad_hidden * upper * rise).astype(low)
    grad_upper = (grad_hidden * active).astype(low)
    dn_scr[...] += nt(grad_gate, gate_ref[...]) + nt(grad_upper, up_ref[...])
    slot = lax.rem(step, 2)

    def sends(at, which):
        first = pl.multiple_of(at * block, LANES)
        yield pltpu.make_async_copy(gate_buf.at[which], packed.at[:, :, pl.ds(first, block)], sem.at[which, 0])
        yield pltpu.make_async_copy(up_buf.at[which], packed.at[:, :, pl.ds(pl.multiple_of(inner + at * block, LANES), block)], sem.at[which, 1])
        for k in range(slabs):
            column = 2 * inner + k * width
            yield pltpu.make_async_copy(
                down_buf.at[which, :, k], packed.at[pl.ds(at * owners, owners), :, column : column + width], sem.at[which, 2 + k]
            )

    @pl.when(step >= 2)
    def _():
        for copy in sends(step - 2, slot):
            copy.wait()

    turned = n3t_scr[...]
    gate_buf[slot] = nn(turned, grad_gate).reshape(world, share, block).astype(low)
    up_buf[slot] = nn(turned, grad_upper).reshape(world, share, block).astype(low)
    grad_down = tn(hidden, df)
    for o in range(owners):
        for k in range(slabs):
            size = min(share, hidden_share - k * share)
            start = o * hidden_share + k * share
            down_buf[slot, o, k, :size] = grad_down[start : start + size].astype(low)
    for copy in sends(step, slot):
        copy.start()

    @pl.when(step == steps - 1)
    def _():
        out_ref[...] = result_scr[...].astype(low)
        x2, grad_normed = x2_scr[...], dn_scr[...]
        scale = scale_of(x2)
        unit = x2 * scale
        grad_unit = grad_normed * gains_ref[2:3, :]
        gain_ref[...] = jnp.broadcast_to(jnp.sum(grad_normed * unit, axis=0, keepdims=True), gain_ref.shape)
        back = scale * (grad_unit - unit * jnp.mean(grad_unit * unit, axis=-1, keepdims=True))
        dx = df.astype(jnp.float32) + back
        dx_ref[...] = dx
        branch = dx.astype(low)
        dm_ref[...] = nt(branch, co_ref[...]).astype(low)
        co_grad_ref[...] = tn(mixed_ref[...], branch).astype(low)
        if steps > 1:
            for copy in sends(step - 1, 1 - slot):
                copy.wait()
        for copy in sends(step, slot):
            copy.wait()


def middle(scalars, x1, mixed, gains, cotangent, weights, inner, world):
    rows, width = x1.shape
    block = min(BLOCK, inner)
    steps = inner // block
    share, hidden_share = width // world, inner // world
    slabs = -(-hidden_share // share)
    owners = block // hidden_share
    ahead = (1 + slabs) * width // block
    fixed = lambda *shape: pl.BlockSpec(shape, lambda j: (0,) * len(shape))
    f32 = jnp.float32
    return pl.pallas_call(
        functools.partial(middle_kernel, slabs),
        grid=(steps,),
        in_specs=[
            pl.BlockSpec(memory_space=pltpu.SMEM), fixed(rows, width), fixed(rows, width), fixed(width, width),
            fixed(8, width), fixed(rows, width),
            pl.BlockSpec((width, block), lambda j: (0, ahead + j)), pl.BlockSpec((width, block), lambda j: (0, ahead + steps + j)),
            *[pl.BlockSpec((owners, share, width), lambda j, k=k: (j, 0, 1 + k)) for k in range(slabs)],
        ],
        out_specs=[
            fixed(rows, width), fixed(rows, width), fixed(rows, width), fixed(width, width), fixed(8, width),
            pl.BlockSpec(memory_space=pl.ANY),
        ],
        out_shape=[
            jax.ShapeDtypeStruct((rows, width), low), jax.ShapeDtypeStruct((rows, width), f32),
            jax.ShapeDtypeStruct((rows, width), low), jax.ShapeDtypeStruct((width, width), low),
            jax.ShapeDtypeStruct((8, width), f32),
            jax.ShapeDtypeStruct((world, share, 2 * inner + slabs * width), low),
        ],
        scratch_shapes=[
            pltpu.VMEM((rows, width), f32), pltpu.VMEM((rows, width), low), pltpu.VMEM((width, rows), low),
            pltpu.VMEM((rows, width), low), pltpu.VMEM((rows, width), f32), pltpu.VMEM((rows, width), f32),
            pltpu.VMEM((block, width), low),
            pltpu.VMEM((2, world, share, block), low), pltpu.VMEM((2, world, share, block), low),
            pltpu.VMEM((2, owners, slabs, share, width), low), pltpu.SemaphoreType.DMA((2, 2 + slabs)),
        ],
        compiler_params=pltpu.CompilerParams(vmem_limit_bytes=62 * 2**20),
        cost_estimate=pl.CostEstimate(
            flops=2 * rows * width * (9 * inner + 3 * width), transcendentals=rows * inner, bytes_accessed=26 * width * inner // 4
        ),
        name="middle",
    )(scalars, x1, mixed, weights, gains, cotangent, weights, weights, *[weights.reshape(world, share, -1)] * slabs)


def encode_kernel(enc_ref, w_ref, key_ref, value_ref):
    for n, out in enumerate((key_ref, value_ref)):
        out[...] = nn(enc_ref[...], w_ref[n]).astype(low)


def encode(encoded, squares):
    count, width = encoded.shape
    part = width // 3
    columns = pl.BlockSpec((count, part), lambda j: (0, j))
    return pl.pallas_call(
        encode_kernel,
        grid=(3,),
        in_specs=[pl.BlockSpec((count, width), lambda j: (0, 0)), pl.BlockSpec((2, width, part), lambda j: (1, 0, j))],
        out_specs=[columns] * 2,
        out_shape=[jax.ShapeDtypeStruct((count, width), low)] * 2,
        compiler_params=pltpu.CompilerParams(vmem_limit_bytes=62 * 2**20),
        cost_estimate=pl.CostEstimate(flops=4 * count * width * width, transcendentals=0, bytes_accessed=8 * width * width),
        name="encode",
    )(encoded, squares)


def enter_kernel(group_width, x_ref, mixed_ref, w_ref, gains_ref, attended_ref, normed_ref, query_ref):
    total = x_ref[...].astype(jnp.float32)
    for s in range(mixed_ref.shape[0]):
        total += nn(mixed_ref[s, :, :group_width], w_ref[0, s * group_width : (s + 1) * group_width])
    attended_ref[...] = total
    normed = (total * scale_of(total) * gains_ref[1:2, :]).astype(low)
    normed_ref[...] = normed
    query_ref[...] = nn(normed, w_ref[1]).astype(low)


def enter(tokens, mixed, squares, gains, group_width):
    rows, width = tokens.shape
    seq, _, padded = mixed.shape
    block = min(256, rows)
    by_rows = pl.BlockSpec((block, width), lambda i: (i, 0))
    return pl.pallas_call(
        functools.partial(enter_kernel, group_width),
        grid=(rows // block,),
        in_specs=[
            by_rows, pl.BlockSpec((seq, block, padded), lambda i: (0, i, 0)), pl.BlockSpec((2, width, width), lambda i: (0, 0, 0)),
            pl.BlockSpec((8, width), lambda i: (0, 0)),
        ],
        out_specs=[by_rows] * 3,
        out_shape=[jax.ShapeDtypeStruct((rows, width), t) for t in (jnp.float32, low, low)],
        compiler_params=pltpu.CompilerParams(vmem_limit_bytes=62 * 2**20),
        cost_estimate=pl.CostEstimate(flops=4 * rows * width * width, transcendentals=0, bytes_accessed=12 * width * width),
        name="enter",
    )(tokens, mixed, squares, gains)


def leave_kernel(group_width, grad_ref, w_ref, attended_ref, gains_ref, dx_ref, total_ref, branch_ref, dm_ref, gain_ref):
    @pl.when(pl.program_id(0) == 0)
    def _():
        gain_ref[...] = jnp.zeros_like(gain_ref)

    grad_normed = nt(grad_ref[...], w_ref[1])
    values = attended_ref[...]
    scale = scale_of(values)
    unit = values * scale
    grad_unit = grad_normed * gains_ref[1:2, :]
    gain_ref[...] += jnp.broadcast_to(jnp.sum(grad_normed * unit, axis=0, keepdims=True), gain_ref.shape)
    total = dx_ref[...] + scale * (grad_unit - unit * jnp.mean(grad_unit * unit, axis=-1, keepdims=True))
    total_ref[...] = total
    branch = total.astype(low)
    branch_ref[...] = branch
    for s in range(dm_ref.shape[0]):
        dm_ref[s, :, :group_width] = nt(branch, w_ref[0, s * group_width : (s + 1) * group_width]).astype(low)
        if dm_ref.shape[2] > group_width:
            dm_ref[s, :, group_width:] = jnp.zeros((branch.shape[0], dm_ref.shape[2] - group_width), low)


def leave(grad_queries, squares, attended, gains, grad_crossed, seq, group_width, padded):
    rows, width = grad_queries.shape
    block = min(256, rows)
    by_rows = pl.BlockSpec((block, width), lambda i: (i, 0))
    fixed = pl.BlockSpec((8, width), lambda i: (0, 0))
    return pl.pallas_call(
        functools.partial(leave_kernel, group_width),
        grid=(rows // block,),
        in_specs=[by_rows, pl.BlockSpec((2, width, width), lambda i: (0, 0, 0)), by_rows, fixed, by_rows],
        out_specs=[by_rows, by_rows, pl.BlockSpec((seq, block, padded), lambda i: (0, i, 0)), fixed],
        out_shape=[
            jax.ShapeDtypeStruct((rows, width), jnp.float32), jax.ShapeDtypeStruct((rows, width), low),
            jax.ShapeDtypeStruct((seq, rows, padded), low), jax.ShapeDtypeStruct((8, width), jnp.float32),
        ],
        compiler_params=pltpu.CompilerParams(vmem_limit_bytes=62 * 2**20),
        cost_estimate=pl.CostEstimate(flops=4 * rows * width * width, transcendentals=0, bytes_accessed=16 * width * width),
        name="leave",
    )(grad_queries, squares, attended, gains, grad_crossed)


def square_terms_kernel(group_width, normed, grad_q, encoded, grad_k, grad_v, w_ref, mixed, branch, q_out, k_out, v_out, o_out, e_out, *scratch):
    normed_t, encoded_t, mixed_t, total = scratch
    step = pl.program_id(0)

    @pl.when(step == 0)
    def _():
        normed_t[...] = normed[...].T
        encoded_t[...] = encoded[...].T
        for s in range(mixed.shape[0]):
            mixed_t[s * group_width : (s + 1) * group_width] = mixed[s].T[:group_width]
        total[...] = jnp.zeros_like(total)

    q_out[...] = nn(normed_t[...], grad_q[...]).astype(low)
    k_out[...] = nn(encoded_t[...], grad_k[...]).astype(low)
    v_out[...] = nn(encoded_t[...], grad_v[...]).astype(low)
    o_out[...] = nn(mixed_t[...], branch[...]).astype(low)
    total[...] += nt(grad_k[...], w_ref[0]) + nt(grad_v[...], w_ref[1])

    @pl.when(step == pl.num_programs(0) - 1)
    def _():
        e_out[...] = total[...].astype(low)


def square_terms(normed, grad_q, encoded, grad_k, grad_v, squares, mixed, branch, group_width):
    rows, width = normed.shape
    count = encoded.shape[0]
    part = width // 3
    fixed = lambda v: pl.BlockSpec(v.shape, lambda j: (0,) * v.ndim)
    columns = lambda n: pl.BlockSpec((n, part), lambda j: (0, j))
    return pl.pallas_call(
        functools.partial(square_terms_kernel, group_width),
        grid=(3,),
        in_specs=[
            fixed(normed), columns(rows), fixed(encoded), columns(count), columns(count),
            pl.BlockSpec((2, width, part), lambda j: (1, 0, j)), fixed(mixed), columns(rows),
        ],
        out_specs=[columns(width)] * 4 + [fixed(encoded)],
        out_shape=[jax.ShapeDtypeStruct((width, width), low)] * 4 + [jax.ShapeDtypeStruct((count, width), low)],
        scratch_shapes=[
            pltpu.VMEM((width, rows), low), pltpu.VMEM((width, count), low), pltpu.VMEM((width, rows), low),
            pltpu.VMEM((count, width), jnp.float32),
        ],
        compiler_params=pltpu.CompilerParams(vmem_limit_bytes=62 * 2**20),
        cost_estimate=pl.CostEstimate(flops=12 * rows * width * width, transcendentals=0, bytes_accessed=24 * width * width),
        name="square_terms",
    )(normed, grad_q, encoded, grad_k, grad_v, squares, mixed, branch)


def coordinates():
    place, slot = lax.axis_index("seq"), lax.axis_index("fsdp")
    return place // 2, lax.rem(place, 2), slot // 2, lax.rem(slot, 2)


def device(x, c, z, y):
    return (x * 2 + c, z * 2 + y)


class Near:
    def __init__(self, nz):
        self.nz = nz
        x, c, z, y = self.x, self.c, self.z, self.y = coordinates()
        self.by_x, self.by_core, self.by_y = device(1 - x, c, z, y), device(x, 1 - c, z, y), device(x, c, z, 1 - y)
        self.diagonal = device(1 - x, 1 - c, z, y)
        self.steps = [lax.rem(z + t, nz) for t in range(nz)]
        self.backs = [lax.rem(z - t + nz, nz) for t in range(nz)]
        self.by_z = [device(x, c, self.steps[t], y) for t in range(nz)]


def greet(others):
    barrier = pltpu.get_barrier_semaphore()
    for other in others:
        pl.semaphore_signal(barrier, inc=1, device_id=other, device_id_type=MESH)
    pl.semaphore_wait(barrier, len(others))


class Copies:
    def __init__(self, send_sem, recv_sem):
        self.send_sem, self.recv_sem, self.made = send_sem, recv_sem, []

    def add(self, source, target, other):
        self.made.append((source, target, other))
        return len(self.made) - 1

    def copy(self, number):
        source, target, other = self.made[number]
        return pltpu.make_async_remote_copy(
            src_ref=source(), dst_ref=target(), send_sem=self.send_sem.at[number], recv_sem=self.recv_sem.at[number],
            device_id=other, device_id_type=MESH,
        )

    def start(self, *numbers):
        for number in numbers:
            self.copy(number).start()

    def arrive(self, *numbers):
        for number in numbers:
            self.copy(number).wait_recv()

    def finish(self):
        for number in range(len(self.made)):
            self.copy(number).wait_send()


def add_low(target, left, right):
    count = left.shape[0]
    unroll = 4 if count % 4 == 0 else 1

    @pl.loop(0, count // unroll)
    def _(n):
        for k in range(unroll):
            at = n * unroll + k
            if target.dtype == low:
                target[at] = left[at] + right[at]
            else:
                target[at] = left[at].astype(target.dtype) + right[at].astype(target.dtype)


def whole(space=pltpu.VMEM):
    return pl.BlockSpec(memory_space=space)


class GatherPlan:
    inputs, outputs = 1, 2

    def __init__(self, nz, count, share, width, rows, tiles):
        self.nz, self.count, self.share, self.width, self.rows, self.tiles = nz, count, share, width, rows, tiles
        self.total = 8 * nz - 1 + 3 * tiles

    def in_specs(self):
        return [whole()]

    def out_specs(self):
        return [whole(pl.ANY)] * 2

    def out_shape(self):
        return [
            jax.ShapeDtypeStruct((self.count, 2, 2, self.nz, 2, self.share, self.width), low),
            jax.ShapeDtypeStruct((2, 2, self.rows, self.tiles * LANES), low),
        ]

    def scratch(self):
        sems = [pltpu.SemaphoreType.DMA((n,)) for n in (self.total, self.total, 1 + self.tiles)]
        return [pltpu.VMEM((self.tiles, 2, 2, self.rows, LANES), low), *sems]

    def params(self):
        return pltpu.CompilerParams(collective_id=2, has_side_effects=True, vmem_limit_bytes=62 * 2**20)

    def stages(self, given, made, scratch):
        (src,), (out, got), (parts, send_sem, recv_sem, local_sem) = given, made, scratch
        nz, my = self.nz, Near(self.nz)
        x, c, z, y, backs = my.x, my.c, my.z, my.y, my.backs
        copies = Copies(send_sem, recv_sem)
        own = lambda: src
        at = lambda xx, cc, zz, yy: lambda: out.at[:, xx, cc, zz, yy]
        mine = at(x, c, z, y)
        by_z = [None] + [copies.add(own, mine, my.by_z[t]) for t in range(1, nz)]
        held = [mine if t == 0 else at(x, c, backs[t], y) for t in range(nz)]
        source = [own if t == 0 else held[t] for t in range(nz)]
        by_y = [copies.add(source[t], held[t], my.by_y) for t in range(nz)]
        by_x = [copies.add(source[t], held[t], my.by_x) for t in range(nz)]
        by_core = [copies.add(source[t], held[t], my.by_core) for t in range(nz)]
        from_x = [at(1 - x, c, backs[t], y) for t in range(nz)]
        from_y = [at(x, c, backs[t], 1 - y) for t in range(nz)]
        far = [at(1 - x, c, backs[t], 1 - y) for t in range(nz)]
        corner = [
            copies.add(from_x[t], from_x[t], my.by_y) if t % 2 == 0 else copies.add(from_y[t], from_y[t], my.by_x)
            for t in range(nz)
        ]
        core_x = [copies.add(from_x[t], from_x[t], my.by_core) for t in range(nz)]
        core_y = [copies.add(from_y[t], from_y[t], my.by_core) for t in range(nz)]
        core_far = [copies.add(far[t], far[t], my.by_core) for t in range(nz)]
        local = lambda: pltpu.make_async_copy(src, mine(), local_sem.at[0])
        lands = [lambda t=t: got.at[x, c, :, t * LANES : (t + 1) * LANES] for t in range(self.tiles)]
        exchange = [
            [
                copies.add(lambda t=t: parts.at[t, 1 - x, c], lands[t], my.by_x),
                copies.add(lambda t=t: parts.at[t, x, 1 - c], lands[t], my.by_core),
                copies.add(lambda t=t: parts.at[t, 1 - x, 1 - c], lands[t], my.diagonal),
            ]
            for t in range(self.tiles)
        ]
        keep = lambda t: pltpu.make_async_copy(parts.at[t, x, c], lands[t](), local_sem.at[1 + t])

        def send(tile, mixed):
            for s in range(4):
                parts[tile, s // 2, s % 2] = mixed[s * self.rows : (s + 1) * self.rows, :]
            copies.start(*exchange[tile])
            keep(tile).start()

        self.send = send

        def begin():
            greet([my.by_x, my.by_core, my.diagonal, my.by_y, *my.by_z[1:]])
            copies.start(*by_z[1:], by_y[0], by_x[0], by_core[0])
            local().start()

        def line(t):
            copies.arrive(by_z[t])
            copies.start(by_y[t], by_x[t], by_core[t])

        def plane(t):
            copies.arrive(by_x[t])
            copies.start(*([corner[t]] if t % 2 == 0 else []), core_x[t])
            copies.arrive(by_y[t])
            copies.start(*([corner[t]] if t % 2 == 1 else []), core_y[t])

        def turn(t):
            copies.arrive(corner[t])
            copies.start(core_far[t])

        def end():
            local().wait()
            copies.arrive(*by_core, *core_x, *core_y, *core_far)
            for tile in range(self.tiles):
                copies.arrive(*exchange[tile])
                keep(tile).wait()
            copies.finish()

        work = [functools.partial(line, t) for t in range(1, nz)]
        work += [functools.partial(plane, t) for t in range(nz)] + [functools.partial(turn, t) for t in range(nz)]
        points = 3 * FORWARD_POINTS - 1
        stages = [(0, begin)]
        for number, stage in enumerate(work):
            stages.append((1 + number * points // (len(work) + 1), stage))
        return stages + [(-1, end)]


class ReducePlan:
    def __init__(self, nz, count, share, width, number, points, slabs=None):
        self.nz, self.count, self.share, self.width, self.slabs = nz, count, share, width, slabs
        self.number, self.points = number, points
        self.inputs = count + (slabs is not None)
        self.outputs = 1 + (slabs is not None)
        self.total = count * (nz + 1) + count + 2 * (slabs is not None)

    def in_specs(self):
        return [whole()] * self.inputs

    def out_specs(self):
        return [whole()] * self.outputs

    def out_shape(self):
        shapes = [jax.ShapeDtypeStruct((self.count, self.share, self.width), jnp.float32)]
        return shapes + ([jax.ShapeDtypeStruct(self.slabs, jnp.float32)] if self.slabs else [])

    def scratch(self):
        nz, tail = self.nz, (self.share, self.width)
        vmem = lambda *shape: pltpu.VMEM((self.count, *shape, *tail), low)
        slabs = [pltpu.VMEM((*lead, *self.slabs), low) for lead in ((2,), (2,), ())] if self.slabs else []
        sems = [pltpu.SemaphoreType.DMA((self.total,)), pltpu.SemaphoreType.DMA((self.total,))]
        return [vmem(2, 2, nz), vmem(2, nz, 2), vmem(2, nz), vmem(2, nz), vmem(nz), vmem(nz), vmem(nz - 1), *slabs, *sems]

    def params(self):
        return pltpu.CompilerParams(collective_id=self.number, has_side_effects=True, vmem_limit_bytes=62 * 2**20)

    def stages(self, given, made, scratch):
        squares, out, beside = given[: self.count], made[0], self.slabs is not None
        a, ra, b, rb, d, rd, re = scratch[:7]
        send_sem, recv_sem = scratch[-2:]
        if beside:
            enc, out_enc, (enc_r, enc_a, enc_rx) = given[-1], made[1], scratch[7:10]
        nz, my, count = self.nz, Near(self.nz), self.count
        x, c, z, y = my.x, my.c, my.z, my.y
        copies = Copies(send_sem, recv_sem)
        if beside:
            enc_core = copies.add(lambda: enc.at[:, 1 - c], lambda: enc_r, my.by_core)
            enc_x = copies.add(lambda: enc_a.at[1 - x], lambda: enc_rx, my.by_x)
        core = [copies.add(lambda n=n: squares[n].at[:, 1 - c], lambda n=n: ra.at[n], my.by_core) for n in range(count)]
        one, two, three = [], [], []
        for n in range(count):
            y_first = n % 2 == 0
            if y_first:
                one.append(copies.add(lambda n=n: a.at[n, :, 1 - y], lambda n=n: rb.at[n], my.by_y))
                two.append(copies.add(lambda n=n: b.at[n, 1 - x], lambda n=n: rd.at[n], my.by_x))
            else:
                one.append(copies.add(lambda n=n: a.at[n, 1 - x], lambda n=n: rb.at[n], my.by_x))
                two.append(copies.add(lambda n=n: b.at[n, 1 - y], lambda n=n: rd.at[n], my.by_y))
            three.append([
                copies.add(lambda n=n, t=t: d.at[n, my.steps[t]], lambda n=n, t=t: re.at[n, t - 1], my.by_z[t])
                for t in range(1, nz)
            ])

        def begin():
            greet([my.by_x, my.by_core, my.by_y, *my.by_z[1:]])
            copies.start(*core, *([enc_core] if beside else []))

        def after_core(n):
            copies.arrive(core[n])
            for half in range(2):
                for side in range(2):
                    add_low(a.at[n, half, side], squares[n].at[half, c, :, side], ra.at[n, half, :, side])
            copies.start(one[n])

        def after_one(n):
            copies.arrive(one[n])
            for side in range(2):
                if n % 2 == 0:
                    add_low(b.at[n, side], a.at[n, side, y], rb.at[n, side])
                else:
                    add_low(b.at[n, side], a.at[n, x, side], rb.at[n, side])
            copies.start(two[n])

        def after_two(n):
            copies.arrive(two[n])
            add_low(d.at[n], b.at[n, x if n % 2 == 0 else y], rd.at[n])
            copies.start(*three[n])

        def after_three(n):
            copies.arrive(*three[n])
            total = d[n, z].astype(jnp.float32)
            for t in range(nz - 1):
                total += re[n, t].astype(jnp.float32)
            out[n] = total

        def encoder():
            copies.arrive(enc_core)
            for half in range(2):
                add_low(enc_a.at[half], enc.at[half, c], enc_r.at[half])
            copies.start(enc_x)

        def end():
            if beside:
                copies.arrive(enc_x)
                add_low(out_enc, enc_a.at[x], enc_rx)
            for n in range(count):
                after_three(n)
            copies.finish()

        part = functools.partial
        work = [part(after_core, n) for n in range(count)] + ([encoder] if beside else [])
        work += [part(after_one, n) for n in range(count)] + [part(after_two, n) for n in range(count)]
        first, last = self.points // 12, self.points - 1 - self.points // 12
        stages = [(0, begin)]
        for number, stage in enumerate(work):
            stages.append((first + number * (last - first) // max(len(work) - 1, 1), stage))
        return stages + [(-1, end)]


def gather_kernel(nz, tok, enc, own, everyone, encoded, qkv_out, send_sem, recv_sem, local_sem):
    my = Near(nz)
    x, c, z, y, backs = my.x, my.c, my.z, my.y, my.backs
    greet([my.by_x, my.by_core, my.diagonal, my.by_y, *my.by_z[1:]])
    copies = Copies(send_sem, recv_sem)
    local = [
        pltpu.make_async_copy(source, target, local_sem.at[n])
        for n, (source, target) in enumerate(
            [(own.at[x, c], qkv_out.at[x, c, z, y]), (tok, everyone.at[x, c]), (enc, encoded.at[x, c])]
        )
    ]
    for copy in local:
        copy.start()
    mine = lambda: qkv_out.at[x, c, z, y]
    first = [
        copies.add(lambda: own.at[1 - x, c], mine, my.by_x),
        copies.add(lambda: own.at[x, 1 - c], mine, my.by_core),
        copies.add(lambda: own.at[1 - x, 1 - c], mine, my.diagonal),
    ]
    rows = [(tok, everyone), (enc, encoded)]
    rows_x = [copies.add(lambda s=s: s, lambda t=t: t.at[x, c], my.by_x) for s, t in rows]
    rows_core = [copies.add(lambda s=s: s, lambda t=t: t.at[x, c], my.by_core) for s, t in rows]
    rows_far = [copies.add(lambda t=t: t.at[1 - x, c], lambda t=t: t.at[1 - x, c], my.by_core) for s, t in rows]
    line = [lambda t=t: qkv_out.at[:, :, backs[t], y] for t in range(nz)]
    by_z = [None] + [copies.add(line[0], line[0], my.by_z[t]) for t in range(1, nz)]
    by_y = [copies.add(line[t], line[t], my.by_y) for t in range(nz)]
    copies.start(*first, *rows_x, *rows_core)
    for copy in local:
        copy.wait()
    copies.arrive(*first)
    copies.start(*by_z[1:], by_y[0])
    for t in range(1, nz):
        copies.arrive(by_z[t])
        copies.start(by_y[t])
    for n in range(2):
        copies.arrive(rows_x[n])
        copies.start(rows_far[n])
    copies.arrive(*by_y, *rows_core, *rows_far)
    copies.finish()


def gather(nz, tok, enc, own):
    share, wide = own.shape[-2:]
    shapes = [
        jax.ShapeDtypeStruct((2, 2, *tok.shape), tok.dtype),
        jax.ShapeDtypeStruct((2, 2, *enc.shape), enc.dtype),
        jax.ShapeDtypeStruct((2, 2, nz, 2, share, wide), own.dtype),
    ]
    total = 9 + 2 * nz - 1
    return pl.pallas_call(
        functools.partial(gather_kernel, nz),
        in_specs=[whole()] * 3,
        out_specs=[whole(pl.ANY)] * 3,
        out_shape=shapes,
        scratch_shapes=[
            pltpu.SemaphoreType.DMA((total,)), pltpu.SemaphoreType.DMA((total,)), pltpu.SemaphoreType.DMA((3,)),
        ],
        compiler_params=pltpu.CompilerParams(collective_id=0, has_side_effects=True, vmem_limit_bytes=62 * 2**20),
        name="gather",
    )(tok, enc, own)


def reduce_kernel(nz, group_width, square, own, tok, gain, near, out_square, out_q, out_k, out_v, out_tok, out_gain, out_near, *refs):
    (a, ra, b, rb, d, rd, re, own_r, own_a, own_rz, own_f, own_in, tok_r, tok_a, tok_rx, gain_r, near_r,
     send_sem, recv_sem, gain_send, gain_recv) = refs
    my = Near(nz)
    x, c, z, y = my.x, my.c, my.z, my.y
    world, slots = 8 * nz, 2 * nz
    place, slot = lax.axis_index("seq"), lax.axis_index("fsdp")
    me = place * slots + slot
    barrier = pltpu.get_barrier_semaphore()

    @pl.loop(1, world)
    def _(t):
        other = lax.rem(me + t, world)
        pl.semaphore_signal(barrier, inc=1, device_id=(other // slots, lax.rem(other, slots)), device_id_type=MESH)

    pl.semaphore_wait(barrier, world - 1)
    copies = Copies(send_sem, recv_sem)
    add = copies.add
    half = tok.shape[2] // 2
    padded = own.shape[-1] // 3
    cut = lambda p: slice(p * half, (p + 1) * half)
    own_cut = lambda n: slice(n * padded, (n + 1) * padded)
    tok_core = [
        add(lambda h=h, p=p: tok.at[h, 1 - c, cut(p)], lambda h=h, p=p: tok_r.at[h, cut(p)], my.by_core)
        for h in (1 - x, x) for p in range(2)
    ]
    own_y = [
        add(lambda n=n: own.at[:, :, :, 1 - y, :, own_cut(n)], lambda n=n: own_r.at[n], my.by_y) for n in range(3)
    ]
    core = add(lambda: square.at[:, 1 - c], lambda: ra, my.by_core)
    near_all = [add(lambda: near, lambda t=t: near_r.at[t - 1], (place, lax.rem(slot + t, slots))) for t in range(1, slots)]
    tok_x = [add(lambda p=p: tok_a.at[1 - x, cut(p)], lambda p=p: tok_rx.at[cut(p)], my.by_x) for p in range(2)]
    one = add(lambda: a.at[:, 1 - y], lambda: rb, my.by_y)
    two = add(lambda: b.at[1 - x], lambda: rd, my.by_x)
    three = [add(lambda t=t: d.at[my.steps[t]], lambda t=t: re.at[t - 1], my.by_z[t]) for t in range(1, nz)]
    own_z = [
        [add(lambda n=n, t=t: own_a.at[n, :, :, my.steps[t]], lambda n=n, t=t: own_rz.at[n, t - 1], my.by_z[t]) for t in range(1, nz)]
        for n in range(3)
    ]
    landing = lambda: own_in.at[:, x, c]
    own_seq = [
        add(lambda: own_f.at[:, 1 - x, c], landing, my.by_x),
        add(lambda: own_f.at[:, x, 1 - c], landing, my.by_core),
        add(lambda: own_f.at[:, 1 - x, 1 - c], landing, my.diagonal),
    ]

    def gain_copy(t):
        other = lax.rem(me + t, world)
        return pltpu.make_async_remote_copy(
            src_ref=gain.at[other], dst_ref=gain_r.at[t - 1], send_sem=gain_send.at[t - 1], recv_sem=gain_recv.at[t - 1],
            device_id=(other // slots, lax.rem(other, slots)), device_id_type=MESH,
        )

    copies.start(own_y[0], *tok_core[:2], own_y[1], core, *tok_core[2:], own_y[2], *near_all)

    @pl.loop(1, world)
    def _(t):
        gain_copy(t).start()

    def tok_sum(h, p):
        add_low(tok_a.at[h, cut(p)], tok.at[h, c, cut(p)], tok_r.at[h, cut(p)])

    for p in range(2):
        copies.arrive(tok_core[p])
        tok_sum(1 - x, p)
        copies.start(tok_x[p])
    copies.arrive(core)
    for h in range(2):
        for side in range(2):
            add_low(a.at[h, side], square.at[h, c, :, side], ra.at[h, :, side])
    copies.start(one)

    def own_sum(n):
        copies.arrive(own_y[n])
        for h in range(2):
            for side in range(2):
                for k in range(nz):
                    own_a[n, h, side, k] = own[h, side, k, y, :, own_cut(n)] + own_r[n, h, side, k]
        copies.start(*own_z[n])

    own_sum(0)
    for p in range(2):
        copies.arrive(tok_core[2 + p])
        tok_sum(x, p)
    own_sum(1)
    own_sum(2)
    copies.arrive(one)
    for side in range(2):
        add_low(b.at[side], a.at[side, y], rb.at[side])
    copies.start(two)
    for n in range(3):
        copies.arrive(*own_z[n])
        for h in range(2):
            for side in range(2):
                total = own_a[n, h, side, z].astype(jnp.float32)
                for t in range(nz - 1):
                    total += own_rz[n, t, h, side].astype(jnp.float32)
                own_f[n, h, side] = total.astype(low)
    copies.start(*own_seq)
    own_in[:, x, c] = own_f[:, x, c]
    copies.arrive(two)
    add_low(d, b.at[x], rd)
    copies.start(*three)
    copies.arrive(*near_all)
    total = near[...]
    for t in range(slots - 1):
        total += near_r[t]
    out_near[...] = total
    out_gain[...] = gain[me]

    @pl.loop(1, world)
    def _(t):
        gain_copy(t).wait_recv()
        out_gain[...] += gain_r[t - 1]

    for p in range(2):
        copies.arrive(tok_x[p])
        add_low(out_tok.at[cut(p)], tok_a.at[x, cut(p)], tok_rx.at[cut(p)])
    copies.arrive(*own_seq)
    for n, out in enumerate((out_q, out_k, out_v)):
        parts = [own_in[n, s // 2, s % 2, :, :group_width].astype(jnp.float32) for s in range(4)]
        out[...] = jnp.concatenate(parts, axis=1)
    copies.arrive(*three)
    total = d[z].astype(jnp.float32)
    for t in range(nz - 1):
        total += re[t].astype(jnp.float32)
    out_square[...] = total
    copies.finish()

    @pl.loop(1, world)
    def _(t):
        gain_copy(t).wait_send()


def reduce(nz, group_width, square, own, tok, gain, near):
    share, width = square.shape[-2:]
    wide = own.shape[-1]
    vmem = lambda *shape: pltpu.VMEM(shape, low)
    slabs = tok.shape[2:]
    world = 8 * nz
    padded = wide // 3
    total = 4 + 3 + 1 + 2 * nz - 1 + 2 + 2 + nz - 1 + 3 * (nz - 1) + 3
    f32 = lambda *shape: jax.ShapeDtypeStruct(shape, jnp.float32)
    return pl.pallas_call(
        functools.partial(reduce_kernel, nz, group_width),
        in_specs=[whole()] * 5,
        out_specs=[whole()] * 7,
        out_shape=[f32(share, width)] * 4 + [f32(*slabs), f32(*gain.shape[1:]), f32(*near.shape)],
        scratch_shapes=[
            vmem(2, 2, nz, share, width), vmem(2, nz, 2, share, width), vmem(2, nz, share, width), vmem(2, nz, share, width),
            vmem(nz, share, width), vmem(nz, share, width), vmem(nz - 1, share, width),
            vmem(3, 2, 2, nz, share, padded), vmem(3, 2, 2, nz, share, padded), vmem(3, nz - 1, 2, 2, share, padded),
            vmem(3, 2, 2, share, padded), vmem(3, 2, 2, share, padded),
            vmem(2, *slabs), vmem(2, *slabs), vmem(*slabs),
            pltpu.VMEM((world - 1, *gain.shape[1:]), jnp.float32), pltpu.VMEM((2 * nz - 1, *near.shape), jnp.float32),
            pltpu.SemaphoreType.DMA((total,)), pltpu.SemaphoreType.DMA((total,)),
            pltpu.SemaphoreType.DMA((world - 1,)), pltpu.SemaphoreType.DMA((world - 1,)),
        ],
        compiler_params=pltpu.CompilerParams(collective_id=1, has_side_effects=True, vmem_limit_bytes=62 * 2**20),
        name="reduce",
    )(square, own, tok, gain, near)


def finish_kernel(
    slabs, x_ref, attended_ref, normed_ref, rows_ref, share_gain_ref, near_ref, map_ref, ffn_ref, enc_ref, early_ref, last_ref, *refs
):
    squares, refs = refs[:4], refs[4:]
    dx_ref, gain_ref, table_ref, gate_ref, up_ref, down_ref, enc_out = refs[:7]
    outs = refs[7:]
    values = x_ref[...].astype(jnp.float32)
    scale = scale_of(values)
    unit = values * scale
    grad_unit = normed_ref[...] * rows_ref[0:1, :]
    dx_ref[0] = attended_ref[...] + scale * (grad_unit - unit * jnp.mean(grad_unit * unit, axis=-1, keepdims=True))

    @pl.when(pl.program_id(0) == 0)
    def _():
        share, inner = gate_ref.shape
        width = down_ref.shape[1]
        for n in range(3):
            gain_ref[n : n + 1, :] = share_gain_ref[0:1, n * share : (n + 1) * share]
        table = lax.dot_general(
            map_ref[...], near_ref[...], (((1,), (1,)), ((), ())), precision=highest, preferred_element_type=jnp.float32
        )
        table_ref[...] = table[:, : table_ref.shape[1]]
        gate_ref[...] = ffn_ref[:, :inner].astype(jnp.float32)
        up_ref[...] = ffn_ref[:, inner : 2 * inner].astype(jnp.float32)
        for k in range(slabs):
            size = min(share, down_ref.shape[0] - k * share)
            column = 2 * inner + k * width
            down_ref[k * share : k * share + size] = ffn_ref[:size, column : column + width].astype(jnp.float32)
        enc_out[0] = enc_ref[...]
        for n, square in enumerate(squares):
            outs[n][...] = square[...]
        for n in range(3):
            outs[4 + n][...] = early_ref[n]
        outs[7][...] = last_ref[0]


def finish(tokens, grad_attended, grad_normed, gains, share_gains, by_distance, share_ffn, grad_encoded, early, last, squares, group, bins, sizes):
    rows, width = tokens.shape
    share, inner, hidden_share = sizes
    block = min(128, rows)
    place = np.arange(LANES)
    far = 16 + np.sum(place[:, None] >= bounds[None], axis=1)
    bucket = np.where(place < 16, place, far)
    table_map = (bucket[None] == np.arange(bins)[:, None]).astype(np.float32)
    table_map[bins - 1] = -(bucket < bins - 1).astype(np.float32)
    by_rows = pl.BlockSpec((block, width), lambda i: (i, 0))
    fixed = lambda shape: pl.BlockSpec(shape, lambda i: (0,) * len(shape))
    f32 = lambda *shape: jax.ShapeDtypeStruct(shape, jnp.float32)
    given = [gains, share_gains, by_distance, jnp.asarray(table_map), share_ffn, grad_encoded, early, last, *squares]
    made = [
        f32(3, share), f32(bins, group), f32(share, inner), f32(share, inner), f32(hidden_share, width),
        f32(1, *grad_encoded.shape), *[f32(share, width)] * 8,
    ]
    return pl.pallas_call(
        functools.partial(finish_kernel, -(-hidden_share // share)),
        grid=(rows // block,),
        in_specs=[by_rows] * 3 + [fixed(v.shape) for v in given],
        out_specs=[pl.BlockSpec((1, block, width), lambda i: (0, i, 0))] + [fixed(v.shape) for v in made],
        out_shape=[f32(1, rows, width), *made],
        compiler_params=pltpu.CompilerParams(vmem_limit_bytes=62 * 2**20),
        name="finish",
    )(tokens, grad_attended, grad_normed, *given)


def rms_norm(values, gain):
    scale = lax.rsqrt(jnp.mean(values * values, axis=-1, keepdims=True) + epsilon)
    return values * scale * gain


def rms_back(values, gain, grad_normed):
    scale = lax.rsqrt(jnp.mean(values * values, axis=-1, keepdims=True) + epsilon)
    unit = values * scale
    grad_unit = grad_normed * gain
    grad_gain = jnp.sum(grad_normed * unit, axis=0)
    grad_values = scale * (grad_unit - unit * jnp.mean(grad_unit * unit, axis=-1, keepdims=True))
    return (grad_values, grad_gain)


def activate(gate, upper):
    return jax.nn.gelu(gate, approximate=True) * upper


def per_device(
    tokens, encoder, cotangent, lengths, gains, self_query, self_key, self_value, self_output,
    cross_query, cross_key, cross_value, cross_output, ffn_gate, ffn_up, ffn_down, rel_bias,
):
    both = ("seq", "fsdp")
    seq, fsdp = lax.axis_size("seq"), lax.axis_size("fsdp")
    world = seq * fsdp
    nz = fsdp // 2
    share, width = self_query.shape
    hidden_share = ffn_down.shape[0]
    inner = ffn_gate.shape[1]
    rows = tokens.shape[1]
    group = rel_bias.shape[1]
    group_width = group * HEAD
    padded = -(-group_width // LANES) * LANES
    spare = padded - group_width
    heads = width // HEAD
    place = lax.axis_index("seq")
    aligned = share % 8 == 0

    slabs = -(-hidden_share // share)
    squares = jnp.stack([w.astype(low) for w in (self_output, cross_query, cross_key, cross_value)])
    if aligned:
        down = jnp.pad(ffn_down.astype(low), ((0, slabs * share - hidden_share), (0, 0))).reshape(slabs, share, width)
        wide_share = [cross_output.astype(low), *[down[k] for k in range(slabs)], ffn_gate.astype(low), ffn_up.astype(low)]
        wide_weights = lax.all_gather(jnp.concatenate(wide_share, axis=1), both, axis=0, tiled=True)
    else:
        gate_up = lax.all_gather(jnp.concatenate([ffn_gate.astype(low), ffn_up.astype(low)], axis=1), both, axis=0, tiled=True)
        w_down = lax.all_gather(ffn_down.astype(low), both, axis=0, tiled=True)
        c_output = lax.all_gather(cross_output.astype(low), both, axis=0, tiled=True)
    gain_columns = jnp.pad(gains.astype(low).T, ((0, 0), (0, spare - 3)))
    pieces = []
    for s in range(seq):
        for n, w in enumerate((self_query, self_key, self_value)):
            pieces.append(w[:, s * group_width : (s + 1) * group_width].astype(low))
            pieces.append(gain_columns if n == 0 else jnp.zeros((share, spare), low))
    own = jnp.concatenate(pieces, axis=1).reshape(share, seq, 3 * padded).transpose(1, 0, 2)
    if aligned:
        everyone, encoded, w_qkv = gather(nz, tokens[0], encoder[0], own.reshape(2, 2, share, 3 * padded))
    else:
        everyone = lax.all_gather(tokens[0], "seq", axis=0)
        encoded = lax.all_gather(encoder[0], "seq", axis=0)
        w_qkv = lax.all_to_all(own, "seq", split_axis=0, concat_axis=0, tiled=True)
        w_qkv = lax.all_gather(w_qkv, "fsdp", axis=1)
    everyone = everyone.reshape(seq * rows, width)
    encoded = encoded.reshape(-1, width)
    w_qkv = w_qkv.reshape(width, 3 * padded)
    length = lengths[0]
    values_in = tokens[0].astype(jnp.float32)
    qkv, normed_all, gain_rows = project(everyone, w_qkv, group_width)
    bias = bias_rows(rel_bias)
    plan = GatherPlan(nz, 4, share, width, rows, padded // LANES) if aligned else None
    own_mixed, own_logsum, *gathered = attend_forward(
        qkv, qkv, qkv, group, padded, bias, lengths, plan, (squares,) if aligned else ()
    )
    squares = gathered[0] if aligned else jnp.moveaxis(lax.all_gather(squares, both, axis=0), 1, 0)
    squares = squares.reshape(4, width, width)
    if aligned:
        mixed = gathered[1].reshape(seq, rows, padded)
    else:
        mixed = lax.all_to_all(own_mixed.reshape(seq, rows, padded), "seq", split_axis=0, concat_axis=0, tiled=True)
    cross_keys, cross_values = encode(encoded, squares)
    attended, normed_two, cross_queries = enter(tokens[0], mixed, squares, gain_rows, group_width)
    cross_mixed, cross_logsum = attend_forward(cross_queries, cross_keys, cross_values, heads)
    if aligned:
        scalars = jnp.stack([length, place * rows])
        result, grad_crossed, grad_cmixed, grad_coutput, gain_two, packed = middle(
            scalars, attended, cross_mixed, gain_rows, cotangent[0], wide_weights, inner, world
        )
        grad_gain_two = gain_two[0]
        packed = packed.reshape(width, -1)
    else:
        crossed = attended + nn(cross_mixed, c_output)
        normed_three = rms_norm(crossed, gain_rows[2]).astype(low)
        both_parts = nn(normed_three, gate_up)
        gate, upper = both_parts[:, :inner], both_parts[:, inner:]
        hidden = activate(gate, upper).astype(low)
        result = (crossed + nn(hidden, w_down)).astype(low)

        positions = place * rows + jnp.arange(rows, dtype=jnp.int32)
        grad_out = cotangent[0].astype(jnp.float32) * (positions < length).astype(jnp.float32)[:, None]
        grad_ffn = grad_out.astype(low)
        grad_hidden = nt(grad_ffn, w_down)
        _, pullback = jax.vjp(activate, gate, upper)
        grad_gate, grad_upper = pullback(grad_hidden)
        grad_both = jnp.concatenate([grad_gate.astype(low), grad_upper.astype(low)], axis=1)
        grad_down = tn(hidden, grad_ffn).astype(low).reshape(world, hidden_share, width)
        grad_down = jnp.pad(grad_down, ((0, 0), (0, slabs * share - hidden_share), (0, 0)))
        grad_down = grad_down.reshape(world, slabs, share, width).transpose(0, 2, 1, 3).reshape(world * share, slabs * width)
        packed = jnp.concatenate([tn(normed_three, grad_both).astype(low), grad_down], axis=1)

        grad_normed_three = nt(grad_both, gate_up)
        norm_part, grad_gain_two = rms_back(crossed, gain_rows[2], grad_normed_three)
        grad_crossed = grad_out + norm_part
        grad_branch = grad_crossed.astype(low)
        grad_coutput = tn(cross_mixed, grad_branch).astype(low)
        grad_cmixed = nt(grad_branch, c_output).astype(low)
    share_ffn = lax.psum_scatter(packed, both, scatter_dimension=0, tiled=True)
    slab = 64
    chunked = lambda g: g.reshape(2, 2, nz, 2, share, g.shape[-1])
    by_place = lambda g: g.reshape(2, 2, -1, slab, width)
    plan = ReducePlan(nz, 1, share, width, 4, heads) if aligned else None
    grad_cq, grad_ck, grad_cv, *first_sums = attend_backward(
        cross_queries, cross_keys, cross_values, grad_cmixed, cross_mixed, cross_logsum, heads,
        plan=plan, extra=(chunked(grad_coutput),) if aligned else (),
    )
    grad_attended, branch, grad_mixed, gain_one = leave(
        grad_cq, squares, attended, gain_rows, grad_crossed, seq, group_width, padded
    )
    grad_gain_one = gain_one[0]
    own_grad_mixed = lax.all_to_all(grad_mixed, "seq", split_axis=0, concat_axis=0, tiled=True).reshape(seq * rows, padded)
    grad_cquery, grad_ckey, grad_cvalue, grad_output, grad_encoded = square_terms(
        normed_two, grad_cq, encoded, grad_ck, grad_cv, squares, mixed, branch, group_width
    )
    early = [grad_cquery, grad_ckey, grad_cvalue]
    plan, extra = None, ()
    if aligned:
        extra = (*[chunked(g) for g in early], by_place(grad_encoded))
        plan = ReducePlan(nz, len(early), share, width, 3, 3 * BACKWARD_POINTS, extra[-1].shape[2:])
    own_dq, own_dk, own_dv, by_distance, *sums = attend_backward(
        qkv, qkv, qkv, own_grad_mixed, own_mixed, own_logsum, group, padded, bias, lengths, plan, extra
    )
    grad_normed_part, grad_own, gain_zero = unproject(everyone, normed_all, w_qkv, own_dq, own_dk, own_dv)
    grad_gain_zero = gain_zero[0]
    grad_gains = jnp.stack([grad_gain_zero, grad_gain_one, grad_gain_two])
    grad_gains = grad_gains.reshape(3, world, share).transpose(1, 0, 2).reshape(world, 1, 3 * share)
    grad_gains = jnp.pad(grad_gains, ((0, 0), (0, 7), (0, LANES - 3 * share)))
    wide = jnp.float32
    if aligned:
        share_output, *share_own, grad_normed, share_gains, by_distance = reduce(
            nz, group_width, chunked(grad_output), chunked(grad_own), by_place(grad_normed_part), grad_gains, by_distance
        )
        share_early, grad_encoded = sums
        grad_input, share_gains, table_grad, share_gate, share_up, share_down, grad_encoded, *shares = finish(
            tokens[0], grad_attended, grad_normed.reshape(rows, width), gain_rows, share_gains, by_distance, share_ffn,
            grad_encoded.reshape(-1, width), share_early, first_sums[0], (*share_own, share_output),
            group, rel_bias.shape[0], (share, inner, hidden_share),
        )
        return (
            result[None], grad_input, grad_encoded, share_gains, *shares, share_gate, share_up, share_down, table_grad,
        )
    else:
        scatter = lambda g, axes: lax.psum_scatter(g, axes, scatter_dimension=0, tiled=True)
        share_squares = scatter(jnp.concatenate([grad_output, *early, grad_coutput], axis=1), both).astype(wide)
        share_squares = [share_squares[:, n * width : (n + 1) * width] for n in range(5)]
        grad_own = scatter(grad_own.reshape(seq, fsdp, share, 3 * padded).transpose(1, 0, 2, 3), "fsdp")[0]
        grad_own = lax.all_to_all(grad_own, "seq", split_axis=0, concat_axis=0, tiled=True).astype(wide)
        grad_own = grad_own.reshape(seq, share, 3, padded)[:, :, :, :group_width].transpose(2, 1, 0, 3).reshape(3, share, width)
        share_own = [grad_own[n] for n in range(3)]
        grad_normed = scatter(grad_normed_part, "seq").astype(wide)
        grad_encoded = scatter(grad_encoded, "seq").astype(wide)
        share_gains = scatter(grad_gains, both)[0]
        by_distance = lax.psum(by_distance, "fsdp")
    share_gains = share_gains[0, : 3 * share].reshape(3, share)
    norm_part, _ = rms_back(values_in, gain_rows[0], grad_normed)
    grad_input = grad_attended + norm_part
    bins = rel_bias.shape[0]
    near_map = (buckets(jnp.arange(LANES, dtype=jnp.int32))[:, None] == jnp.arange(bins - 1, dtype=jnp.int32)[None]).astype(wide)
    near_sums = jnp.dot(near_map.T, by_distance[:group].T, precision=highest)
    table_grad = jnp.concatenate([near_sums, -jnp.sum(near_sums, axis=0, keepdims=True)], axis=0)
    share_ffn = share_ffn.astype(wide)
    share_down = share_ffn[:, 2 * inner :].reshape(share, slabs, width).transpose(1, 0, 2).reshape(slabs * share, width)
    return (
        result[None], grad_input[None], grad_encoded[None], share_gains, *share_own, *share_squares,
        share_ffn[:, :inner], share_ffn[:, inner : 2 * inner], share_down[:hidden_share], table_grad,
    )


def solution(mesh):
    split = P(("seq", "fsdp"), None)
    rows = P("fsdp", "seq", None)
    gains = P(None, ("seq", "fsdp"))
    return jax.shard_map(
        per_device,
        mesh=mesh,
        in_specs=(rows, rows, rows, P("fsdp"), gains, *([split] * 11), P(None, "seq")),
        out_specs=(rows, rows, rows, gains, *([split] * 11), P(None, "seq")),
        check_vma=False,
    )
```
